32 devices in a mesh: sec: 2 (over core), row: 4 (over y, x), nest: 4 (over z).
Axes of the slice: x: 2, y: 2, z: 4, core: 2. Of those that a mesh axis runs over, the one named last changes fastest.
Arguments:
- ocean_state: float32 [2, 3, 256, 512], P('sec', None, 'row', 'nest'), may hold values from -1.2 to 1.2
- face_depth: float32 [2, 2, 256, 512], P('sec', None, 'row', 'nest'), may hold values from 2 to 4
- face_open: int32 [2, 2, 256, 512], P('sec', None, 'row', 'nest'), may hold values 0 or 1
- nest_place: int32 [16], replicated, may hold values from 0 to 95, as said below
- nest_host: int32 [16], replicated, may hold values from 0 to 31, as said below
Outputs:
- final_state: float32 [2, 3, 256, 512], P('sec', None, 'row', 'nest')
The draws below stay inside these ranges and needn't reach their ends.
Inputs may be any that keep to these rules, and one draw needn't show every extreme that they name: `nest_place`: distinct positions; the first and the last position are always covered. `nest_host`: distinct slots; both slots of some device hold a nest; the nest at the first position lives in the last slot and the nest at the last position in the first slot.
All inputs are finite; a program needn't handle non-finite values. No bound on the sum of `face_open` on one device may be relied on, other than what follows from the above.
Results may differ from the reference program's by a relative error of at most 0.00013.
Values sent between devices are 32-bit elements; how exact they have to be, the bound alone decides.
A program may use at most 64 MiB of HBM per device.

```python
import math
import jax
import jax.numpy as jnp
from jax import lax

PH = 8
PW = 32
RR = 4
K = 2
STEPS = 4
NT = 16
SLOTS = 32
NPOS = 6
NESTS = 16
OH = 256
OW = 512
N_ROW = 4
N_NEST = 4


def draw_nest_place(key, part):
    total = NT * NPOS
    inner = jax.random.permutation(jax.random.fold_in(key, 11), total - 2).astype(jnp.int32) + 1
    chosen = jnp.concatenate([jnp.array([0, total - 1], jnp.int32), inner[:NESTS - 2]])
    shuffle = jax.random.permutation(jax.random.fold_in(key, 12), NESTS)
    return chosen[shuffle].astype(jnp.int32)


def draw_nest_host(key, part):
    base_key = jax.random.fold_in(key, 23)
    chosen = jax.random.randint(jax.random.fold_in(base_key, 1), (), 0, NT)
    ordering = jax.random.permutation(jax.random.fold_in(base_key, 2), SLOTS).astype(jnp.int32)
    flagged = (ordering // K == chosen).astype(jnp.int32)
    counter = jnp.arange(SLOTS, dtype=jnp.int32)
    scores = jnp.where(ordering == SLOTS - 1, 0, jnp.where(ordering == 0, 1, (3 - flagged) * SLOTS + counter)).astype(jnp.int32)
    assigned = ordering[jnp.argsort(scores)][:NESTS]
    shuffle = jax.random.permutation(jax.random.fold_in(key, 12), NESTS)
    return assigned[shuffle].astype(jnp.int32)


def plant(values, own_key, least, largest):
    dims = values.shape
    spot = [jax.random.randint(jax.random.fold_in(own_key, axis), (), 0, dims[axis]) for axis in range(len(dims))]
    values = values.at[tuple(spot)].set(least)
    longest = dims.index(max(dims))
    spot[longest] = (spot[longest] + 1) % dims[longest]
    return values.at[tuple(spot)].set(largest)


def block_levels(stream_key, dims, pieces, least, largest):
    gain, own = 1.0, jax.random.fold_in(stream_key, 6)
    for dim, blocks in pieces:
        draws = jnp.exp(jax.random.uniform(jax.random.fold_in(own, dim), (blocks,), jnp.float32, least / len(pieces), largest / len(pieces)))
        gain = gain * jnp.repeat(draws, dims[dim] // blocks).reshape([-1 if axis == dim else 1 for axis in range(len(dims))])
    return gain


def normal_values(stream_key, dims, spread, reach, shards=(), kind=jnp.bfloat16):
    gain = block_levels(stream_key, dims, shards, -0.22, 0.18) if shards else 1.0
    values = jax.random.normal(stream_key, dims, jnp.float32) * spread * gain
    return jnp.minimum(jnp.maximum(values, -reach), reach).astype(kind)


def setup_inputs(seed: int = 0) -> dict:
    keys = jax.random.split(jax.random.key(seed), 6)
    return {
        "ocean_state": normal_values(keys[0], (2, 3, OH, OW), 0.3, 1.2, ((0, 2), (2, 4), (3, 4)), jnp.float32),
        "face_depth": jnp.clip(jnp.exp(math.log(4.0) - 0.6931472 * jax.random.uniform(keys[1], (2, 2, OH, OW), jnp.float32) ** block_levels(keys[1], (2, 2, OH, OW), ((0, 2), (2, 4), (3, 4)), -0.2, 0.2)), 2.0, 4.0),
        "face_open": plant((jax.random.randint(keys[2], (2, 2, OH, OW), 0, 8) < 7).astype(jnp.int32), jax.random.fold_in(keys[2], 1), 0, 1),
        "nest_place": draw_nest_place(jax.random.fold_in(keys[5], 71), 0),
        "nest_host": draw_nest_host(jax.random.fold_in(keys[5], 71), 0),
    }


COURANT = 0.3


def surface_update(surface, eastward, southward, west_ghost, north_ghost):
    east_behind = jnp.concatenate([west_ghost, eastward[..., :-1]], axis=-1)
    south_behind = jnp.concatenate([north_ghost, southward[..., :-1, :]], axis=-2)
    return surface - COURANT * ((eastward - east_behind) + (southward - south_behind))


def flux_update(eastward, southward, new_surface, surface_east, surface_south, depth_east, depth_south, open_east, open_south):
    new_eastward = open_east * (eastward - COURANT * (depth_east + 0.5 * (new_surface + surface_east)) * (surface_east - new_surface))
    new_southward = open_south * (southward - COURANT * (depth_south + 0.5 * (new_surface + surface_south)) * (surface_south - new_surface))
    return new_eastward, new_southward


def restrict(surface, eastward, southward):
    leading = surface.shape[:-2]
    coarse_surface = surface.reshape(leading + (PH, RR, PW, RR)).mean(axis=(-3, -1))
    coarse_east = eastward[..., RR - 1::RR].reshape(leading + (PH, RR, PW)).mean(axis=-2)
    coarse_south = southward[..., RR - 1::RR, :].reshape(leading + (PH, PW, RR)).mean(axis=-1)
    return jnp.stack([coarse_surface, coarse_east, coarse_south], axis=-3)


def to_slots(grid):
    channels = grid.shape[0]
    reshaped = grid.reshape(channels, N_ROW, K, RR * PH, N_NEST, RR * PW).transpose(1, 4, 2, 0, 3, 5)
    return reshaped.reshape(N_ROW * N_NEST * K, channels, RR * PH, RR * PW)


def from_slots(slot_states):
    channels = slot_states.shape[1]
    reshaped = slot_states.reshape(N_ROW, N_NEST, K, channels, RR * PH, RR * PW).transpose(3, 0, 2, 4, 1, 5)
    return reshaped.reshape(channels, N_ROW * K * RR * PH, N_NEST * RR * PW)


def nest_anchors(nest_place):
    positions = K * (RR - 1)
    tile_number = nest_place // positions
    within = nest_place % positions
    band_number = within // (RR - 1)
    column_number = within % (RR - 1)
    first_rows = (tile_number // N_NEST) * (K * RR * PH) + band_number * (RR * PH) + (RR - 1) * PH // 2
    first_cols = (tile_number % N_NEST) * (RR * PW) + PW // 2 + column_number * PW
    return first_rows.astype(jnp.int32), first_cols.astype(jnp.int32)


def gather_strips(outer_grid, first_rows, first_cols):
    def one_nest(row_start, col_start):
        west_flux = lax.dynamic_slice(outer_grid[1], (row_start, col_start - 1), (PH, 1))[:, 0]
        east_level = lax.dynamic_slice(outer_grid[0], (row_start, col_start + PW), (PH, 1))[:, 0]
        north_flux = lax.dynamic_slice(outer_grid[2], (row_start - 1, col_start), (1, PW))[0]
        south_level = lax.dynamic_slice(outer_grid[0], (row_start + PH, col_start), (1, PW))[0]
        return jnp.stack([jnp.concatenate([west_flux, north_flux]), jnp.concatenate([east_level, south_level])])
    return jax.vmap(one_nest)(first_rows, first_cols)


def outer_advance(outer_grid, depth_outer, open_outer):
    grid_rows = outer_grid.shape[1]
    grid_cols = outer_grid.shape[2]
    zero_column = jnp.zeros((grid_rows, 1), jnp.float32)
    zero_row = jnp.zeros((1, grid_cols), jnp.float32)
    new_surface = surface_update(outer_grid[0], outer_grid[1], outer_grid[2], zero_column, zero_row)
    surface_east = jnp.concatenate([new_surface[:, 1:], zero_column], axis=1)
    surface_south = jnp.concatenate([new_surface[1:, :], zero_row], axis=0)
    new_eastward, new_southward = flux_update(outer_grid[1], outer_grid[2], new_surface, surface_east, surface_south, depth_outer[0], depth_outer[1], open_outer[0], open_outer[1])
    return jnp.stack([new_surface, new_eastward, new_southward])


def nest_advance(nest_states, depth_fine, open_fine, old_strips, new_strips):
    surface, eastward, southward = nest_states[:, 0], nest_states[:, 1], nest_states[:, 2]
    for substep in range(1, RR + 1):
        ghost_vals = old_strips + (substep / RR) * (new_strips - old_strips)
        west_ghost = jnp.repeat(ghost_vals[:, 0, :PH], RR, axis=1)[:, :, None]
        north_ghost = jnp.repeat(ghost_vals[:, 0, PH:], RR, axis=1)[:, None, :]
        east_ghost = jnp.repeat(ghost_vals[:, 1, :PH], RR, axis=1)[:, :, None]
        south_ghost = jnp.repeat(ghost_vals[:, 1, PH:], RR, axis=1)[:, None, :]
        new_surface = surface_update(surface, eastward, southward, west_ghost, north_ghost)
        surface_east = jnp.concatenate([new_surface[..., 1:], east_ghost], axis=-1)
        surface_south = jnp.concatenate([new_surface[..., 1:, :], south_ghost], axis=-2)
        eastward, southward = flux_update(eastward, southward, new_surface, surface_east, surface_south, depth_fine[:, 0], depth_fine[:, 1], open_fine[:, 0], open_fine[:, 1])
        surface = new_surface
    return jnp.stack([surface, eastward, southward], axis=1)


def write_back(outer_grid, coarse, first_rows, first_cols):
    def place_one(index, grid):
        return lax.dynamic_update_slice(grid, coarse[index], (jnp.zeros((), jnp.int32), first_rows[index], first_cols[index]))
    return lax.fori_loop(0, coarse.shape[0], place_one, outer_grid)


def reference(ocean_state, face_depth, face_open, nest_place, nest_host):
    outer_grid = ocean_state[0]
    depth_outer = face_depth[0]
    open_outer = face_open[0].astype(jnp.float32)
    slot_states = to_slots(ocean_state[1])
    slot_depth = to_slots(face_depth[1])
    slot_open = to_slots(face_open[1].astype(jnp.float32))
    nest_states = slot_states[nest_host]
    depth_fine = slot_depth[nest_host]
    open_fine = slot_open[nest_host]
    first_rows, first_cols = nest_anchors(nest_place)
    old_strips = gather_strips(outer_grid, first_rows, first_cols)
    for timestep in range(STEPS):
        outer_grid = outer_advance(outer_grid, depth_outer, open_outer)
        new_strips = gather_strips(outer_grid, first_rows, first_cols)
        nest_states = nest_advance(nest_states, depth_fine, open_fine, old_strips, new_strips)
        coarse = restrict(nest_states[:, 0], nest_states[:, 1], nest_states[:, 2])
        outer_grid = write_back(outer_grid, coarse, first_rows, first_cols)
        old_strips = new_strips
    slot_states = slot_states.at[nest_host].set(nest_states)
    return jnp.stack([outer_grid, from_slots(slot_states)])
```

```python
import functools

import jax
import jax.numpy as jnp
from jax import lax
from jax.experimental import pallas as pl
from jax.experimental.pallas import tpu as pltpu
from jax.sharding import PartitionSpec as P

PH = 8
PW = 32
RR = 4
K = 2
STEPS = 4
NPOS = K * (RR - 1)
COURANT = 0.3
MESH = pl.DeviceIdType.MESH
FINE_ROWS = RR * PH
TOP = (RR - 1) * PH // 2
LEFT = PW // 2
NEAR = PW
EDGES = (
    (0, PW - 1),
    (1, PW - 2),
    (1, PW - 1),
    (2, PW - 2),
    (2, PW - 1),
    (0, 0),
    (1, 0),
    (2, 0),
    (2, 1),
)
LEFT_EDGES = 5
BAND = (TOP + PH + STEPS + 7) // 8 * 8
HALO = 8
ROWS_EARLY = ((0, PH), (3, PH + 1), (1, PH), (2, PH), (2, -2), (0, -1), (1, -1), (2, -1))
ROWS_LATE = ((4, PH + 1), (5, -2), (6, -2), (7, PH), (7, -1), (8, PH), (8, -2), (8, -1))
SIDE_FIELDS = (0, 1, 2, 7, 8)


def iota(shape, dim):
    return lax.broadcasted_iota(jnp.int32, shape, dim)


def new_level(surface, eastward, southward, west_ghost, north_ghost):
    rows, cols = iota(surface.shape, 0), iota(surface.shape, 1)
    east_behind = jnp.where(cols == 0, west_ghost, pltpu.roll(eastward, 1, 1))
    south_behind = jnp.where(rows == 0, north_ghost, pltpu.roll(southward, 1, 0))
    return surface - COURANT * ((eastward - east_behind) + (southward - south_behind))


def new_fluxes(eastward, southward, level, east_ghost, south_ghost, depth, opened):
    height, width = level.shape
    rows, cols = iota(level.shape, 0), iota(level.shape, 1)
    level_east = jnp.where(cols == width - 1, east_ghost, pltpu.roll(level, width - 1, 1))
    level_south = jnp.where(rows == height - 1, south_ghost, pltpu.roll(level, height - 1, 0))
    east = opened[0] * (
        eastward - COURANT * (depth[0] + 0.5 * (level + level_east)) * (level_east - level)
    )
    south = opened[1] * (
        southward - COURANT * (depth[1] + 0.5 * (level + level_south)) * (level_south - level)
    )
    return east, south


def new_level_ring(surface, eastward, southward, courant):
    east_gap = eastward - pltpu.roll(eastward, 1, 1)
    south_gap = southward - pltpu.roll(southward, 1, 0)
    return surface - courant * (east_gap + south_gap)


def new_fluxes_ring(eastward, southward, level, wet_east, wet_south):
    height, width = level.shape
    level_east = pltpu.roll(level, width - 1, 1)
    level_south = pltpu.roll(level, height - 1, 0)
    east = eastward - COURANT * (wet_east + 0.5 * (level + level_east)) * (level_east - level)
    south = southward - COURANT * (wet_south + 0.5 * (level + level_south)) * (level_south - level)
    return jnp.where(wet_east > 0, east, 0.0), jnp.where(wet_south > 0, south, 0.0)


def parts(x):
    high = x.astype(jnp.bfloat16).astype(jnp.float32)
    rest = x - high
    middle = rest.astype(jnp.bfloat16).astype(jnp.float32)
    return high, middle, rest - middle


def dot_by(x, chosen):
    rows = x.shape[0]
    stacked = jnp.concatenate(parts(x), axis=0).astype(jnp.bfloat16)
    y = jnp.dot(stacked, chosen, preferred_element_type=jnp.float32)
    return y[:rows] + (y[rows : 2 * rows] + y[2 * rows :])


def pack_strips(times):
    width = times[0][0].shape[-1]
    lane, sub = iota((PH, width), 1), iota((PH, width), 0)
    block = jnp.zeros((PH, width), jnp.float32)
    span = (RR - 1) * PW
    inner = (lane >= LEFT) & (lane < LEFT + span)
    for t, fields in enumerate(times):
        surface, eastward, southward = fields
        for band in range(K):
            first = band * FINE_ROWS + TOP
            east8 = eastward[first : first + PH, :]
            level8 = surface[first : first + PH, :]
            for j in range(RR - 1):
                column = LEFT + j * PW
                west_lane = t * (LEFT + span) + band * 2 * (RR - 1) + j
                east_lane = west_lane + RR - 1
                block = jnp.where(
                    lane == west_lane, pltpu.roll(east8, (west_lane - column + 1) % width, 1), block
                )
                block = jnp.where(
                    lane == east_lane, pltpu.roll(level8, (east_lane - column - PW) % width, 1), block
                )
            row = (t * K + band) * 2
            block = jnp.where(inner & (sub == row), southward[first - 1 : first, :], block)
            block = jnp.where(inner & (sub == row + 1), surface[first + PH : first + PH + 1, :], block)
    return block


def pack_sides(free, band):
    width = free.shape[-1]
    lane = iota((PH, width), 1)
    block = jnp.zeros((PH, width), jnp.float32)
    first = band * FINE_ROWS + TOP
    for i, f in enumerate(SIDE_FIELDS):
        values = free[f, first : first + PH, :]
        for j in range(RR - 1):
            column = LEFT + j * PW
            target = j * 8 * len(SIDE_FIELDS) + 8 * i
            for side, source in ((0, column - 4), (4, column + PW)):
                at = target + side
                block = jnp.where(
                    (lane >= at) & (lane < at + 4), pltpu.roll(values, (at - source) % width, 1), block
                )
    return block


def row_sums(x):
    width = x.shape[1]
    sub = iota((8, width), 0)
    out = jnp.zeros((8, width), jnp.float32)
    for v in range(x.shape[0] // 8):
        piece = x[8 * v : 8 * v + 8]
        piece = piece + pltpu.roll(piece, 1, 0)
        piece = piece + pltpu.roll(piece, 2, 0)
        out = jnp.where(sub == 2 * v, piece[3:4], out)
        out = jnp.where(sub == 2 * v + 1, piece[7:8], out)
    return out


def row_picks(x):
    width = x.shape[1]
    sub = iota((8, width), 0)
    out = jnp.zeros((8, width), jnp.float32)
    for v in range(x.shape[0] // 8):
        out = jnp.where(sub == 2 * v, x[8 * v + 3 : 8 * v + 4], out)
        out = jnp.where(sub == 2 * v + 1, x[8 * v + 7 : 8 * v + 8], out)
    return out


def grow_rows(x):
    sub = iota(x.shape, 0)
    return jnp.concatenate(
        [jnp.where(sub < 4, x[2 * v : 2 * v + 1], x[2 * v + 1 : 2 * v + 2]) for v in range(RR)], axis=0
    )


def kernel(
    n_row,
    n_nest,
    place_ref,
    host_ref,
    state_hbm,
    depth_hbm,
    open_hbm,
    out_ref,
    state_ref,
    depth_ref,
    open_ref,
    load_sems,
    st,
    free,
    first_out,
    first_in,
    bulk_out,
    bulk_in,
    edge_out,
    edge_in,
    ret_out,
    ret_in,
    side_out,
    west_in,
    east_in,
    ext,
    courant_ref,
    ghost_cols,
    ghost_rows,
    patch,
    wet,
    later,
    edge_now,
    ret_now,
    first_sems,
    bulk_sems,
    edge_send,
    edge_recv,
    ret_send,
    ret_recv,
    halo_send,
    halo_recv,
):
    tiles = n_row * n_nest
    nests = place_ref.shape[0]
    sec, row, col = lax.axis_index("sec"), lax.axis_index("row"), lax.axis_index("nest")
    tile = row * n_nest + col
    is_outer = sec == 0
    has_west, has_east = col > 0, col < n_nest - 1
    has_north, has_south = row > 0, row < n_row - 1
    west, east = (sec, row, col - 1), (sec, row, col + 1)
    north, south = (sec, row - 1, col), (sec, row + 1, col)
    links = ((has_west, west), (has_east, east), (has_north, north), (has_south, south))
    height, width = state_ref.shape[2], state_ref.shape[3]

    barrier = pltpu.get_barrier_semaphore()

    @pl.loop(0, tiles)
    def _(i):
        t = lax.rem(tile + i, tiles)
        pl.semaphore_signal(
            barrier, inc=1, device_id=(1 - sec, t // n_nest, lax.rem(t, n_nest)), device_id_type=MESH
        )

    loads = [
        pltpu.make_async_copy(source, target, load_sems.at[i])
        for i, (source, target) in enumerate(
            ((state_hbm, state_ref), (depth_hbm, depth_ref), (open_hbm, open_ref))
        )
    ]
    for load in loads:
        load.start()

    def send_to(section, count, src, dst, send_sem, recv_sem):
        @pl.loop(0, tiles)
        def _(i):
            t = lax.rem(2 * tiles - 1 - tile - i, tiles)

            def go():
                pltpu.make_async_remote_copy(
                    src_ref=src,
                    dst_ref=dst,
                    send_sem=send_sem,
                    recv_sem=recv_sem,
                    device_id=(section, t // n_nest, lax.rem(t, n_nest)),
                    device_id_type=MESH,
                ).start()

            if count == tiles:
                go()
            else:
                pl.when(t != tile)(go)

    def send_all(src, dst, send_sem, recv_sem):
        send_to(1 - sec, tiles, src, dst, send_sem, recv_sem)

    def wait_all(whole, sem):
        pltpu.make_async_copy(whole, whole, sem).wait()

    @pl.when(is_outer)
    def _():
        for present, device in links:

            @pl.when(present)
            def _():
                pl.semaphore_signal(barrier, inc=1, device_id=device, device_id_type=MESH)

        slots, covers = [], []
        for p in range(NPOS):
            slot, cover = jnp.int32(0), jnp.int32(0)
            for n in range(nests):
                hit = place_ref[n] == tile * NPOS + p
                slot = jnp.where(hit, host_ref[n], slot)
                cover = jnp.where(hit, 1, cover)
            slots.append(slot)
            covers.append(cover)
        for load in loads:
            load.wait()
        for i in range(2):
            free[7 + i] = jnp.where(open_ref[0, i] > 0, depth_ref[0, i], 0.0)
        levels = []
        for band in range(K):
            lo = band * FINE_ROWS
            hi = lo + BAND
            old = [state_ref[0, f, lo:hi] for f in range(3)]
            level = new_level_ring(old[0], old[1], old[2], COURANT)
            flux_e, flux_s = new_fluxes_ring(old[1], old[2], level, free[7, lo:hi], free[8, lo:hi])
            free[0, lo:hi] = level
            free[1, lo:hi] = flux_e
            free[2, lo:hi] = flux_s
        first_out[...] = pack_strips(
            [[ref.at[f] for f in range(3)] for ref in (state_ref.at[0], free)]
        )
        for band in range(K):
            lo = band * FINE_ROWS
            hi = lo + BAND
            level, flux_e, flux_s = [free[f, lo:hi] for f in range(3)]
            for i in range(2):
                east_gap = flux_e - pltpu.roll(flux_e, 1, 1)
                free[3 + i, lo:hi] = level - COURANT * (east_gap + flux_s)
                level = level - COURANT * (east_gap + (flux_s - pltpu.roll(flux_s, 1, 0)))
                if i == 0:
                    flux_e, flux_s = new_fluxes_ring(
                        flux_e, flux_s, level, free[7, lo:hi], free[8, lo:hi]
                    )
            free[5, lo:hi] = level
            free[6, lo:hi] = flux_s
        for band in range(K):
            first = band * FINE_ROWS + TOP
            for part, chosen in enumerate((ROWS_EARLY, ROWS_LATE)):
                for i, (f, shift) in enumerate(chosen):
                    at = first + shift
                    bulk_out[3 * band + part, i : i + 1] = free[f, at : at + 1]
            bulk_out[3 * band + 2] = pack_sides(free, band)

        peers = jnp.int32(tiles)
        for present, _device in links:
            peers = peers + jnp.where(present, 1, 0)
        pl.semaphore_wait(barrier, peers)
        send_all(first_out, first_in.at[tile], first_sems.at[0], first_sems.at[1])
        send_all(bulk_out, bulk_in.at[tile], bulk_sems.at[0], bulk_sems.at[1])

        def halo(kind, src, dst, device):
            return pltpu.make_async_remote_copy(
                src_ref=src,
                dst_ref=dst,
                send_sem=halo_send.at[kind],
                recv_sem=halo_recv.at[kind],
                device_id=device,
                device_id_type=MESH,
            )

        fields = [state_ref.at[0, f] for f in range(3)] + [free.at[7 + i] for i in range(2)]
        lane = iota((height, width), 1)
        packed = jnp.zeros((height, width), jnp.float32)
        for i, field in enumerate(fields):
            x = field[...]
            ext[i, 0:height, 0:width] = x
            packed = jnp.where((lane >= 8 * i) & (lane < 8 * i + 4), pltpu.roll(x, 8 * i, 1), packed)
            packed = jnp.where(
                (lane >= 8 * i + 4) & (lane < 8 * i + 8), pltpu.roll(x, 8 * i + 8, 1), packed
            )
        side_out[...] = packed
        to_east = halo(0, side_out, west_in, east)
        to_west = halo(1, side_out, east_in, west)
        top, bottom = pl.ds(0, HALO), pl.ds(height - HALO, HALO)
        below, above = pl.ds(height, HALO), pl.ds(height + HALO, HALO)
        to_south = halo(2, ext.at[:, bottom], ext.at[:, above], south)
        to_north = halo(3, ext.at[:, top], ext.at[:, below], north)

        for present, copy in ((has_east, to_east), (has_west, to_west)):

            @pl.when(present)
            def _():
                copy.start()

        for present, buffer in ((has_west, west_in), (has_east, east_in)):

            @pl.when(jnp.logical_not(present))
            def _():
                buffer[...] = jnp.zeros(buffer.shape, jnp.float32)

        for present, where in ((has_south, below), (has_north, above)):

            @pl.when(jnp.logical_not(present))
            def _():
                ext[:, where] = jnp.zeros((len(fields), HALO, 2 * width), jnp.float32)

        rows, lanes = iota((height + 2 * HALO, 2 * width), 0), iota((height + 2 * HALO, 2 * width), 1)

        def allowed(region, present):
            return jnp.logical_not(region) | (jnp.full(rows.shape, present.astype(jnp.int32)) > 0)

        inside = allowed((rows >= height) & (rows < height + HALO), has_south)
        inside = inside & allowed(rows >= height + HALO, has_north)
        inside = inside & allowed((lanes >= width) & (lanes < width + width // 2), has_east)
        inside = inside & allowed(lanes >= width + width // 2, has_west)
        courant_ref[...] = jnp.where(inside, COURANT, 0.0)

        for present, copy in ((has_west, to_east), (has_east, to_west)):

            @pl.when(present)
            def _():
                copy.wait_recv()

        from_west, from_east = west_in[...], east_in[...]
        for i in range(len(fields)):
            ext[i, 0:height, width:] = jnp.where(
                lane < 4,
                pltpu.roll(from_east, (width - 8 * i) % width, 1),
                jnp.where(lane >= width - 4, pltpu.roll(from_west, width - 8 - 8 * i, 1), 0.0),
            )

        for present, copy in ((has_south, to_south), (has_north, to_north)):

            @pl.when(present)
            def _():
                copy.start()

        for present, copy in ((has_north, to_south), (has_south, to_north)):

            @pl.when(present)
            def _():
                copy.wait_recv()

        for present, copy in (
            (has_east, to_east),
            (has_west, to_west),
            (has_south, to_south),
            (has_north, to_north),
        ):

            @pl.when(present)
            def _():
                copy.wait_send()

        @pl.loop(0, STEPS)
        def _(s):
            surface, eastward, southward = ext[0], ext[1], ext[2]
            level = new_level_ring(surface, eastward, southward, courant_ref[...])
            flux_e, flux_s = new_fluxes_ring(eastward, southward, level, ext[3], ext[4])
            ext[0] = level
            ext[1] = flux_e
            ext[2] = flux_s

            wait_all(ret_in.at[s], ret_recv.at[s])
            ret_now[...] = ret_in[s]
            lane = iota((PH, width), 1)
            for band in range(K):
                first = band * FINE_ROWS + TOP
                merged = [ext[f, first : first + PH, 0:width] for f in range(3)]
                for j in range(RR - 1):
                    p = band * (RR - 1) + j
                    column = LEFT + j * PW
                    block = ret_now[slots[p]]
                    mask = (
                        (lane >= column)
                        & (lane < column + PW)
                        & (jnp.full((PH, width), covers[p], jnp.int32) > 0)
                    )
                    for f in range(3):
                        shifted = pltpu.roll(block, (column - f * PW) % width, 1)
                        merged[f] = jnp.where(mask, shifted, merged[f])
                for f in range(3):
                    ext[f, first : first + PH, 0:width] = merged[f]

        for f in range(3):
            out_ref[0, f] = ext[f, 0:height, 0:width]

        wait_all(first_in, first_sems.at[0])
        wait_all(bulk_in, bulk_sems.at[0])

    @pl.when(jnp.logical_not(is_outer))
    def _():
        @pl.loop(0, tiles - 1)
        def _(i):
            t = lax.rem(tile + i + 1, tiles)
            pl.semaphore_signal(
                barrier, inc=1, device_id=(sec, t // n_nest, lax.rem(t, n_nest)), device_id_type=MESH
            )

        spots, lives = [], []
        for k in range(K):
            spot, live = jnp.int32(0), jnp.int32(0)
            for n in range(nests):
                hit = host_ref[n] == tile * K + k
                spot = jnp.where(hit, place_ref[n], spot)
                live = jnp.where(hit, 1, live)
            spots.append(spot)
            lives.append(live)
        homes = [spot // NPOS for spot in spots]
        bands = [lax.rem(spot, NPOS) // (RR - 1) for spot in spots]
        columns = [lax.rem(spot, RR - 1) for spot in spots]
        near = []
        for k in range(K):
            pair = []
            for side in (-1, 1):
                inside = (columns[k] + side >= 0) & (columns[k] + side < RR - 1)
                slot, cover = jnp.int32(0), jnp.int32(0)
                for n in range(nests):
                    hit = inside & (place_ref[n] == spots[k] + side)
                    slot = jnp.where(hit, host_ref[n], slot)
                    cover = jnp.where(hit, 1, cover)
                pair.append((slot // K, lax.rem(slot, K), cover))
            near.append(pair)

        gather_from = iota((3 * width, 2 * width), 0)
        gather_to = iota((3 * width, 2 * width), 1)
        field, lane_in = gather_from // width, lax.rem(gather_from, width)
        weight = jnp.where(
            field == 0,
            1.0 / (RR * RR),
            jnp.where((field == 2) | (lax.rem(lane_in, RR) == RR - 1), 1.0 / RR, 0.0),
        )
        gather = jnp.where(gather_to == field * PW + lane_in // RR, weight, 0.0)
        for i, (f, c) in enumerate(EDGES):
            gather = gather + jnp.where(
                (gather_to >= width)
                & (lax.rem(gather_to, 16) == i)
                & (field == f)
                & (lane_in // RR == c),
                weight,
                0.0,
            )
        widen = (
            iota((width, width), 0) == NEAR + iota((width, width), 1) // RR
        ).astype(jnp.float32)
        gather, widen = [m.astype(jnp.bfloat16) for m in (gather, widen)]
        lane, sub = iota((PH, width), 1), iota((PH, width), 0)
        own_lanes = (lane >= NEAR) & (lane < NEAR + PW)

        def by_column(k, choices):
            out = choices[0]
            for j in range(1, len(choices)):
                out = jnp.where(jnp.full(out.shape, columns[k], jnp.int32) == j, choices[j], out)
            return out

        def centred(x, k):
            return by_column(
                k, [pltpu.roll(x, (NEAR - LEFT - j * PW) % width, 1) for j in range(RR - 1)]
            )

        def pick_lane(block, index):
            return jnp.sum(jnp.where(lane == index, block, 0.0), axis=1, keepdims=True)

        def pick_row(block, index):
            return jnp.sum(jnp.where(sub == index, block, 0.0), axis=0, keepdims=True)

        for load in loads:
            load.wait()
        st[...] = state_ref[0]
        pl.semaphore_wait(barrier, 2 * tiles - 1)
        wait_all(first_in, first_sems.at[1])
        lines = jnp.zeros((PH, width), jnp.float32)
        for k in range(K):
            block = first_in[homes[k]]
            level_block = centred(block, k)
            for t in range(2):
                at = t * (LEFT + (RR - 1) * PW) + bands[k] * (2 * (RR - 1)) + columns[k]
                cols = jnp.where(lane < width // 2, pick_lane(block, at), pick_lane(block, at + RR - 1))
                ghost_cols[t, k] = grow_rows(cols)
                for i in range(2):
                    line = pick_row(level_block, 2 * (t * K + bands[k]) + i)
                    lines = jnp.where(sub == (t * K + k) * 2 + i, line, lines)
        lines = dot_by(lines, widen)
        for t in range(2):
            for k in range(K):
                at = (t * K + k) * 2
                ghost_rows[t, k, 0:2] = lines[at : at + 2]

        @pl.loop(0, STEPS)
        def _(s):
            lane, sub = iota((PH, width), 1), iota((PH, width), 0)
            slots = [pl.ds(k * FINE_ROWS, FINE_ROWS) for k in range(K)]
            old_cols, new_cols = [[ghost_cols[t, k] for k in range(K)] for t in range(2)]
            old_rows, new_rows = [[ghost_rows[t, k] for k in range(K)] for t in range(2)]
            fields = [[st[f, slot] for f in range(3)] for slot in slots]
            depths = [[depth_ref[0, i, slot] for i in range(2)] for slot in slots]
            opens = [[open_ref[0, i, slot].astype(jnp.float32) for i in range(2)] for slot in slots]
            for m in range(1, RR + 1):
                for k in range(K):
                    cols = old_cols[k] + (m / RR) * (new_cols[k] - old_cols[k])
                    rows = old_rows[k] + (m / RR) * (new_rows[k] - old_rows[k])
                    surface, eastward, southward = fields[k]
                    surface = new_level(surface, eastward, southward, cols, rows[0:1])
                    eastward, southward = new_fluxes(
                        eastward, southward, surface, cols, rows[1:2], depths[k], opens[k]
                    )
                    fields[k] = [surface, eastward, southward]
            sums = dot_by(
                jnp.concatenate(
                    [
                        jnp.concatenate([row_sums(s_), row_sums(e_), row_picks(q_)], axis=1)
                        for s_, e_, q_ in fields
                    ],
                    axis=0,
                ),
                gather,
            )
            coarse = [sums[k * PH : (k + 1) * PH, 0:width] for k in range(K)]

            @pl.when(s < STEPS - 1)
            def _():
                for k in range(K):
                    edges = sums[k * PH : (k + 1) * PH, width:]
                    edge_out[s, k : k + 1] = jnp.sum(
                        jnp.where(lane // 16 == sub, edges, 0.0), axis=0, keepdims=True
                    )
                send_to(
                    1,
                    tiles - 1,
                    edge_out.at[s, pl.ds(0, K)],
                    edge_in.at[s, tile, pl.ds(0, K)],
                    edge_send.at[s],
                    edge_recv.at[s],
                )

            for k in range(K):
                ret_out[s, k] = coarse[k]
            send_all(ret_out.at[s], ret_in.at[s, pl.ds(tile * K, K)], ret_send.at[s], ret_recv.at[s])
            for k in range(K):
                for f in range(3):
                    st[f, slots[k]] = fields[k][f]

            @pl.when(s == 0)
            def _():
                wait_all(bulk_in, bulk_sems.at[1])
                for k in range(K):
                    early, late = [centred(bulk_in[homes[k], 3 * bands[k] + i], k) for i in range(2)]
                    flat = bulk_in[homes[k], 3 * bands[k] + 2]
                    sides = by_column(
                        k,
                        [pltpu.roll(flat, (-8 * len(SIDE_FIELDS) * j) % width, 1) for j in range(RR - 1)],
                    )

                    def tile_of(block, spots):
                        out = jnp.zeros((PH, width), jnp.float32)
                        for target, source in spots:
                            out = jnp.where(sub == target, block[source : source + 1], out)
                        return out

                    outside = [
                        tile_of(early, ((0, 0), (1, 1), (7, 5))),
                        tile_of(early, ((0, 2), (7, 6))),
                        tile_of(early, ((0, 3), (6, 4), (7, 7))),
                        tile_of(late, ((0, 3), (7, 4))),
                        tile_of(late, ((0, 5), (6, 6), (7, 7))),
                    ]
                    for i in range(5):
                        beside = jnp.where(
                            lane < NEAR + PW // 2,
                            pltpu.roll(sides, (NEAR - 4 - 8 * i) % width, 1),
                            pltpu.roll(sides, (NEAR + PW - 4 - 8 * i) % width, 1),
                        )
                        target = patch.at[k, i] if i < 3 else wet.at[k, i - 3]
                        target[0:PH] = beside
                        target[PH : 2 * PH] = outside[i]
                    later[k, 0] = tile_of(late, ((1, 0), (6, 1)))
                    later[k, 1] = tile_of(late, ((5, 2), (6, 2)))

            @pl.when(s == 1)
            def _():
                given = (sub == 1) | (sub == 5) | (sub == 6)
                for k in range(K):
                    for f, value in enumerate((later[k, 0], 0.0, later[k, 1])):
                        patch[k, f, PH : 2 * PH] = jnp.where(given, value, patch[k, f, PH : 2 * PH])

            @pl.when(s < STEPS - 1)
            def _():
                for k in range(K):
                    ghost_cols[0, k] = new_cols[k]
                    ghost_rows[0, k] = new_rows[k]
                    for f in range(3):
                        patch[k, f, 0:PH] = jnp.where(
                            own_lanes, pltpu.roll(coarse[k], (NEAR - f * PW) % width, 1), patch[k, f, 0:PH]
                        )
                wait_all(edge_in.at[s, pl.ds(0, tiles - 1), pl.ds(0, K)], edge_recv.at[s])
                edge_now[:, 0:K] = edge_in[s, :, 0:K]
                edge_now[tile, 0:K] = edge_out[s, 0:K]
                lines = jnp.zeros((PH, width), jnp.float32)
                for k in range(K):
                    (left_at, left_slot, left_on), (right_at, right_slot, right_on) = near[k]
                    left = edge_now[left_at, pl.ds(left_slot, 1)]
                    right = edge_now[right_at, pl.ds(right_slot, 1)]
                    both = jnp.where(lax.rem(lane, 16) < LEFT_EDGES, left, right)
                    items = both
                    for r in range(1, PH):
                        items = jnp.where(sub == r, pltpu.roll(both, width - 16 * r, 1), items)
                    on_left = jnp.full((PH, width), left_on, jnp.int32) > 0
                    on_right = jnp.full((PH, width), right_on, jnp.int32) > 0
                    state = []
                    for f, (a, left_first, b, right_last) in enumerate(
                        ((31, NEAR - 1, 59, NEAR + PW), (29, NEAR - 2, 58, NEAR + PW), (27, NEAR - 2, 57, NEAR + PW + 1))
                    ):
                        x = patch[k, f, 0:PH]
                        x = jnp.where(
                            on_left & (lane >= left_first) & (lane < NEAR), pltpu.roll(items, a, 1), x
                        )
                        x = jnp.where(
                            on_right & (lane >= NEAR + PW) & (lane <= right_last),
                            pltpu.roll(items, b, 1),
                            x,
                        )
                        state.append(jnp.concatenate([x, patch[k, f, PH : 2 * PH]], axis=0))
                    level = new_level_ring(state[0], state[1], state[2], COURANT)
                    flux_e, flux_s = new_fluxes_ring(state[1], state[2], level, wet[k, 0], wet[k, 1])
                    for f, x in enumerate((level, flux_e, flux_s)):
                        patch[k, f] = x
                    cols = jnp.where(
                        lane < width // 2,
                        pltpu.roll(flux_e[0:PH], width - NEAR + 1, 1),
                        pltpu.roll(level[0:PH], width - 1 - NEAR - PW, 1),
                    )
                    ghost_cols[1, k] = grow_rows(cols)
                    lines = jnp.where(sub == 2 * k, flux_s[2 * PH - 1 : 2 * PH], lines)
                    lines = jnp.where(sub == 2 * k + 1, level[PH : PH + 1], lines)
                lines = dot_by(lines, widen)
                for k in range(K):
                    ghost_rows[1, k, 0:2] = lines[2 * k : 2 * k + 2]

        for k in range(K):
            slot = pl.ds(k * FINE_ROWS, FINE_ROWS)
            live = jnp.full((FINE_ROWS, width), lives[k], jnp.int32) > 0
            for f in range(3):
                out_ref[0, f, slot] = jnp.where(live, st[f, slot], state_ref[0, f, slot])

        for s in range(STEPS):
            wait_all(ret_in.at[s], ret_send.at[s])
        for s in range(STEPS - 1):
            wait_all(edge_in.at[s, pl.ds(0, tiles - 1), pl.ds(0, K)], edge_send.at[s])


def on_device(n_row, n_nest, ocean_state, face_depth, face_open, nest_place, nest_host):
    tiles = n_row * n_nest
    height, width = ocean_state.shape[2:]
    f32 = jnp.float32
    vmem = pl.BlockSpec(memory_space=pltpu.VMEM)
    hbm = pl.BlockSpec(memory_space=pl.ANY)
    smem = pl.BlockSpec(memory_space=pltpu.SMEM)
    dma = pltpu.SemaphoreType.DMA
    return pl.pallas_call(
        functools.partial(kernel, n_row, n_nest),
        out_shape=jax.ShapeDtypeStruct(ocean_state.shape, f32),
        in_specs=[smem, smem, hbm, hbm, hbm],
        out_specs=vmem,
        scratch_shapes=[
            pltpu.VMEM(ocean_state.shape, f32),
            pltpu.VMEM(face_depth.shape, f32),
            pltpu.VMEM(face_open.shape, jnp.int32),
            dma((3,)),
            pltpu.VMEM((3, height, width), f32),
            pltpu.VMEM((9, height, width), f32),
            pltpu.VMEM((PH, width), f32),
            pltpu.VMEM((tiles, PH, width), f32),
            pltpu.VMEM((3 * K, PH, width), f32),
            pltpu.VMEM((tiles, 3 * K, PH, width), f32),
            pltpu.VMEM((STEPS - 1, PH, width), f32),
            pltpu.VMEM((STEPS - 1, tiles, PH, width), f32),
            pltpu.VMEM((STEPS, K, PH, width), f32),
            pltpu.VMEM((STEPS, tiles * K, PH, width), f32),
            pltpu.VMEM((height, width), f32),
            pltpu.VMEM((height, width), f32),
            pltpu.VMEM((height, width), f32),
            pltpu.VMEM((5, height + 2 * HALO, 2 * width), f32),
            pltpu.VMEM((height + 2 * HALO, 2 * width), f32),
            pltpu.VMEM((2, K, FINE_ROWS, width), f32),
            pltpu.VMEM((2, K, PH, width), f32),
            pltpu.VMEM((K, 3, 2 * PH, width), f32),
            pltpu.VMEM((K, 2, 2 * PH, width), f32),
            pltpu.VMEM((K, 2, PH, width), f32),
            pltpu.VMEM((tiles, PH, width), f32),
            pltpu.VMEM((tiles * K, PH, width), f32),
            dma((2,)),
            dma((2,)),
            dma((STEPS - 1,)),
            dma((STEPS - 1,)),
            dma((STEPS,)),
            dma((STEPS,)),
            dma((4,)),
            dma((4,)),
        ],
        compiler_params=pltpu.CompilerParams(collective_id=0, has_side_effects=True),
    )(nest_place, nest_host, ocean_state, face_depth, face_open)


def solution(mesh):
    field = P("sec", None, "row", "nest")
    return jax.shard_map(
        functools.partial(on_device, mesh.shape["row"], mesh.shape["nest"]),
        mesh=mesh,
        in_specs=(field, field, field, P(), P()),
        out_specs=field,
        check_vma=False,
    )
```

```python
import functools

import jax
import jax.numpy as jnp
from jax import lax
from jax.experimental import pallas as pl
from jax.experimental.pallas import tpu as pltpu
from jax.sharding import PartitionSpec as P

PH = 8
PW = 32
RR = 4
K = 2
STEPS = 4
NPOS = K * (RR - 1)
COURANT = 0.3
MESH = pl.DeviceIdType.MESH
FINE_ROWS = RR * PH
TOP = (RR - 1) * PH // 2
LEFT = PW // 2
NEAR = PW
EDGES = (
    (0, PW - 1),
    (1, PW - 2),
    (1, PW - 1),
    (2, PW - 2),
    (2, PW - 1),
    (0, 0),
    (1, 0),
    (2, 0),
    (2, 1),
)
LEFT_EDGES = 5
BAND = (TOP + PH + STEPS + 7) // 8 * 8
HALO = 8
ROWS_EARLY = ((0, PH), (3, PH + 1), (1, PH), (2, PH), (2, -2), (0, -1), (1, -1), (2, -1))
ROWS_LATE = ((4, PH + 1), (5, -2), (6, -2), (7, PH), (7, -1), (8, PH), (8, -2), (8, -1))
SIDE_FIELDS = (0, 1, 2, 7, 8)


def iota(shape, dim):
    return lax.broadcasted_iota(jnp.int32, shape, dim)


def new_level(surface, eastward, southward, west_ghost, north_ghost):
    rows, cols = iota(surface.shape, 0), iota(surface.shape, 1)
    east_behind = jnp.where(cols == 0, west_ghost, pltpu.roll(eastward, 1, 1))
    south_behind = jnp.where(rows == 0, north_ghost, pltpu.roll(southward, 1, 0))
    return surface - COURANT * ((eastward - east_behind) + (southward - south_behind))


def new_fluxes(eastward, southward, level, east_ghost, south_ghost, depth, opened):
    height, width = level.shape
    rows, cols = iota(level.shape, 0), iota(level.shape, 1)
    level_east = jnp.where(cols == width - 1, east_ghost, pltpu.roll(level, width - 1, 1))
    level_south = jnp.where(rows == height - 1, south_ghost, pltpu.roll(level, height - 1, 0))
    east = opened[0] * (
        eastward - COURANT * (depth[0] + 0.5 * (level + level_east)) * (level_east - level)
    )
    south = opened[1] * (
        southward - COURANT * (depth[1] + 0.5 * (level + level_south)) * (level_south - level)
    )
    return east, south


def new_level_ring(surface, eastward, southward, courant):
    east_gap = eastward - pltpu.roll(eastward, 1, 1)
    south_gap = southward - pltpu.roll(southward, 1, 0)
    return surface - courant * (east_gap + south_gap)


def new_fluxes_ring(eastward, southward, level, wet_east, wet_south):
    height, width = level.shape
    level_east = pltpu.roll(level, width - 1, 1)
    level_south = pltpu.roll(level, height - 1, 0)
    east = eastward - COURANT * (wet_east + 0.5 * (level + level_east)) * (level_east - level)
    south = southward - COURANT * (wet_south + 0.5 * (level + level_south)) * (level_south - level)
    return jnp.where(wet_east > 0, east, 0.0), jnp.where(wet_south > 0, south, 0.0)


def parts(x):
    high = x.astype(jnp.bfloat16).astype(jnp.float32)
    rest = x - high
    middle = rest.astype(jnp.bfloat16).astype(jnp.float32)
    return high, middle, rest - middle


def dot_by(x, chosen):
    rows = x.shape[0]
    stacked = jnp.concatenate(parts(x), axis=0).astype(jnp.bfloat16)
    y = jnp.dot(stacked, chosen, preferred_element_type=jnp.float32)
    return y[:rows] + (y[rows : 2 * rows] + y[2 * rows :])


def pack_strips(times):
    width = times[0][0].shape[-1]
    lane, sub = iota((PH, width), 1), iota((PH, width), 0)
    block = jnp.zeros((PH, width), jnp.float32)
    span = (RR - 1) * PW
    inner = (lane >= LEFT) & (lane < LEFT + span)
    for t, fields in enumerate(times):
        surface, eastward, southward = fields
        for band in range(K):
            first = band * FINE_ROWS + TOP
            east8 = eastward[first : first + PH, :]
            level8 = surface[first : first + PH, :]
            for j in range(RR - 1):
                column = LEFT + j * PW
                west_lane = t * (LEFT + span) + band * 2 * (RR - 1) + j
                east_lane = west_lane + RR - 1
                block = jnp.where(
                    lane == west_lane, pltpu.roll(east8, (west_lane - column + 1) % width, 1), block
                )
                block = jnp.where(
                    lane == east_lane, pltpu.roll(level8, (east_lane - column - PW) % width, 1), block
                )
            row = (t * K + band) * 2
            block = jnp.where(inner & (sub == row), southward[first - 1 : first, :], block)
            block = jnp.where(inner & (sub == row + 1), surface[first + PH : first + PH + 1, :], block)
    return block


def pack_sides(free, band):
    width = free.shape[-1]
    lane = iota((PH, width), 1)
    block = jnp.zeros((PH, width), jnp.float32)
    first = band * FINE_ROWS + TOP
    for i, f in enumerate(SIDE_FIELDS):
        values = free[f, first : first + PH, :]
        for j in range(RR - 1):
            column = LEFT + j * PW
            target = j * 8 * len(SIDE_FIELDS) + 8 * i
            for side, source in ((0, column - 4), (4, column + PW)):
                at = target + side
                block = jnp.where(
                    (lane >= at) & (lane < at + 4), pltpu.roll(values, (at - source) % width, 1), block
                )
    return block


def row_sums(x):
    width = x.shape[1]
    sub = iota((8, width), 0)
    out = jnp.zeros((8, width), jnp.float32)
    for v in range(x.shape[0] // 8):
        piece = x[8 * v : 8 * v + 8]
        piece = piece + pltpu.roll(piece, 1, 0)
        piece = piece + pltpu.roll(piece, 2, 0)
        out = jnp.where(sub == 2 * v, piece[3:4], out)
        out = jnp.where(sub == 2 * v + 1, piece[7:8], out)
    return out


def row_picks(x):
    width = x.shape[1]
    sub = iota((8, width), 0)
    out = jnp.zeros((8, width), jnp.float32)
    for v in range(x.shape[0] // 8):
        out = jnp.where(sub == 2 * v, x[8 * v + 3 : 8 * v + 4], out)
        out = jnp.where(sub == 2 * v + 1, x[8 * v + 7 : 8 * v + 8], out)
    return out


def grow_rows(x):
    sub = iota(x.shape, 0)
    return jnp.concatenate(
        [jnp.where(sub < 4, x[2 * v : 2 * v + 1], x[2 * v + 1 : 2 * v + 2]) for v in range(RR)], axis=0
    )


def kernel(
    n_row,
    n_nest,
    place_ref,
    host_ref,
    state_hbm,
    depth_hbm,
    open_hbm,
    out_ref,
    state_ref,
    depth_ref,
    open_ref,
    load_sems,
    st,
    free,
    first_out,
    first_in,
    bulk_out,
    bulk_in,
    edge_out,
    edge_in,
    ret_out,
    ret_in,
    side_out,
    west_in,
    east_in,
    ext,
    courant_ref,
    ghost_cols,
    ghost_rows,
    patch,
    wet,
    later,
    edge_now,
    ret_now,
    first_sems,
    bulk_sems,
    edge_send,
    edge_recv,
    ret_send,
    ret_recv,
    halo_send,
    halo_recv,
):
    tiles = n_row * n_nest
    nests = place_ref.shape[0]
    sec, row, col = lax.axis_index("sec"), lax.axis_index("row"), lax.axis_index("nest")
    tile = row * n_nest + col
    is_outer = sec == 0
    has_west, has_east = col > 0, col < n_nest - 1
    has_north, has_south = row > 0, row < n_row - 1
    west, east = (sec, row, col - 1), (sec, row, col + 1)
    north, south = (sec, row - 1, col), (sec, row + 1, col)
    links = ((has_west, west), (has_east, east), (has_north, north), (has_south, south))
    height, width = state_ref.shape[2], state_ref.shape[3]

    barrier = pltpu.get_barrier_semaphore()

    @pl.loop(0, tiles)
    def _(i):
        t = lax.rem(tile + i, tiles)
        pl.semaphore_signal(
            barrier, inc=1, device_id=(1 - sec, t // n_nest, lax.rem(t, n_nest)), device_id_type=MESH
        )

    loads = [
        pltpu.make_async_copy(source, target, load_sems.at[i])
        for i, (source, target) in enumerate(
            ((state_hbm, state_ref), (depth_hbm, depth_ref), (open_hbm, open_ref))
        )
    ]
    for load in loads:
        load.start()

    def send_to(section, count, src, dst, send_sem, recv_sem):
        @pl.loop(0, tiles)
        def _(i):
            t = lax.rem(2 * tiles - 1 - tile - i, tiles)

            def go():
                pltpu.make_async_remote_copy(
                    src_ref=src,
                    dst_ref=dst,
                    send_sem=send_sem,
                    recv_sem=recv_sem,
                    device_id=(section, t // n_nest, lax.rem(t, n_nest)),
                    device_id_type=MESH,
                ).start()

            if count == tiles:
                go()
            else:
                pl.when(t != tile)(go)

    def send_all(src, dst, send_sem, recv_sem):
        send_to(1 - sec, tiles, src, dst, send_sem, recv_sem)

    def wait_all(whole, sem):
        pltpu.make_async_copy(whole, whole, sem).wait()

    @pl.when(is_outer)
    def _():
        for present, device in links:

            @pl.when(present)
            def _():
                pl.semaphore_signal(barrier, inc=1, device_id=device, device_id_type=MESH)

        slots, covers = [], []
        for p in range(NPOS):
            slot, cover = jnp.int32(0), jnp.int32(0)
            for n in range(nests):
                hit = place_ref[n] == tile * NPOS + p
                slot = jnp.where(hit, host_ref[n], slot)
                cover = jnp.where(hit, 1, cover)
            slots.append(slot)
            covers.append(cover)
        for load in loads:
            load.wait()
        for i in range(2):
            free[7 + i] = jnp.where(open_ref[0, i] > 0, depth_ref[0, i], 0.0)
        levels = []
        for band in range(K):
            lo = band * FINE_ROWS
            hi = lo + BAND
            old = [state_ref[0, f, lo:hi] for f in range(3)]
            level = new_level_ring(old[0], old[1], old[2], COURANT)
            flux_e, flux_s = new_fluxes_ring(old[1], old[2], level, free[7, lo:hi], free[8, lo:hi])
            free[0, lo:hi] = level
            free[1, lo:hi] = flux_e
            free[2, lo:hi] = flux_s
        first_out[...] = pack_strips(
            [[ref.at[f] for f in range(3)] for ref in (state_ref.at[0], free)]
        )
        for band in range(K):
            lo = band * FINE_ROWS
            hi = lo + BAND
            level, flux_e, flux_s = [free[f, lo:hi] for f in range(3)]
            for i in range(2):
                east_gap = flux_e - pltpu.roll(flux_e, 1, 1)
                free[3 + i, lo:hi] = level - COURANT * (east_gap + flux_s)
                level = level - COURANT * (east_gap + (flux_s - pltpu.roll(flux_s, 1, 0)))
                if i == 0:
                    flux_e, flux_s = new_fluxes_ring(
                        flux_e, flux_s, level, free[7, lo:hi], free[8, lo:hi]
                    )
            free[5, lo:hi] = level
            free[6, lo:hi] = flux_s
        for band in range(K):
            first = band * FINE_ROWS + TOP
            for part, chosen in enumerate((ROWS_EARLY, ROWS_LATE)):
                for i, (f, shift) in enumerate(chosen):
                    at = first + shift
                    bulk_out[3 * band + part, i : i + 1] = free[f, at : at + 1]
            bulk_out[3 * band + 2] = pack_sides(free, band)

        peers = jnp.int32(tiles)
        for present, _device in links:
            peers = peers + jnp.where(present, 1, 0)
        pl.semaphore_wait(barrier, peers)
        send_all(first_out, first_in.at[tile], first_sems.at[0], first_sems.at[1])
        send_all(bulk_out, bulk_in.at[tile], bulk_sems.at[0], bulk_sems.at[1])

        def halo(kind, src, dst, device):
            return pltpu.make_async_remote_copy(
                src_ref=src,
                dst_ref=dst,
                send_sem=halo_send.at[kind],
                recv_sem=halo_recv.at[kind],
                device_id=device,
                device_id_type=MESH,
            )

        fields = [state_ref.at[0, f] for f in range(3)] + [free.at[7 + i] for i in range(2)]
        lane = iota((height, width), 1)
        packed = jnp.zeros((height, width), jnp.float32)
        for i, field in enumerate(fields):
            x = field[...]
            ext[i, 0:height, 0:width] = x
            packed = jnp.where((lane >= 8 * i) & (lane < 8 * i + 4), pltpu.roll(x, 8 * i, 1), packed)
            packed = jnp.where(
                (lane >= 8 * i + 4) & (lane < 8 * i + 8), pltpu.roll(x, 8 * i + 8, 1), packed
            )
        side_out[...] = packed
        to_east = halo(0, side_out, west_in, east)
        to_west = halo(1, side_out, east_in, west)
        top, bottom = pl.ds(0, HALO), pl.ds(height - HALO, HALO)
        below, above = pl.ds(height, HALO), pl.ds(height + HALO, HALO)
        to_south = halo(2, ext.at[:, bottom], ext.at[:, above], south)
        to_north = halo(3, ext.at[:, top], ext.at[:, below], north)

        for present, copy in ((has_east, to_east), (has_west, to_west)):

            @pl.when(present)
            def _():
                copy.start()

        for present, buffer in ((has_west, west_in), (has_east, east_in)):

            @pl.when(jnp.logical_not(present))
            def _():
                buffer[...] = jnp.zeros(buffer.shape, jnp.float32)

        for present, where in ((has_south, below), (has_north, above)):

            @pl.when(jnp.logical_not(present))
            def _():
                ext[:, where] = jnp.zeros((len(fields), HALO, 2 * width), jnp.float32)

        rows, lanes = iota((height + 2 * HALO, 2 * width), 0), iota((height + 2 * HALO, 2 * width), 1)

        def allowed(region, present):
            return jnp.logical_not(region) | (jnp.full(rows.shape, present.astype(jnp.int32)) > 0)

        inside = allowed((rows >= height) & (rows < height + HALO), has_south)
        inside = inside & allowed(rows >= height + HALO, has_north)
        inside = inside & allowed((lanes >= width) & (lanes < width + width // 2), has_east)
        inside = inside & allowed(lanes >= width + width // 2, has_west)
        courant_ref[...] = jnp.where(inside, COURANT, 0.0)

        for present, copy in ((has_west, to_east), (has_east, to_west)):

            @pl.when(present)
            def _():
                copy.wait_recv()

        from_west, from_east = west_in[...], east_in[...]
        for i in range(len(fields)):
            ext[i, 0:height, width:] = jnp.where(
                lane < 4,
                pltpu.roll(from_east, (width - 8 * i) % width, 1),
                jnp.where(lane >= width - 4, pltpu.roll(from_west, width - 8 - 8 * i, 1), 0.0),
            )

        for present, copy in ((has_south, to_south), (has_north, to_north)):

            @pl.when(present)
            def _():
                copy.start()

        for present, copy in ((has_north, to_south), (has_south, to_north)):

            @pl.when(present)
            def _():
                copy.wait_recv()

        for present, copy in (
            (has_east, to_east),
            (has_west, to_west),
            (has_south, to_south),
            (has_north, to_north),
        ):

            @pl.when(present)
            def _():
                copy.wait_send()

        @pl.loop(0, STEPS)
        def _(s):
            surface, eastward, southward = ext[0], ext[1], ext[2]
            level = new_level_ring(surface, eastward, southward, courant_ref[...])
            flux_e, flux_s = new_fluxes_ring(eastward, southward, level, ext[3], ext[4])
            ext[0] = level
            ext[1] = flux_e
            ext[2] = flux_s

            wait_all(ret_in.at[s], ret_recv.at[s])
            ret_now[...] = ret_in[s]
            lane = iota((PH, width), 1)
            for band in range(K):
                first = band * FINE_ROWS + TOP
                merged = [ext[f, first : first + PH, 0:width] for f in range(3)]
                for j in range(RR - 1):
                    p = band * (RR - 1) + j
                    column = LEFT + j * PW
                    block = ret_now[slots[p]]
                    mask = (
                        (lane >= column)
                        & (lane < column + PW)
                        & (jnp.full((PH, width), covers[p], jnp.int32) > 0)
                    )
                    for f in range(3):
                        shifted = pltpu.roll(block, (column - f * PW) % width, 1)
                        merged[f] = jnp.where(mask, shifted, merged[f])
                for f in range(3):
                    ext[f, first : first + PH, 0:width] = merged[f]

        for f in range(3):
            out_ref[0, f] = ext[f, 0:height, 0:width]

        wait_all(first_in, first_sems.at[0])
        wait_all(bulk_in, bulk_sems.at[0])

    @pl.when(jnp.logical_not(is_outer))
    def _():
        @pl.loop(0, tiles - 1)
        def _(i):
            t = lax.rem(tile + i + 1, tiles)
            pl.semaphore_signal(
                barrier, inc=1, device_id=(sec, t // n_nest, lax.rem(t, n_nest)), device_id_type=MESH
            )

        spots, lives = [], []
        for k in range(K):
            spot, live = jnp.int32(0), jnp.int32(0)
            for n in range(nests):
                hit = host_ref[n] == tile * K + k
                spot = jnp.where(hit, place_ref[n], spot)
                live = jnp.where(hit, 1, live)
            spots.append(spot)
            lives.append(live)
        homes = [spot // NPOS for spot in spots]
        bands = [lax.rem(spot, NPOS) // (RR - 1) for spot in spots]
        columns = [lax.rem(spot, RR - 1) for spot in spots]
        near = []
        for k in range(K):
            pair = []
            for side in (-1, 1):
                inside = (columns[k] + side >= 0) & (columns[k] + side < RR - 1)
                slot, cover = jnp.int32(0), jnp.int32(0)
                for n in range(nests):
                    hit = inside & (place_ref[n] == spots[k] + side)
                    slot = jnp.where(hit, host_ref[n], slot)
                    cover = jnp.where(hit, 1, cover)
                pair.append((slot // K, lax.rem(slot, K), cover))
            near.append(pair)

        gather_from = iota((3 * width, 2 * width), 0)
        gather_to = iota((3 * width, 2 * width), 1)
        field, lane_in = gather_from // width, lax.rem(gather_from, width)
        weight = jnp.where(
            field == 0,
            1.0 / (RR * RR),
            jnp.where((field == 2) | (lax.rem(lane_in, RR) == RR - 1), 1.0 / RR, 0.0),
        )
        gather = jnp.where(gather_to == field * PW + lane_in // RR, weight, 0.0)
        for i, (f, c) in enumerate(EDGES):
            gather = gather + jnp.where(
                (gather_to >= width)
                & (lax.rem(gather_to, 16) == i)
                & (field == f)
                & (lane_in // RR == c),
                weight,
                0.0,
            )
        widen = (
            iota((width, width), 0) == NEAR + iota((width, width), 1) // RR
        ).astype(jnp.float32)
        gather, widen = [m.astype(jnp.bfloat16) for m in (gather, widen)]
        lane, sub = iota((PH, width), 1), iota((PH, width), 0)
        own_lanes = (lane >= NEAR) & (lane < NEAR + PW)

        def by_column(k, choices):
            out = choices[0]
            for j in range(1, len(choices)):
                out = jnp.where(jnp.full(out.shape, columns[k], jnp.int32) == j, choices[j], out)
            return out

        def centred(x, k):
            return by_column(
                k, [pltpu.roll(x, (NEAR - LEFT - j * PW) % width, 1) for j in range(RR - 1)]
            )

        def pick_lane(block, index):
            return jnp.sum(jnp.where(lane == index, block, 0.0), axis=1, keepdims=True)

        def pick_row(block, index):
            return jnp.sum(jnp.where(sub == index, block, 0.0), axis=0, keepdims=True)

        for load in loads:
            load.wait()
        st[...] = state_ref[0]
        pl.semaphore_wait(barrier, 2 * tiles - 1)
        wait_all(first_in, first_sems.at[1])
        lines = jnp.zeros((PH, width), jnp.float32)
        for k in range(K):
            block = first_in[homes[k]]
            level_block = centred(block, k)
            for t in range(2):
                at = t * (LEFT + (RR - 1) * PW) + bands[k] * (2 * (RR - 1)) + columns[k]
                cols = jnp.where(lane < width // 2, pick_lane(block, at), pick_lane(block, at + RR - 1))
                ghost_cols[t, k] = grow_rows(cols)
                for i in range(2):
                    line = pick_row(level_block, 2 * (t * K + bands[k]) + i)
                    lines = jnp.where(sub == (t * K + k) * 2 + i, line, lines)
        lines = dot_by(lines, widen)
        for t in range(2):
            for k in range(K):
                at = (t * K + k) * 2
                ghost_rows[t, k, 0:2] = lines[at : at + 2]

        @pl.loop(0, STEPS)
        def _(s):
            lane, sub = iota((PH, width), 1), iota((PH, width), 0)
            slots = [pl.ds(k * FINE_ROWS, FINE_ROWS) for k in range(K)]
            old_cols, new_cols = [[ghost_cols[t, k] for k in range(K)] for t in range(2)]
            old_rows, new_rows = [[ghost_rows[t, k] for k in range(K)] for t in range(2)]
            fields = [[st[f, slot] for f in range(3)] for slot in slots]
            depths = [[depth_ref[0, i, slot] for i in range(2)] for slot in slots]
            opens = [[open_ref[0, i, slot].astype(jnp.float32) for i in range(2)] for slot in slots]
            for m in range(1, RR + 1):
                for k in range(K):
                    cols = old_cols[k] + (m / RR) * (new_cols[k] - old_cols[k])
                    rows = old_rows[k] + (m / RR) * (new_rows[k] - old_rows[k])
                    surface, eastward, southward = fields[k]
                    surface = new_level(surface, eastward, southward, cols, rows[0:1])
                    eastward, southward = new_fluxes(
                        eastward, southward, surface, cols, rows[1:2], depths[k], opens[k]
                    )
                    fields[k] = [surface, eastward, southward]
            sums = dot_by(
                jnp.concatenate(
                    [
                        jnp.concatenate([row_sums(s_), row_sums(e_), row_picks(q_)], axis=1)
                        for s_, e_, q_ in fields
                    ],
                    axis=0,
                ),
                gather,
            )
            coarse = [sums[k * PH : (k + 1) * PH, 0:width] for k in range(K)]

            @pl.when(s < STEPS - 1)
            def _():
                for k in range(K):
                    edges = sums[k * PH : (k + 1) * PH, width:]
                    edge_out[s, k : k + 1] = jnp.sum(
                        jnp.where(lane // 16 == sub, edges, 0.0), axis=0, keepdims=True
                    )
                send_to(
                    1,
                    tiles - 1,
                    edge_out.at[s, pl.ds(0, K)],
                    edge_in.at[s, tile, pl.ds(0, K)],
                    edge_send.at[s],
                    edge_recv.at[s],
                )

            for k in range(K):
                ret_out[s, k] = coarse[k]
            send_all(ret_out.at[s], ret_in.at[s, pl.ds(tile * K, K)], ret_send.at[s], ret_recv.at[s])
            for k in range(K):
                for f in range(3):
                    st[f, slots[k]] = fields[k][f]

            @pl.when(s == 0)
            def _():
                wait_all(bulk_in, bulk_sems.at[1])
                for k in range(K):
                    early, late = [centred(bulk_in[homes[k], 3 * bands[k] + i], k) for i in range(2)]
                    flat = bulk_in[homes[k], 3 * bands[k] + 2]
                    sides = by_column(
                        k,
                        [pltpu.roll(flat, (-8 * len(SIDE_FIELDS) * j) % width, 1) for j in range(RR - 1)],
                    )

                    def tile_of(block, spots):
                        out = jnp.zeros((PH, width), jnp.float32)
                        for target, source in spots:
                            out = jnp.where(sub == target, block[source : source + 1], out)
                        return out

                    outside = [
                        tile_of(early, ((0, 0), (1, 1), (7, 5))),
                        tile_of(early, ((0, 2), (7, 6))),
                        tile_of(early, ((0, 3), (6, 4), (7, 7))),
                        tile_of(late, ((0, 3), (7, 4))),
                        tile_of(late, ((0, 5), (6, 6), (7, 7))),
                    ]
                    for i in range(5):
                        beside = jnp.where(
                            lane < NEAR + PW // 2,
                            pltpu.roll(sides, (NEAR - 4 - 8 * i) % width, 1),
                            pltpu.roll(sides, (NEAR + PW - 4 - 8 * i) % width, 1),
                        )
                        target = patch.at[k, i] if i < 3 else wet.at[k, i - 3]
                        target[0:PH] = beside
                        target[PH : 2 * PH] = outside[i]
                    later[k, 0] = tile_of(late, ((1, 0), (6, 1)))
                    later[k, 1] = tile_of(late, ((5, 2), (6, 2)))

            @pl.when(s == 1)
            def _():
                given = (sub == 1) | (sub == 5) | (sub == 6)
                for k in range(K):
                    for f, value in enumerate((later[k, 0], 0.0, later[k, 1])):
                        patch[k, f, PH : 2 * PH] = jnp.where(given, value, patch[k, f, PH : 2 * PH])

            @pl.when(s < STEPS - 1)
            def _():
                for k in range(K):
                    ghost_cols[0, k] = new_cols[k]
                    ghost_rows[0, k] = new_rows[k]
                    for f in range(3):
                        patch[k, f, 0:PH] = jnp.where(
                            own_lanes, pltpu.roll(coarse[k], (NEAR - f * PW) % width, 1), patch[k, f, 0:PH]
                        )
                wait_all(edge_in.at[s, pl.ds(0, tiles - 1), pl.ds(0, K)], edge_recv.at[s])
                edge_now[:, 0:K] = edge_in[s, :, 0:K]
                edge_now[tile, 0:K] = edge_out[s, 0:K]
                lines = jnp.zeros((PH, width), jnp.float32)
                for k in range(K):
                    (left_at, left_slot, left_on), (right_at, right_slot, right_on) = near[k]
                    left = edge_now[left_at, pl.ds(left_slot, 1)]
                    right = edge_now[right_at, pl.ds(right_slot, 1)]
                    both = jnp.where(lax.rem(lane, 16) < LEFT_EDGES, left, right)
                    items = both
                    for r in range(1, PH):
                        items = jnp.where(sub == r, pltpu.roll(both, width - 16 * r, 1), items)
                    on_left = jnp.full((PH, width), left_on, jnp.int32) > 0
                    on_right = jnp.full((PH, width), right_on, jnp.int32) > 0
                    state = []
                    for f, (a, left_first, b, right_last) in enumerate(
                        ((31, NEAR - 1, 59, NEAR + PW), (29, NEAR - 2, 58, NEAR + PW), (27, NEAR - 2, 57, NEAR + PW + 1))
                    ):
                        x = patch[k, f, 0:PH]
                        x = jnp.where(
                            on_left & (lane >= left_first) & (lane < NEAR), pltpu.roll(items, a, 1), x
                        )
                        x = jnp.where(
                            on_right & (lane >= NEAR + PW) & (lane <= right_last),
                            pltpu.roll(items, b, 1),
                            x,
                        )
                        state.append(jnp.concatenate([x, patch[k, f, PH : 2 * PH]], axis=0))
                    level = new_level_ring(state[0], state[1], state[2], COURANT)
                    flux_e, flux_s = new_fluxes_ring(state[1], state[2], level, wet[k, 0], wet[k, 1])
                    for f, x in enumerate((level, flux_e, flux_s)):
                        patch[k, f] = x
                    cols = jnp.where(
                        lane < width // 2,
                        pltpu.roll(flux_e[0:PH], width - NEAR + 1, 1),
                        pltpu.roll(level[0:PH], width - 1 - NEAR - PW, 1),
                    )
                    ghost_cols[1, k] = grow_rows(cols)
                    lines = jnp.where(sub == 2 * k, flux_s[2 * PH - 1 : 2 * PH], lines)
                    lines = jnp.where(sub == 2 * k + 1, level[PH : PH + 1], lines)
                lines = dot_by(lines, widen)
                for k in range(K):
                    ghost_rows[1, k, 0:2] = lines[2 * k : 2 * k + 2]

        for k in range(K):
            slot = pl.ds(k * FINE_ROWS, FINE_ROWS)
            live = jnp.full((FINE_ROWS, width), lives[k], jnp.int32) > 0
            for f in range(3):
                out_ref[0, f, slot] = jnp.where(live, st[f, slot], state_ref[0, f, slot])

        for s in range(STEPS):
            wait_all(ret_in.at[s], ret_send.at[s])
        for s in range(STEPS - 1):
            wait_all(edge_in.at[s, pl.ds(0, tiles - 1), pl.ds(0, K)], edge_send.at[s])


def on_device(n_row, n_nest, ocean_state, face_depth, face_open, nest_place, nest_host):
    tiles = n_row * n_nest
    height, width = ocean_state.shape[2:]
    f32 = jnp.float32
    vmem = pl.BlockSpec(memory_space=pltpu.VMEM)
    hbm = pl.BlockSpec(memory_space=pl.ANY)
    smem = pl.BlockSpec(memory_space=pltpu.SMEM)
    dma = pltpu.SemaphoreType.DMA
    return pl.pallas_call(
        functools.partial(kernel, n_row, n_nest),
        out_shape=pltpu.VMEM(ocean_state.shape, f32),
        in_specs=[smem, smem, hbm, hbm, hbm],
        out_specs=vmem,
        scratch_shapes=[
            pltpu.VMEM(ocean_state.shape, f32),
            pltpu.VMEM(face_depth.shape, f32),
            pltpu.VMEM(face_open.shape, jnp.int32),
            dma((3,)),
            pltpu.VMEM((3, height, width), f32),
            pltpu.VMEM((9, height, width), f32),
            pltpu.VMEM((PH, width), f32),
            pltpu.VMEM((tiles, PH, width), f32),
            pltpu.VMEM((3 * K, PH, width), f32),
            pltpu.VMEM((tiles, 3 * K, PH, width), f32),
            pltpu.VMEM((STEPS - 1, PH, width), f32),
            pltpu.VMEM((STEPS - 1, tiles, PH, width), f32),
            pltpu.VMEM((STEPS, K, PH, width), f32),
            pltpu.VMEM((STEPS, tiles * K, PH, width), f32),
            pltpu.VMEM((height, width), f32),
            pltpu.VMEM((height, width), f32),
            pltpu.VMEM((height, width), f32),
            pltpu.VMEM((5, height + 2 * HALO, 2 * width), f32),
            pltpu.VMEM((height + 2 * HALO, 2 * width), f32),
            pltpu.VMEM((2, K, FINE_ROWS, width), f32),
            pltpu.VMEM((2, K, PH, width), f32),
            pltpu.VMEM((K, 3, 2 * PH, width), f32),
            pltpu.VMEM((K, 2, 2 * PH, width), f32),
            pltpu.VMEM((K, 2, PH, width), f32),
            pltpu.VMEM((tiles, PH, width), f32),
            pltpu.VMEM((tiles * K, PH, width), f32),
            dma((2,)),
            dma((2,)),
            dma((STEPS - 1,)),
            dma((STEPS - 1,)),
            dma((STEPS,)),
            dma((STEPS,)),
            dma((4,)),
            dma((4,)),
        ],
        compiler_params=pltpu.CompilerParams(collective_id=0, has_side_effects=True),
    )(nest_place, nest_host, ocean_state, face_depth, face_open)


def solution(mesh):
    field = P("sec", None, "row", "nest")
    return jax.shard_map(
        functools.partial(on_device, mesh.shape["row"], mesh.shape["nest"]),
        mesh=mesh,
        in_specs=(field, field, field, P(), P()),
        out_specs=field,
        check_vma=False,
    )
```

```python
import functools

import jax
import jax.numpy as jnp
from jax import lax
from jax.experimental import pallas as pl
from jax.experimental.pallas import tpu as pltpu
from jax.sharding import PartitionSpec as P

PH = 8
PW = 32
RR = 4
K = 2
STEPS = 4
NPOS = K * (RR - 1)
COURANT = 0.3
MESH = pl.DeviceIdType.MESH
FINE_ROWS = RR * PH
TOP = (RR - 1) * PH // 2
LEFT = PW // 2
NEAR = PW
EDGES = (
    (0, PW - 1),
    (1, PW - 2),
    (1, PW - 1),
    (2, PW - 2),
    (2, PW - 1),
    (0, 0),
    (1, 0),
    (2, 0),
    (2, 1),
)
LEFT_EDGES = 5
BAND = (TOP + PH + STEPS + 7) // 8 * 8
HALO = 8
ROWS_EARLY = ((0, PH), (3, PH + 1), (1, PH), (2, PH), (2, -2), (0, -1), (1, -1), (2, -1))
ROWS_LATE = ((4, PH + 1), (5, -2), (6, -2), (7, PH), (7, -1), (8, PH), (8, -2), (8, -1))
SIDE_FIELDS = (0, 1, 2, 7, 8)


def iota(shape, dim):
    return lax.broadcasted_iota(jnp.int32, shape, dim)


def new_level(surface, eastward, southward, west_ghost, north_ghost):
    rows, cols = iota(surface.shape, 0), iota(surface.shape, 1)
    east_behind = jnp.where(cols == 0, west_ghost, pltpu.roll(eastward, 1, 1))
    south_behind = jnp.where(rows == 0, north_ghost, pltpu.roll(southward, 1, 0))
    return surface - COURANT * ((eastward - east_behind) + (southward - south_behind))


def new_fluxes(eastward, southward, level, east_ghost, south_ghost, depth, opened):
    height, width = level.shape
    rows, cols = iota(level.shape, 0), iota(level.shape, 1)
    level_east = jnp.where(cols == width - 1, east_ghost, pltpu.roll(level, width - 1, 1))
    level_south = jnp.where(rows == height - 1, south_ghost, pltpu.roll(level, height - 1, 0))
    east = opened[0] * (
        eastward - COURANT * (depth[0] + 0.5 * (level + level_east)) * (level_east - level)
    )
    south = opened[1] * (
        southward - COURANT * (depth[1] + 0.5 * (level + level_south)) * (level_south - level)
    )
    return east, south


def new_level_ring(surface, eastward, southward, courant):
    east_gap = eastward - pltpu.roll(eastward, 1, 1)
    south_gap = southward - pltpu.roll(southward, 1, 0)
    return surface - courant * (east_gap + south_gap)


def new_fluxes_ring(eastward, southward, level, wet_east, wet_south):
    height, width = level.shape
    level_east = pltpu.roll(level, width - 1, 1)
    level_south = pltpu.roll(level, height - 1, 0)
    east = eastward - COURANT * (wet_east + 0.5 * (level + level_east)) * (level_east - level)
    south = southward - COURANT * (wet_south + 0.5 * (level + level_south)) * (level_south - level)
    return jnp.where(wet_east > 0, east, 0.0), jnp.where(wet_south > 0, south, 0.0)


def parts(x):
    high = x.astype(jnp.bfloat16).astype(jnp.float32)
    rest = x - high
    middle = rest.astype(jnp.bfloat16).astype(jnp.float32)
    return high, middle, rest - middle


def dot_by(x, chosen):
    rows = x.shape[0]
    stacked = jnp.concatenate(parts(x), axis=0).astype(jnp.bfloat16)
    y = jnp.dot(stacked, chosen, preferred_element_type=jnp.float32)
    return y[:rows] + (y[rows : 2 * rows] + y[2 * rows :])


def pack_strips(times):
    width = times[0][0].shape[-1]
    lane, sub = iota((PH, width), 1), iota((PH, width), 0)
    block = jnp.zeros((PH, width), jnp.float32)
    span = (RR - 1) * PW
    inner = (lane >= LEFT) & (lane < LEFT + span)
    for t, fields in enumerate(times):
        surface, eastward, southward = fields
        for band in range(K):
            first = band * FINE_ROWS + TOP
            east8 = eastward[first : first + PH, :]
            level8 = surface[first : first + PH, :]
            for j in range(RR - 1):
                column = LEFT + j * PW
                west_lane = t * (LEFT + span) + band * 2 * (RR - 1) + j
                east_lane = west_lane + RR - 1
                block = jnp.where(
                    lane == west_lane, pltpu.roll(east8, (west_lane - column + 1) % width, 1), block
                )
                block = jnp.where(
                    lane == east_lane, pltpu.roll(level8, (east_lane - column - PW) % width, 1), block
                )
            row = (t * K + band) * 2
            block = jnp.where(inner & (sub == row), southward[first - 1 : first, :], block)
            block = jnp.where(inner & (sub == row + 1), surface[first + PH : first + PH + 1, :], block)
    return block


def pack_sides(free, band):
    width = free.shape[-1]
    lane = iota((PH, width), 1)
    block = jnp.zeros((PH, width), jnp.float32)
    first = band * FINE_ROWS + TOP
    for i, f in enumerate(SIDE_FIELDS):
        values = free[f, first : first + PH, :]
        for j in range(RR - 1):
            column = LEFT + j * PW
            target = j * 8 * len(SIDE_FIELDS) + 8 * i
            for side, source in ((0, column - 4), (4, column + PW)):
                at = target + side
                block = jnp.where(
                    (lane >= at) & (lane < at + 4), pltpu.roll(values, (at - source) % width, 1), block
                )
    return block


def row_sums(x):
    width = x.shape[1]
    sub = iota((8, width), 0)
    out = jnp.zeros((8, width), jnp.float32)
    for v in range(x.shape[0] // 8):
        piece = x[8 * v : 8 * v + 8]
        piece = piece + pltpu.roll(piece, 1, 0)
        piece = piece + pltpu.roll(piece, 2, 0)
        out = jnp.where(sub == 2 * v, piece[3:4], out)
        out = jnp.where(sub == 2 * v + 1, piece[7:8], out)
    return out


def row_picks(x):
    width = x.shape[1]
    sub = iota((8, width), 0)
    out = jnp.zeros((8, width), jnp.float32)
    for v in range(x.shape[0] // 8):
        out = jnp.where(sub == 2 * v, x[8 * v + 3 : 8 * v + 4], out)
        out = jnp.where(sub == 2 * v + 1, x[8 * v + 7 : 8 * v + 8], out)
    return out


def grow_rows(x):
    sub = iota(x.shape, 0)
    return jnp.concatenate(
        [jnp.where(sub < 4, x[2 * v : 2 * v + 1], x[2 * v + 1 : 2 * v + 2]) for v in range(RR)], axis=0
    )


def kernel(
    n_row,
    n_nest,
    place_ref,
    host_ref,
    state_hbm,
    depth_hbm,
    open_hbm,
    out_ref,
    state_ref,
    depth_ref,
    open_ref,
    load_sems,
    st,
    free,
    first_out,
    first_in,
    bulk_out,
    bulk_in,
    edge_out,
    edge_in,
    ret_out,
    ret_in,
    side_out,
    west_in,
    east_in,
    ext,
    courant_ref,
    ghost_cols,
    ghost_rows,
    patch,
    wet,
    later,
    edge_now,
    ret_now,
    first_sems,
    bulk_sems,
    edge_send,
    edge_recv,
    ret_send,
    ret_recv,
    halo_send,
    halo_recv,
):
    tiles = n_row * n_nest
    nests = place_ref.shape[0]
    sec, row, col = lax.axis_index("sec"), lax.axis_index("row"), lax.axis_index("nest")
    tile = row * n_nest + col
    is_outer = sec == 0
    has_west, has_east = col > 0, col < n_nest - 1
    has_north, has_south = row > 0, row < n_row - 1
    west, east = (sec, row, col - 1), (sec, row, col + 1)
    north, south = (sec, row - 1, col), (sec, row + 1, col)
    links = ((has_west, west), (has_east, east), (has_north, north), (has_south, south))
    height, width = state_ref.shape[2], state_ref.shape[3]

    barrier = pltpu.get_barrier_semaphore()

    @pl.when(jnp.logical_not(is_outer))
    def _():
        pl.semaphore_signal(barrier, inc=1, device_id=(0, row, col), device_id_type=MESH)

        @pl.loop(0, tiles - 1)
        def _(i):
            t = lax.rem(tile + i + 1, tiles)
            pl.semaphore_signal(
                barrier, inc=1, device_id=(sec, t // n_nest, lax.rem(t, n_nest)), device_id_type=MESH
            )

    loads = [
        pltpu.make_async_copy(source, target, load_sems.at[i])
        for i, (source, target) in enumerate(
            ((state_hbm, state_ref), (depth_hbm, depth_ref), (open_hbm, open_ref))
        )
    ]
    for load in loads:
        load.start()

    def send_to(section, count, src, dst, send_sem, recv_sem):
        @pl.loop(0, tiles)
        def _(i):
            t = lax.rem(2 * tiles - 1 - tile - i, tiles)

            def go():
                pltpu.make_async_remote_copy(
                    src_ref=src,
                    dst_ref=dst,
                    send_sem=send_sem,
                    recv_sem=recv_sem,
                    device_id=(section, t // n_nest, lax.rem(t, n_nest)),
                    device_id_type=MESH,
                ).start()

            if count == tiles:
                go()
            else:
                pl.when(t != tile)(go)

    def send_all(src, dst, send_sem, recv_sem):
        send_to(1 - sec, tiles, src, dst, send_sem, recv_sem)

    def wait_all(whole, sem):
        pltpu.make_async_copy(whole, whole, sem).wait()

    def relays():
        return [
            pltpu.make_async_remote_copy(
                src_ref=src,
                dst_ref=dst.at[tile],
                send_sem=sems.at[0],
                recv_sem=sems.at[1],
                device_id=(1, row, col),
                device_id_type=MESH,
            )
            for src, dst, sems in ((first_out, first_in, first_sems), (bulk_out, bulk_in, bulk_sems))
        ]

    @pl.when(is_outer)
    def _():
        for present, device in links:

            @pl.when(present)
            def _():
                pl.semaphore_signal(barrier, inc=1, device_id=device, device_id_type=MESH)

        slots, covers = [], []
        for p in range(NPOS):
            slot, cover = jnp.int32(0), jnp.int32(0)
            for n in range(nests):
                hit = place_ref[n] == tile * NPOS + p
                slot = jnp.where(hit, host_ref[n], slot)
                cover = jnp.where(hit, 1, cover)
            slots.append(slot)
            covers.append(cover)
        for load in loads:
            load.wait()
        for i in range(2):
            free[7 + i] = jnp.where(open_ref[0, i] > 0, depth_ref[0, i], 0.0)
        levels = []
        for band in range(K):
            lo = band * FINE_ROWS
            hi = lo + BAND
            old = [state_ref[0, f, lo:hi] for f in range(3)]
            level = new_level_ring(old[0], old[1], old[2], COURANT)
            flux_e, flux_s = new_fluxes_ring(old[1], old[2], level, free[7, lo:hi], free[8, lo:hi])
            free[0, lo:hi] = level
            free[1, lo:hi] = flux_e
            free[2, lo:hi] = flux_s
        first_out[...] = pack_strips(
            [[ref.at[f] for f in range(3)] for ref in (state_ref.at[0], free)]
        )
        for band in range(K):
            lo = band * FINE_ROWS
            hi = lo + BAND
            level, flux_e, flux_s = [free[f, lo:hi] for f in range(3)]
            for i in range(2):
                east_gap = flux_e - pltpu.roll(flux_e, 1, 1)
                free[3 + i, lo:hi] = level - COURANT * (east_gap + flux_s)
                level = level - COURANT * (east_gap + (flux_s - pltpu.roll(flux_s, 1, 0)))
                if i == 0:
                    flux_e, flux_s = new_fluxes_ring(
                        flux_e, flux_s, level, free[7, lo:hi], free[8, lo:hi]
                    )
            free[5, lo:hi] = level
            free[6, lo:hi] = flux_s
        for band in range(K):
            first = band * FINE_ROWS + TOP
            for part, chosen in enumerate((ROWS_EARLY, ROWS_LATE)):
                for i, (f, shift) in enumerate(chosen):
                    at = first + shift
                    bulk_out[3 * band + part, i : i + 1] = free[f, at : at + 1]
            bulk_out[3 * band + 2] = pack_sides(free, band)

        peers = jnp.int32(1)
        for present, _device in links:
            peers = peers + jnp.where(present, 1, 0)
        pl.semaphore_wait(barrier, peers)
        for copy in relays():
            copy.start()

        def halo(kind, src, dst, device):
            return pltpu.make_async_remote_copy(
                src_ref=src,
                dst_ref=dst,
                send_sem=halo_send.at[kind],
                recv_sem=halo_recv.at[kind],
                device_id=device,
                device_id_type=MESH,
            )

        fields = [state_ref.at[0, f] for f in range(3)] + [free.at[7 + i] for i in range(2)]
        lane = iota((height, width), 1)
        packed = jnp.zeros((height, width), jnp.float32)
        for i, field in enumerate(fields):
            x = field[...]
            ext[i, 0:height, 0:width] = x
            packed = jnp.where((lane >= 8 * i) & (lane < 8 * i + 4), pltpu.roll(x, 8 * i, 1), packed)
            packed = jnp.where(
                (lane >= 8 * i + 4) & (lane < 8 * i + 8), pltpu.roll(x, 8 * i + 8, 1), packed
            )
        side_out[...] = packed
        to_east = halo(0, side_out, west_in, east)
        to_west = halo(1, side_out, east_in, west)
        top, bottom = pl.ds(0, HALO), pl.ds(height - HALO, HALO)
        below, above = pl.ds(height, HALO), pl.ds(height + HALO, HALO)
        to_south = halo(2, ext.at[:, bottom], ext.at[:, above], south)
        to_north = halo(3, ext.at[:, top], ext.at[:, below], north)

        for present, copy in ((has_east, to_east), (has_west, to_west)):

            @pl.when(present)
            def _():
                copy.start()

        for present, buffer in ((has_west, west_in), (has_east, east_in)):

            @pl.when(jnp.logical_not(present))
            def _():
                buffer[...] = jnp.zeros(buffer.shape, jnp.float32)

        for present, where in ((has_south, below), (has_north, above)):

            @pl.when(jnp.logical_not(present))
            def _():
                ext[:, where] = jnp.zeros((len(fields), HALO, 2 * width), jnp.float32)

        rows, lanes = iota((height + 2 * HALO, 2 * width), 0), iota((height + 2 * HALO, 2 * width), 1)

        def allowed(region, present):
            return jnp.logical_not(region) | (jnp.full(rows.shape, present.astype(jnp.int32)) > 0)

        inside = allowed((rows >= height) & (rows < height + HALO), has_south)
        inside = inside & allowed(rows >= height + HALO, has_north)
        inside = inside & allowed((lanes >= width) & (lanes < width + width // 2), has_east)
        inside = inside & allowed(lanes >= width + width // 2, has_west)
        courant_ref[...] = jnp.where(inside, COURANT, 0.0)

        for present, copy in ((has_west, to_east), (has_east, to_west)):

            @pl.when(present)
            def _():
                copy.wait_recv()

        from_west, from_east = west_in[...], east_in[...]
        for i in range(len(fields)):
            ext[i, 0:height, width:] = jnp.where(
                lane < 4,
                pltpu.roll(from_east, (width - 8 * i) % width, 1),
                jnp.where(lane >= width - 4, pltpu.roll(from_west, width - 8 - 8 * i, 1), 0.0),
            )

        for present, copy in ((has_south, to_south), (has_north, to_north)):

            @pl.when(present)
            def _():
                copy.start()

        for present, copy in ((has_north, to_south), (has_south, to_north)):

            @pl.when(present)
            def _():
                copy.wait_recv()

        for present, copy in (
            (has_east, to_east),
            (has_west, to_west),
            (has_south, to_south),
            (has_north, to_north),
        ):

            @pl.when(present)
            def _():
                copy.wait_send()

        @pl.loop(0, STEPS)
        def _(s):
            surface, eastward, southward = ext[0], ext[1], ext[2]
            level = new_level_ring(surface, eastward, southward, courant_ref[...])
            flux_e, flux_s = new_fluxes_ring(eastward, southward, level, ext[3], ext[4])
            ext[0] = level
            ext[1] = flux_e
            ext[2] = flux_s

            wait_all(ret_in.at[s], ret_recv.at[s])
            ret_now[...] = ret_in[s]
            lane = iota((PH, width), 1)
            for band in range(K):
                first = band * FINE_ROWS + TOP
                merged = [ext[f, first : first + PH, 0:width] for f in range(3)]
                for j in range(RR - 1):
                    p = band * (RR - 1) + j
                    column = LEFT + j * PW
                    block = ret_now[slots[p]]
                    mask = (
                        (lane >= column)
                        & (lane < column + PW)
                        & (jnp.full((PH, width), covers[p], jnp.int32) > 0)
                    )
                    for f in range(3):
                        shifted = pltpu.roll(block, (column - f * PW) % width, 1)
                        merged[f] = jnp.where(mask, shifted, merged[f])
                for f in range(3):
                    ext[f, first : first + PH, 0:width] = merged[f]

        for f in range(3):
            out_ref[0, f] = ext[f, 0:height, 0:width]

        for copy in relays():
            copy.wait_send()

    @pl.when(jnp.logical_not(is_outer))
    def _():
        spots, lives = [], []
        for k in range(K):
            spot, live = jnp.int32(0), jnp.int32(0)
            for n in range(nests):
                hit = host_ref[n] == tile * K + k
                spot = jnp.where(hit, place_ref[n], spot)
                live = jnp.where(hit, 1, live)
            spots.append(spot)
            lives.append(live)
        homes = [spot // NPOS for spot in spots]
        bands = [lax.rem(spot, NPOS) // (RR - 1) for spot in spots]
        columns = [lax.rem(spot, RR - 1) for spot in spots]
        near = []
        for k in range(K):
            pair = []
            for side in (-1, 1):
                inside = (columns[k] + side >= 0) & (columns[k] + side < RR - 1)
                slot, cover = jnp.int32(0), jnp.int32(0)
                for n in range(nests):
                    hit = inside & (place_ref[n] == spots[k] + side)
                    slot = jnp.where(hit, host_ref[n], slot)
                    cover = jnp.where(hit, 1, cover)
                pair.append((slot // K, lax.rem(slot, K), cover))
            near.append(pair)

        gather_from = iota((3 * width, 2 * width), 0)
        gather_to = iota((3 * width, 2 * width), 1)
        field, lane_in = gather_from // width, lax.rem(gather_from, width)
        weight = jnp.where(
            field == 0,
            1.0 / (RR * RR),
            jnp.where((field == 2) | (lax.rem(lane_in, RR) == RR - 1), 1.0 / RR, 0.0),
        )
        gather = jnp.where(gather_to == field * PW + lane_in // RR, weight, 0.0)
        for i, (f, c) in enumerate(EDGES):
            gather = gather + jnp.where(
                (gather_to >= width)
                & (lax.rem(gather_to, 16) == i)
                & (field == f)
                & (lane_in // RR == c),
                weight,
                0.0,
            )
        widen = (
            iota((width, width), 0) == NEAR + iota((width, width), 1) // RR
        ).astype(jnp.float32)
        gather, widen = [m.astype(jnp.bfloat16) for m in (gather, widen)]
        lane, sub = iota((PH, width), 1), iota((PH, width), 0)
        own_lanes = (lane >= NEAR) & (lane < NEAR + PW)

        def by_column(k, choices):
            out = choices[0]
            for j in range(1, len(choices)):
                out = jnp.where(jnp.full(out.shape, columns[k], jnp.int32) == j, choices[j], out)
            return out

        def centred(x, k):
            return by_column(
                k, [pltpu.roll(x, (NEAR - LEFT - j * PW) % width, 1) for j in range(RR - 1)]
            )

        def pick_lane(block, index):
            return jnp.sum(jnp.where(lane == index, block, 0.0), axis=1, keepdims=True)

        def pick_row(block, index):
            return jnp.sum(jnp.where(sub == index, block, 0.0), axis=0, keepdims=True)

        for load in loads:
            load.wait()
        st[...] = state_ref[0]
        pl.semaphore_wait(barrier, tiles - 1)
        for copy, whole, sems in zip(relays(), (first_in, bulk_in), (first_sems, bulk_sems)):
            copy.wait_recv()
            send_to(1, tiles - 1, whole.at[tile], whole.at[tile], sems.at[2], sems.at[3])
        wait_all(first_in.at[pl.ds(0, tiles - 1)], first_sems.at[3])
        lines = jnp.zeros((PH, width), jnp.float32)
        for k in range(K):
            block = first_in[homes[k]]
            level_block = centred(block, k)
            for t in range(2):
                at = t * (LEFT + (RR - 1) * PW) + bands[k] * (2 * (RR - 1)) + columns[k]
                cols = jnp.where(lane < width // 2, pick_lane(block, at), pick_lane(block, at + RR - 1))
                ghost_cols[t, k] = grow_rows(cols)
                for i in range(2):
                    line = pick_row(level_block, 2 * (t * K + bands[k]) + i)
                    lines = jnp.where(sub == (t * K + k) * 2 + i, line, lines)
        lines = dot_by(lines, widen)
        for t in range(2):
            for k in range(K):
                at = (t * K + k) * 2
                ghost_rows[t, k, 0:2] = lines[at : at + 2]

        @pl.loop(0, STEPS)
        def _(s):
            lane, sub = iota((PH, width), 1), iota((PH, width), 0)
            slots = [pl.ds(k * FINE_ROWS, FINE_ROWS) for k in range(K)]
            old_cols, new_cols = [[ghost_cols[t, k] for k in range(K)] for t in range(2)]
            old_rows, new_rows = [[ghost_rows[t, k] for k in range(K)] for t in range(2)]
            fields = [[st[f, slot] for f in range(3)] for slot in slots]
            depths = [[depth_ref[0, i, slot] for i in range(2)] for slot in slots]
            opens = [[open_ref[0, i, slot].astype(jnp.float32) for i in range(2)] for slot in slots]
            for m in range(1, RR + 1):
                for k in range(K):
                    cols = old_cols[k] + (m / RR) * (new_cols[k] - old_cols[k])
                    rows = old_rows[k] + (m / RR) * (new_rows[k] - old_rows[k])
                    surface, eastward, southward = fields[k]
                    surface = new_level(surface, eastward, southward, cols, rows[0:1])
                    eastward, southward = new_fluxes(
                        eastward, southward, surface, cols, rows[1:2], depths[k], opens[k]
                    )
                    fields[k] = [surface, eastward, southward]
            sums = dot_by(
                jnp.concatenate(
                    [
                        jnp.concatenate([row_sums(s_), row_sums(e_), row_picks(q_)], axis=1)
                        for s_, e_, q_ in fields
                    ],
                    axis=0,
                ),
                gather,
            )
            coarse = [sums[k * PH : (k + 1) * PH, 0:width] for k in range(K)]

            @pl.when(s < STEPS - 1)
            def _():
                for k in range(K):
                    edges = sums[k * PH : (k + 1) * PH, width:]
                    edge_out[s, k : k + 1] = jnp.sum(
                        jnp.where(lane // 16 == sub, edges, 0.0), axis=0, keepdims=True
                    )
                send_to(
                    1,
                    tiles - 1,
                    edge_out.at[s, pl.ds(0, K)],
                    edge_in.at[s, tile, pl.ds(0, K)],
                    edge_send.at[s],
                    edge_recv.at[s],
                )

            for k in range(K):
                ret_out[s, k] = coarse[k]
            send_all(ret_out.at[s], ret_in.at[s, pl.ds(tile * K, K)], ret_send.at[s], ret_recv.at[s])
            for k in range(K):
                for f in range(3):
                    st[f, slots[k]] = fields[k][f]

            @pl.when(s == 0)
            def _():
                wait_all(bulk_in.at[pl.ds(0, tiles - 1)], bulk_sems.at[3])
                for k in range(K):
                    early, late = [centred(bulk_in[homes[k], 3 * bands[k] + i], k) for i in range(2)]
                    flat = bulk_in[homes[k], 3 * bands[k] + 2]
                    sides = by_column(
                        k,
                        [pltpu.roll(flat, (-8 * len(SIDE_FIELDS) * j) % width, 1) for j in range(RR - 1)],
                    )

                    def tile_of(block, spots):
                        out = jnp.zeros((PH, width), jnp.float32)
                        for target, source in spots:
                            out = jnp.where(sub == target, block[source : source + 1], out)
                        return out

                    outside = [
                        tile_of(early, ((0, 0), (1, 1), (7, 5))),
                        tile_of(early, ((0, 2), (7, 6))),
                        tile_of(early, ((0, 3), (6, 4), (7, 7))),
                        tile_of(late, ((0, 3), (7, 4))),
                        tile_of(late, ((0, 5), (6, 6), (7, 7))),
                    ]
                    for i in range(5):
                        beside = jnp.where(
                            lane < NEAR + PW // 2,
                            pltpu.roll(sides, (NEAR - 4 - 8 * i) % width, 1),
                            pltpu.roll(sides, (NEAR + PW - 4 - 8 * i) % width, 1),
                        )
                        target = patch.at[k, i] if i < 3 else wet.at[k, i - 3]
                        target[0:PH] = beside
                        target[PH : 2 * PH] = outside[i]
                    later[k, 0] = tile_of(late, ((1, 0), (6, 1)))
                    later[k, 1] = tile_of(late, ((5, 2), (6, 2)))

            @pl.when(s == 1)
            def _():
                given = (sub == 1) | (sub == 5) | (sub == 6)
                for k in range(K):
                    for f, value in enumerate((later[k, 0], 0.0, later[k, 1])):
                        patch[k, f, PH : 2 * PH] = jnp.where(given, value, patch[k, f, PH : 2 * PH])

            @pl.when(s < STEPS - 1)
            def _():
                for k in range(K):
                    ghost_cols[0, k] = new_cols[k]
                    ghost_rows[0, k] = new_rows[k]
                    for f in range(3):
                        patch[k, f, 0:PH] = jnp.where(
                            own_lanes, pltpu.roll(coarse[k], (NEAR - f * PW) % width, 1), patch[k, f, 0:PH]
                        )
                wait_all(edge_in.at[s, pl.ds(0, tiles - 1), pl.ds(0, K)], edge_recv.at[s])
                edge_now[:, 0:K] = edge_in[s, :, 0:K]
                edge_now[tile, 0:K] = edge_out[s, 0:K]
                lines = jnp.zeros((PH, width), jnp.float32)
                for k in range(K):
                    (left_at, left_slot, left_on), (right_at, right_slot, right_on) = near[k]
                    left = edge_now[left_at, pl.ds(left_slot, 1)]
                    right = edge_now[right_at, pl.ds(right_slot, 1)]
                    both = jnp.where(lax.rem(lane, 16) < LEFT_EDGES, left, right)
                    items = both
                    for r in range(1, PH):
                        items = jnp.where(sub == r, pltpu.roll(both, width - 16 * r, 1), items)
                    on_left = jnp.full((PH, width), left_on, jnp.int32) > 0
                    on_right = jnp.full((PH, width), right_on, jnp.int32) > 0
                    state = []
                    for f, (a, left_first, b, right_last) in enumerate(
                        ((31, NEAR - 1, 59, NEAR + PW), (29, NEAR - 2, 58, NEAR + PW), (27, NEAR - 2, 57, NEAR + PW + 1))
                    ):
                        x = patch[k, f, 0:PH]
                        x = jnp.where(
                            on_left & (lane >= left_first) & (lane < NEAR), pltpu.roll(items, a, 1), x
                        )
                        x = jnp.where(
                            on_right & (lane >= NEAR + PW) & (lane <= right_last),
                            pltpu.roll(items, b, 1),
                            x,
                        )
                        state.append(jnp.concatenate([x, patch[k, f, PH : 2 * PH]], axis=0))
                    level = new_level_ring(state[0], state[1], state[2], COURANT)
                    flux_e, flux_s = new_fluxes_ring(state[1], state[2], level, wet[k, 0], wet[k, 1])
                    for f, x in enumerate((level, flux_e, flux_s)):
                        patch[k, f] = x
                    cols = jnp.where(
                        lane < width // 2,
                        pltpu.roll(flux_e[0:PH], width - NEAR + 1, 1),
                        pltpu.roll(level[0:PH], width - 1 - NEAR - PW, 1),
                    )
                    ghost_cols[1, k] = grow_rows(cols)
                    lines = jnp.where(sub == 2 * k, flux_s[2 * PH - 1 : 2 * PH], lines)
                    lines = jnp.where(sub == 2 * k + 1, level[PH : PH + 1], lines)
                lines = dot_by(lines, widen)
                for k in range(K):
                    ghost_rows[1, k, 0:2] = lines[2 * k : 2 * k + 2]

        for k in range(K):
            slot = pl.ds(k * FINE_ROWS, FINE_ROWS)
            live = jnp.full((FINE_ROWS, width), lives[k], jnp.int32) > 0
            for f in range(3):
                out_ref[0, f, slot] = jnp.where(live, st[f, slot], state_ref[0, f, slot])

        wait_all(first_in.at[pl.ds(0, tiles - 1)], first_sems.at[2])
        wait_all(bulk_in.at[pl.ds(0, tiles - 1)], bulk_sems.at[2])
        for s in range(STEPS):
            wait_all(ret_in.at[s], ret_send.at[s])
        for s in range(STEPS - 1):
            wait_all(edge_in.at[s, pl.ds(0, tiles - 1), pl.ds(0, K)], edge_send.at[s])


def on_device(n_row, n_nest, ocean_state, face_depth, face_open, nest_place, nest_host):
    tiles = n_row * n_nest
    height, width = ocean_state.shape[2:]
    f32 = jnp.float32
    vmem = pl.BlockSpec(memory_space=pltpu.VMEM)
    hbm = pl.BlockSpec(memory_space=pl.ANY)
    smem = pl.BlockSpec(memory_space=pltpu.SMEM)
    dma = pltpu.SemaphoreType.DMA
    return pl.pallas_call(
        functools.partial(kernel, n_row, n_nest),
        out_shape=pltpu.VMEM(ocean_state.shape, f32),
        in_specs=[smem, smem, hbm, hbm, hbm],
        out_specs=vmem,
        scratch_shapes=[
            pltpu.VMEM(ocean_state.shape, f32),
            pltpu.VMEM(face_depth.shape, f32),
            pltpu.VMEM(face_open.shape, jnp.int32),
            dma((3,)),
            pltpu.VMEM((3, height, width), f32),
            pltpu.VMEM((9, height, width), f32),
            pltpu.VMEM((PH, width), f32),
            pltpu.VMEM((tiles, PH, width), f32),
            pltpu.VMEM((3 * K, PH, width), f32),
            pltpu.VMEM((tiles, 3 * K, PH, width), f32),
            pltpu.VMEM((STEPS - 1, PH, width), f32),
            pltpu.VMEM((STEPS - 1, tiles, PH, width), f32),
            pltpu.VMEM((STEPS, K, PH, width), f32),
            pltpu.VMEM((STEPS, tiles * K, PH, width), f32),
            pltpu.VMEM((height, width), f32),
            pltpu.VMEM((height, width), f32),
            pltpu.VMEM((height, width), f32),
            pltpu.VMEM((5, height + 2 * HALO, 2 * width), f32),
            pltpu.VMEM((height + 2 * HALO, 2 * width), f32),
            pltpu.VMEM((2, K, FINE_ROWS, width), f32),
            pltpu.VMEM((2, K, PH, width), f32),
            pltpu.VMEM((K, 3, 2 * PH, width), f32),
            pltpu.VMEM((K, 2, 2 * PH, width), f32),
            pltpu.VMEM((K, 2, PH, width), f32),
            pltpu.VMEM((tiles, PH, width), f32),
            pltpu.VMEM((tiles * K, PH, width), f32),
            dma((4,)),
            dma((4,)),
            dma((STEPS - 1,)),
            dma((STEPS - 1,)),
            dma((STEPS,)),
            dma((STEPS,)),
            dma((4,)),
            dma((4,)),
        ],
        compiler_params=pltpu.CompilerParams(collective_id=0, has_side_effects=True),
    )(nest_place, nest_host, ocean_state, face_depth, face_open)


def solution(mesh):
    field = P("sec", None, "row", "nest")
    return jax.shard_map(
        functools.partial(on_device, mesh.shape["row"], mesh.shape["nest"]),
        mesh=mesh,
        in_specs=(field, field, field, P(), P()),
        out_specs=field,
        check_vma=False,
    )
```

```python
import functools

import jax
import jax.numpy as jnp
from jax import lax
from jax.experimental import pallas as pl
from jax.experimental.pallas import tpu as pltpu
from jax.sharding import PartitionSpec as P

PH = 8
PW = 32
RR = 4
K = 2
STEPS = 4
NPOS = K * (RR - 1)
COURANT = 0.3
MESH = pl.DeviceIdType.MESH
FINE_ROWS = RR * PH
TOP = (RR - 1) * PH // 2
LEFT = PW // 2
NEAR = PW
STRIP = 16
STRIP_TILES = 3
BAND = (TOP + PH + STEPS + 7) // 8 * 8
HALO = 8
ROWS_EARLY = ((0, PH), (3, PH + 1), (1, PH), (2, PH), (2, -2), (0, -1), (1, -1), (2, -1))
ROWS_LATE = ((4, PH + 1), (5, -2), (6, -2), (7, PH), (7, -1), (8, PH), (8, -2), (8, -1))
SIDE_FIELDS = (0, 1, 2, 7, 8)


def iota(shape, dim):
    return lax.broadcasted_iota(jnp.int32, shape, dim)


def slab_step(fields, wet, cols, rows, west_at, east_at):
    surface, eastward, southward = fields
    height, width = surface.shape
    sub = iota(surface.shape, 0)
    east_behind = jnp.where(west_at, cols, pltpu.roll(eastward, 1, 1))
    south_behind = jnp.where(sub == 0, rows[0:1], pltpu.roll(southward, 1, 0))
    level = surface - COURANT * ((eastward - east_behind) + (southward - south_behind))
    level_east = jnp.where(east_at, cols, pltpu.roll(level, width - 1, 1))
    level_south = jnp.where(sub == height - 1, rows[1:2], pltpu.roll(level, height - 1, 0))
    east = eastward - COURANT * (wet[0] + 0.5 * (level + level_east)) * (level_east - level)
    south = southward - COURANT * (wet[1] + 0.5 * (level + level_south)) * (level_south - level)
    return [level, jnp.where(wet[0] > 0, east, 0.0), jnp.where(wet[1] > 0, south, 0.0)]


def new_level_ring(surface, eastward, southward, courant):
    east_gap = eastward - pltpu.roll(eastward, 1, 1)
    south_gap = southward - pltpu.roll(southward, 1, 0)
    return surface - courant * (east_gap + south_gap)


def new_fluxes_ring(eastward, southward, level, wet_east, wet_south):
    height, width = level.shape
    level_east = pltpu.roll(level, width - 1, 1)
    level_south = pltpu.roll(level, height - 1, 0)
    east = eastward - COURANT * (wet_east + 0.5 * (level + level_east)) * (level_east - level)
    south = southward - COURANT * (wet_south + 0.5 * (level + level_south)) * (level_south - level)
    return jnp.where(wet_east > 0, east, 0.0), jnp.where(wet_south > 0, south, 0.0)


def parts(x):
    high = x.astype(jnp.bfloat16).astype(jnp.float32)
    rest = x - high
    middle = rest.astype(jnp.bfloat16).astype(jnp.float32)
    return high, middle, rest - middle


def dot_by(x, chosen):
    rows = x.shape[0]
    stacked = jnp.concatenate(parts(x), axis=0).astype(jnp.bfloat16)
    y = jnp.dot(stacked, chosen, preferred_element_type=jnp.float32)
    return y[:rows] + (y[rows : 2 * rows] + y[2 * rows :])


def pack_strips(times):
    width = times[0][0].shape[-1]
    lane, sub = iota((PH, width), 1), iota((PH, width), 0)
    block = jnp.zeros((PH, width), jnp.float32)
    span = (RR - 1) * PW
    inner = (lane >= LEFT) & (lane < LEFT + span)
    for t, fields in enumerate(times):
        surface, eastward, southward = fields
        for band in range(K):
            first = band * FINE_ROWS + TOP
            east8 = eastward[first : first + PH, :]
            level8 = surface[first : first + PH, :]
            for j in range(RR - 1):
                column = LEFT + j * PW
                west_lane = t * (LEFT + span) + band * 2 * (RR - 1) + j
                east_lane = west_lane + RR - 1
                block = jnp.where(
                    lane == west_lane, pltpu.roll(east8, (west_lane - column + 1) % width, 1), block
                )
                block = jnp.where(
                    lane == east_lane, pltpu.roll(level8, (east_lane - column - PW) % width, 1), block
                )
            row = (t * K + band) * 2
            block = jnp.where(inner & (sub == row), southward[first - 1 : first, :], block)
            block = jnp.where(inner & (sub == row + 1), surface[first + PH : first + PH + 1, :], block)
    return block


def pack_sides(free, band):
    width = free.shape[-1]
    lane = iota((PH, width), 1)
    block = jnp.zeros((PH, width), jnp.float32)
    first = band * FINE_ROWS + TOP
    for i, f in enumerate(SIDE_FIELDS):
        values = free[f, first : first + PH, :]
        for j in range(RR - 1):
            column = LEFT + j * PW
            target = j * 8 * len(SIDE_FIELDS) + 8 * i
            for side, source in ((0, column - 4), (4, column + PW - 1)):
                at = target + side
                block = jnp.where(
                    (lane >= at) & (lane < at + 4), pltpu.roll(values, (at - source) % width, 1), block
                )
    return block


def row_sums(x):
    width = x.shape[1]
    sub = iota((8, width), 0)
    out = jnp.zeros((8, width), jnp.float32)
    for v in range(x.shape[0] // 8):
        piece = x[8 * v : 8 * v + 8]
        piece = piece + pltpu.roll(piece, 1, 0)
        piece = piece + pltpu.roll(piece, 2, 0)
        out = jnp.where(sub == 2 * v, piece[3:4], out)
        out = jnp.where(sub == 2 * v + 1, piece[7:8], out)
    return out


def row_picks(x):
    width = x.shape[1]
    sub = iota((8, width), 0)
    out = jnp.zeros((8, width), jnp.float32)
    for v in range(x.shape[0] // 8):
        out = jnp.where(sub == 2 * v, x[8 * v + 3 : 8 * v + 4], out)
        out = jnp.where(sub == 2 * v + 1, x[8 * v + 7 : 8 * v + 8], out)
    return out


def grow_rows(x):
    sub = iota(x.shape, 0)
    return jnp.concatenate(
        [jnp.where(sub < 4, x[2 * v : 2 * v + 1], x[2 * v + 1 : 2 * v + 2]) for v in range(RR)], axis=0
    )


def kernel(
    n_row,
    n_nest,
    place_ref,
    host_ref,
    state_hbm,
    depth_hbm,
    open_hbm,
    out_ref,
    state_ref,
    depth_ref,
    open_ref,
    load_sems,
    st,
    free,
    first_out,
    first_in,
    bulk_out,
    bulk_in,
    strip_in,
    chosen_out,
    chosen_in,
    ret_out,
    ret_in,
    side_out,
    west_in,
    east_in,
    ext,
    courant_ref,
    ghost_cols,
    ghost_rows,
    patch,
    wet,
    later,
    slab,
    own_wet,
    ret_now,
    first_sems,
    bulk_sems,
    strip_sems,
    chosen_sems,
    ret_send,
    ret_recv,
    halo_send,
    halo_recv,
):
    tiles = n_row * n_nest
    nests = place_ref.shape[0]
    sec, row, col = lax.axis_index("sec"), lax.axis_index("row"), lax.axis_index("nest")
    tile = row * n_nest + col
    is_outer = sec == 0
    has_west, has_east = col > 0, col < n_nest - 1
    has_north, has_south = row > 0, row < n_row - 1
    west, east = (sec, row, col - 1), (sec, row, col + 1)
    north, south = (sec, row - 1, col), (sec, row + 1, col)
    links = ((has_west, west), (has_east, east), (has_north, north), (has_south, south))
    height, width = state_ref.shape[2], state_ref.shape[3]

    barrier = pltpu.get_barrier_semaphore()

    @pl.when(jnp.logical_not(is_outer))
    def _():
        pl.semaphore_signal(barrier, inc=1, device_id=(0, row, col), device_id_type=MESH)

        @pl.loop(0, tiles - 1)
        def _(i):
            t = lax.rem(tile + i + 1, tiles)
            pl.semaphore_signal(
                barrier, inc=1, device_id=(sec, t // n_nest, lax.rem(t, n_nest)), device_id_type=MESH
            )

    loads = [
        pltpu.make_async_copy(source, target, load_sems.at[i])
        for i, (source, target) in enumerate(
            ((state_hbm, state_ref), (depth_hbm, depth_ref), (open_hbm, open_ref))
        )
    ]
    for load in loads:
        load.start()

    def send_to(section, count, src, dst, send_sem, recv_sem):
        @pl.loop(0, tiles)
        def _(i):
            t = lax.rem(2 * tiles - 1 - tile - i, tiles)

            def go():
                pltpu.make_async_remote_copy(
                    src_ref=src,
                    dst_ref=dst,
                    send_sem=send_sem,
                    recv_sem=recv_sem,
                    device_id=(section, t // n_nest, lax.rem(t, n_nest)),
                    device_id_type=MESH,
                ).start()

            if count == tiles:
                go()
            else:
                pl.when(t != tile)(go)

    def send_all(src, dst, send_sem, recv_sem):
        send_to(1 - sec, tiles, src, dst, send_sem, recv_sem)

    def wait_all(whole, sem):
        pltpu.make_async_copy(whole, whole, sem).wait()

    def relays():
        return [
            pltpu.make_async_remote_copy(
                src_ref=src,
                dst_ref=dst.at[tile],
                send_sem=sems.at[0],
                recv_sem=sems.at[1],
                device_id=(1, row, col),
                device_id_type=MESH,
            )
            for src, dst, sems in ((first_out, first_in, first_sems), (bulk_out, bulk_in, bulk_sems))
        ]

    @pl.when(is_outer)
    def _():
        for present, device in links:

            @pl.when(present)
            def _():
                pl.semaphore_signal(barrier, inc=1, device_id=device, device_id_type=MESH)

        slots, covers = [], []
        for p in range(NPOS):
            slot, cover = jnp.int32(0), jnp.int32(0)
            for n in range(nests):
                hit = place_ref[n] == tile * NPOS + p
                slot = jnp.where(hit, host_ref[n], slot)
                cover = jnp.where(hit, 1, cover)
            slots.append(slot)
            covers.append(cover)
        for load in loads:
            load.wait()
        for i in range(2):
            free[7 + i] = jnp.where(open_ref[0, i] > 0, depth_ref[0, i], 0.0)
        levels = []
        for band in range(K):
            lo = band * FINE_ROWS
            hi = lo + BAND
            old = [state_ref[0, f, lo:hi] for f in range(3)]
            level = new_level_ring(old[0], old[1], old[2], COURANT)
            flux_e, flux_s = new_fluxes_ring(old[1], old[2], level, free[7, lo:hi], free[8, lo:hi])
            free[0, lo:hi] = level
            free[1, lo:hi] = flux_e
            free[2, lo:hi] = flux_s
        first_out[...] = pack_strips(
            [[ref.at[f] for f in range(3)] for ref in (state_ref.at[0], free)]
        )
        for band in range(K):
            lo = band * FINE_ROWS
            hi = lo + BAND
            level, flux_e, flux_s = [free[f, lo:hi] for f in range(3)]
            for i in range(2):
                east_gap = flux_e - pltpu.roll(flux_e, 1, 1)
                free[3 + i, lo:hi] = level - COURANT * (east_gap + flux_s)
                level = level - COURANT * (east_gap + (flux_s - pltpu.roll(flux_s, 1, 0)))
                if i == 0:
                    flux_e, flux_s = new_fluxes_ring(
                        flux_e, flux_s, level, free[7, lo:hi], free[8, lo:hi]
                    )
            free[5, lo:hi] = level
            free[6, lo:hi] = flux_s
        for band in range(K):
            first = band * FINE_ROWS + TOP
            for part, chosen in enumerate((ROWS_EARLY, ROWS_LATE)):
                for i, (f, shift) in enumerate(chosen):
                    at = first + shift
                    bulk_out[3 * band + part, i : i + 1] = free[f, at : at + 1]
            bulk_out[3 * band + 2] = pack_sides(free, band)

        peers = jnp.int32(1)
        for present, _device in links:
            peers = peers + jnp.where(present, 1, 0)
        pl.semaphore_wait(barrier, peers)
        for copy in relays():
            copy.start()

        def halo(kind, src, dst, device):
            return pltpu.make_async_remote_copy(
                src_ref=src,
                dst_ref=dst,
                send_sem=halo_send.at[kind],
                recv_sem=halo_recv.at[kind],
                device_id=device,
                device_id_type=MESH,
            )

        fields = [state_ref.at[0, f] for f in range(3)] + [free.at[7 + i] for i in range(2)]
        lane = iota((height, width), 1)
        packed = jnp.zeros((height, width), jnp.float32)
        for i, field in enumerate(fields):
            x = field[...]
            ext[i, 0:height, 0:width] = x
            packed = jnp.where((lane >= 8 * i) & (lane < 8 * i + 4), pltpu.roll(x, 8 * i, 1), packed)
            packed = jnp.where(
                (lane >= 8 * i + 4) & (lane < 8 * i + 8), pltpu.roll(x, 8 * i + 8, 1), packed
            )
        side_out[...] = packed
        to_east = halo(0, side_out, west_in, east)
        to_west = halo(1, side_out, east_in, west)
        top, bottom = pl.ds(0, HALO), pl.ds(height - HALO, HALO)
        below, above = pl.ds(height, HALO), pl.ds(height + HALO, HALO)
        to_south = halo(2, ext.at[:, bottom], ext.at[:, above], south)
        to_north = halo(3, ext.at[:, top], ext.at[:, below], north)

        for present, copy in ((has_east, to_east), (has_west, to_west)):

            @pl.when(present)
            def _():
                copy.start()

        for present, buffer in ((has_west, west_in), (has_east, east_in)):

            @pl.when(jnp.logical_not(present))
            def _():
                buffer[...] = jnp.zeros(buffer.shape, jnp.float32)

        for present, where in ((has_south, below), (has_north, above)):

            @pl.when(jnp.logical_not(present))
            def _():
                ext[:, where] = jnp.zeros((len(fields), HALO, 2 * width), jnp.float32)

        rows, lanes = iota((height + 2 * HALO, 2 * width), 0), iota((height + 2 * HALO, 2 * width), 1)

        def allowed(region, present):
            return jnp.logical_not(region) | (jnp.full(rows.shape, present.astype(jnp.int32)) > 0)

        inside = allowed((rows >= height) & (rows < height + HALO), has_south)
        inside = inside & allowed(rows >= height + HALO, has_north)
        inside = inside & allowed((lanes >= width) & (lanes < width + width // 2), has_east)
        inside = inside & allowed(lanes >= width + width // 2, has_west)
        courant_ref[...] = jnp.where(inside, COURANT, 0.0)

        for present, copy in ((has_west, to_east), (has_east, to_west)):

            @pl.when(present)
            def _():
                copy.wait_recv()

        from_west, from_east = west_in[...], east_in[...]
        for i in range(len(fields)):
            ext[i, 0:height, width:] = jnp.where(
                lane < 4,
                pltpu.roll(from_east, (width - 8 * i) % width, 1),
                jnp.where(lane >= width - 4, pltpu.roll(from_west, width - 8 - 8 * i, 1), 0.0),
            )

        for present, copy in ((has_south, to_south), (has_north, to_north)):

            @pl.when(present)
            def _():
                copy.start()

        for present, copy in ((has_north, to_south), (has_south, to_north)):

            @pl.when(present)
            def _():
                copy.wait_recv()

        for present, copy in (
            (has_east, to_east),
            (has_west, to_west),
            (has_south, to_south),
            (has_north, to_north),
        ):

            @pl.when(present)
            def _():
                copy.wait_send()

        @pl.loop(0, STEPS)
        def _(s):
            surface, eastward, southward = ext[0], ext[1], ext[2]
            level = new_level_ring(surface, eastward, southward, courant_ref[...])
            flux_e, flux_s = new_fluxes_ring(eastward, southward, level, ext[3], ext[4])
            ext[0] = level
            ext[1] = flux_e
            ext[2] = flux_s

            wait_all(ret_in.at[s], ret_recv.at[s])
            ret_now[...] = ret_in[s]
            lane = iota((PH, width), 1)
            for band in range(K):
                first = band * FINE_ROWS + TOP
                merged = [ext[f, first : first + PH, 0:width] for f in range(3)]
                for j in range(RR - 1):
                    p = band * (RR - 1) + j
                    column = LEFT + j * PW
                    block = ret_now[slots[p]]
                    mask = (
                        (lane >= column)
                        & (lane < column + PW)
                        & (jnp.full((PH, width), covers[p], jnp.int32) > 0)
                    )
                    for f in range(3):
                        shifted = pltpu.roll(block, (column - f * PW) % width, 1)
                        merged[f] = jnp.where(mask, shifted, merged[f])
                for f in range(3):
                    ext[f, first : first + PH, 0:width] = merged[f]

        for f in range(3):
            out_ref[0, f] = ext[f, 0:height, 0:width]

        for copy in relays():
            copy.wait_send()

    @pl.when(jnp.logical_not(is_outer))
    def _():
        lane, sub = iota((PH, width), 1), iota((PH, width), 0)
        groups = FINE_ROWS // 8

        for load in loads:
            load.wait()
        for i in range(2):
            own_wet[i] = jnp.where(open_ref[0, i] > 0, depth_ref[0, i], 0.0)
        sources = [state_ref.at[0, f] for f in range(3)] + [own_wet.at[i] for i in range(2)]
        sources.append(state_ref.at[0, 1])
        for k in range(K):
            for side in range(2):
                packed = [jnp.zeros((PH, width), jnp.float32) for _ in range(STRIP_TILES)]
                for f, source in enumerate(sources):
                    if f == 5 and side == 0:
                        continue
                    first = 0 if side == 0 else width - STRIP * (2 if f == 5 else 1)
                    for g in range(groups):
                        at = (f % 2) * groups * STRIP + g * STRIP
                        piece = source[k * FINE_ROWS + 8 * g : k * FINE_ROWS + 8 * g + 8]
                        packed[f // 2] = jnp.where(
                            (lane >= at) & (lane < at + STRIP),
                            pltpu.roll(piece, (at - first) % width, 1),
                            packed[f // 2],
                        )
                for i, x in enumerate(packed):
                    strip_in[col, k, side, i] = x

        pl.semaphore_wait(barrier, tiles - 1)
        first_copy, bulk_copy = relays()
        first_copy.wait_recv()
        send_to(1, tiles - 1, first_in.at[tile], first_in.at[tile], first_sems.at[2], first_sems.at[3])

        @pl.loop(1, n_nest)
        def _(i):
            pltpu.make_async_remote_copy(
                src_ref=strip_in.at[col],
                dst_ref=strip_in.at[col],
                send_sem=strip_sems.at[0],
                recv_sem=strip_sems.at[1],
                device_id=(sec, row, lax.rem(col + i, n_nest)),
                device_id_type=MESH,
            ).start()

        bulk_copy.wait_recv()
        send_to(1, tiles - 1, bulk_in.at[tile], bulk_in.at[tile], bulk_sems.at[2], bulk_sems.at[3])

        def find(keys, wanted, values):
            out = jnp.int32(0)
            for n in range(nests):
                out = jnp.where(keys[n] == wanted, values[n], out)
            return out

        def present(keys, wanted):
            out = jnp.int32(0)
            for n in range(nests):
                out = jnp.where(keys[n] == wanted, 1, out)
            return out

        wants, spots = [], []
        for i in range(n_row):
            at_row = lax.rem(row + i, n_row)
            for k in range(K):
                spot = find(host_ref, (at_row * n_nest + col) * K + k, place_ref)
                if i == 0:
                    spots.append(spot)
                pair = []
                for side in (-1, 1):
                    slot = find(place_ref, spot + side, host_ref)
                    pair.append((slot // (K * n_nest), lax.rem(slot // K, n_nest), lax.rem(slot, K)))
                wants.append(pair)
        lives = [present(host_ref, tile * K + k) for k in range(K)]
        homes = [spot // NPOS for spot in spots]
        bands = [lax.rem(spot, NPOS) // (RR - 1) for spot in spots]
        columns = [lax.rem(spot, RR - 1) for spot in spots]
        near = []
        for k in range(K):
            near.append(
                [
                    jnp.where(
                        (columns[k] + side >= 0) & (columns[k] + side < RR - 1),
                        present(place_ref, spots[k] + side),
                        0,
                    )
                    for side in (-1, 1)
                ]
            )

        gather_from = iota((3 * width, width), 0)
        gather_to = iota((3 * width, width), 1)
        field, lane_in = gather_from // width, lax.rem(gather_from, width)
        weight = jnp.where(
            field == 0,
            1.0 / (RR * RR),
            jnp.where((field == 2) | (lax.rem(lane_in, RR) == RR - 1), 1.0 / RR, 0.0),
        )
        gather = jnp.where(gather_to == field * PW + lane_in // RR, weight, 0.0)
        half = width // K
        fine = iota((width, 2 * width), 1)
        beside = lax.rem(fine, half)
        coarse_lane = jnp.where(
            fine < width,
            NEAR + fine // RR,
            beside // RR + jnp.where(beside < half // 2, NEAR + PW, NEAR - half // RR),
        )
        widen = (iota((width, 2 * width), 0) == coarse_lane).astype(jnp.float32)
        gather, widen = [m.astype(jnp.bfloat16) for m in (gather, widen)]
        own_lanes = (lane >= NEAR) & (lane < NEAR + PW)
        of_first = (lane < half // 2) | (lane >= width - half // 2)

        def by_column(k, choices):
            out = choices[0]
            for j in range(1, len(choices)):
                out = jnp.where(jnp.full(out.shape, columns[k], jnp.int32) == j, choices[j], out)
            return out

        def centred(x, k):
            return by_column(
                k, [pltpu.roll(x, (NEAR - LEFT - j * PW) % width, 1) for j in range(RR - 1)]
            )

        def pick_lane(block, index):
            return jnp.sum(jnp.where(lane == index, block, 0.0), axis=1, keepdims=True)

        def pick_row(block, index):
            return jnp.sum(jnp.where(sub == index, block, 0.0), axis=0, keepdims=True)

        def four(west_0, east_1, west_1, east_0):
            out = jnp.where(lane < half // 2, west_0, east_1)
            out = jnp.where(lane >= half, west_1, out)
            return jnp.where(lane >= width - half // 2, east_0, out)

        def keep_rows(t, lines):
            for k in range(K):
                ghost_rows[t, k, 0:2] = lines[2 * k : 2 * k + 2, 0:width]
            far = lines[:, width:]
            both = jnp.where(sub < 1, far[0:1], far[1:2])
            other = jnp.where(sub < 1, far[2:3], far[3:4])
            ghost_rows[t, K] = jnp.where(of_first, both, other)

        wait_all(first_in.at[pl.ds(0, tiles - 1)], first_sems.at[3])
        blocks = [first_in[homes[k]] for k in range(K)]
        middles = [centred(block, k) for k, block in enumerate(blocks)]
        for t in range(2):
            lines = jnp.zeros((PH, width), jnp.float32)
            ends = []
            for k in range(K):
                at = t * (LEFT + (RR - 1) * PW) + bands[k] * (2 * (RR - 1)) + columns[k]
                to_east = at + RR - 1
                cols = jnp.where(
                    lane < width // 2, pick_lane(blocks[k], at), pick_lane(blocks[k], to_east)
                )
                ghost_cols[t, k] = grow_rows(cols)
                ends.append((pick_lane(blocks[k], at + 1), pick_lane(blocks[k], to_east - 1)))
                for i in range(2):
                    line = pick_row(middles[k], 2 * (t * K + bands[k]) + i)
                    lines = jnp.where(sub == 2 * k + i, line, lines)
            (west_0, east_0), (west_1, east_1) = ends
            ghost_cols[t, K] = grow_rows(four(west_0, east_1, west_1, east_0))
            keep_rows(t, dot_by(lines, widen))

        fine_lane = iota((FINE_ROWS, width), 1)
        own_ends = (fine_lane == 0, fine_lane == width - 1)
        slab_ends = (lax.rem(fine_lane, half) == 0, lax.rem(fine_lane, half) == half - 1)
        slots = [pl.ds(k * FINE_ROWS, FINE_ROWS) for k in range(K)]

        def load_own(source):
            return [[source[f, slot] for f in range(3)] for slot in slots]

        def substeps(which, states):
            wets = [
                [slab[3 + i] if k == K else own_wet[i, slots[k]] for i in range(2)] for k in which
            ]
            old_cols, new_cols = [[ghost_cols[t, k] for k in which] for t in range(2)]
            old_rows, new_rows = [[ghost_rows[t, k] for k in which] for t in range(2)]
            for m in range(1, RR + 1):
                for n, k in enumerate(which):
                    cols = old_cols[n] + (m / RR) * (new_cols[n] - old_cols[n])
                    rows = old_rows[n] + (m / RR) * (new_rows[n] - old_rows[n])
                    ends = slab_ends if k == K else own_ends
                    states[n] = slab_step(states[n], wets[n], cols, rows, *ends)
            return states

        def averages(states):
            sums = dot_by(
                jnp.concatenate(
                    [
                        jnp.concatenate([row_sums(x[0]), row_sums(x[1]), row_picks(x[2])], axis=1)
                        for x in states
                    ],
                    axis=0,
                ),
                gather,
            )
            return [sums[n * PH : (n + 1) * PH] for n in range(len(states))]

        def send_averages(s, coarse):
            for k in range(K):
                ret_out[s, k] = coarse[k]
            send_all(ret_out.at[s], ret_in.at[s, pl.ds(tile * K, K)], ret_send.at[s], ret_recv.at[s])

        def store_own(states):
            for k in range(K):
                for f in range(3):
                    st[f, slots[k]] = states[k][f]

        def next_ghosts(coarse):
            for k in range(K + 1):
                ghost_cols[0, k] = ghost_cols[1, k]
                ghost_rows[0, k] = ghost_rows[1, k]
            lines = jnp.zeros((PH, width), jnp.float32)
            ends = []
            for k in range(K):
                on_left, on_right = [
                    jnp.full((PH, width), cover, jnp.int32) > 0 for cover in near[k]
                ]
                on_left = on_left & (lane >= NEAR - 4) & (lane < NEAR)
                on_right = on_right & (lane >= NEAR + PW) & (lane < NEAR + PW + 4)
                boundary = k * half // RR
                state = []
                for f in range(3):
                    x = patch[k, f, 0:PH]
                    x = jnp.where(own_lanes, pltpu.roll(coarse[k], (NEAR - f * PW) % width, 1), x)
                    low = f * PW + (boundary - 4) % PW
                    x = jnp.where(on_left, pltpu.roll(coarse[K], (NEAR - 4 - low) % width, 1), x)
                    high = f * PW + boundary
                    x = jnp.where(on_right, pltpu.roll(coarse[K], (NEAR + PW - high) % width, 1), x)
                    state.append(jnp.concatenate([x, patch[k, f, PH : 2 * PH]], axis=0))
                level = new_level_ring(state[0], state[1], state[2], COURANT)
                flux_e, flux_s = new_fluxes_ring(state[1], state[2], level, wet[k, 0], wet[k, 1])
                for f, x in enumerate((level, flux_e, flux_s)):
                    patch[k, f] = x
                level8, east8 = level[0:PH], flux_e[0:PH]
                cols = jnp.where(
                    lane < width // 2,
                    pltpu.roll(east8, width - NEAR + 1, 1),
                    pltpu.roll(level8, width - 1 - NEAR - PW, 1),
                )
                ghost_cols[1, k] = grow_rows(cols)
                at = k * half
                ends.append(
                    (
                        pltpu.roll(east8, (at - (NEAR + PW - 1)) % width, 1),
                        pltpu.roll(level8, (at - 1 - NEAR) % width, 1),
                    )
                )
                lines = jnp.where(sub == 2 * k, flux_s[2 * PH - 1 : 2 * PH], lines)
                lines = jnp.where(sub == 2 * k + 1, level[PH : PH + 1], lines)
            (west_0, east_0), (west_1, east_1) = ends
            ghost_cols[1, K] = grow_rows(four(west_0, east_1, west_1, east_0))
            keep_rows(1, dot_by(lines, widen))

        states = substeps(range(K), load_own(state_ref.at[0]))
        store_own(states)
        coarse = averages(states)

        wait_all(strip_in.at[pl.ds(0, n_nest - 1)], strip_sems.at[1])
        for i in range(n_row):
            for k in range(K):
                for side in range(2):
                    _, at_col, at_slot = wants[i * K + k][side]
                    picked = [strip_in[at_col, at_slot, 1 - side, n] for n in range(STRIP_TILES)]
                    for n, x in enumerate(picked):
                        if i == 0:
                            chosen_in[row, k, side, n] = x
                        else:
                            chosen_out[i - 1, k, side, n] = x
            if i > 0:
                pltpu.make_async_remote_copy(
                    src_ref=chosen_out.at[i - 1],
                    dst_ref=chosen_in.at[row],
                    send_sem=chosen_sems.at[0],
                    recv_sem=chosen_sems.at[1],
                    device_id=(sec, lax.rem(row + i, n_row), col),
                    device_id_type=MESH,
                ).start()
        send_averages(0, coarse)

        wait_all(bulk_in.at[pl.ds(0, tiles - 1)], bulk_sems.at[3])
        for k in range(K):
            early, late = [centred(bulk_in[homes[k], 3 * bands[k] + i], k) for i in range(2)]
            flat = bulk_in[homes[k], 3 * bands[k] + 2]
            sides = by_column(
                k, [pltpu.roll(flat, (-8 * len(SIDE_FIELDS) * j) % width, 1) for j in range(RR - 1)]
            )

            def tile_of(block, spots):
                out = jnp.zeros((PH, width), jnp.float32)
                for target, source in spots:
                    out = jnp.where(sub == target, block[source : source + 1], out)
                return out

            outside = [
                tile_of(early, ((0, 0), (1, 1), (7, 5))),
                tile_of(early, ((0, 2), (7, 6))),
                tile_of(early, ((0, 3), (6, 4), (7, 7))),
                tile_of(late, ((0, 3), (7, 4))),
                tile_of(late, ((0, 5), (6, 6), (7, 7))),
            ]
            for i in range(5):
                beside = jnp.where(
                    lane < NEAR + PW // 2,
                    pltpu.roll(sides, (NEAR - 4 - 8 * i) % width, 1),
                    pltpu.roll(sides, (NEAR + PW - 5 - 8 * i) % width, 1),
                )
                target = patch.at[k, i] if i < 3 else wet.at[k, i - 3]
                target[0:PH] = beside
                target[PH : 2 * PH] = outside[i]
            later[k, 0] = tile_of(late, ((1, 0), (6, 1)))
            later[k, 1] = tile_of(late, ((5, 2), (6, 2)))

        wait_all(chosen_in.at[pl.ds(0, n_row - 1)], chosen_sems.at[1])
        sets = [
            [
                [chosen_in[wants[k][side][0], k, side, n] for n in range(STRIP_TILES)]
                for side in range(2)
            ]
            for k in range(K)
        ]
        fits = []
        for k in range(K):
            start = k * half
            on_left, on_right = [jnp.full((PH, width), cover, jnp.int32) > 0 for cover in near[k]]
            before = (start - STRIP) % width
            fits.append(
                (
                    on_left & (lane >= before) & (lane < before + STRIP),
                    on_right & (lane >= start) & (lane < start + STRIP),
                    on_left & (lane == before - 1),
                )
            )
        for f in range(5):
            for g in range(groups):
                out = jnp.zeros((PH, width), jnp.float32)
                at = (f % 2) * groups * STRIP + g * STRIP
                for k in range(K):
                    start = k * half
                    before = (start - STRIP) % width
                    left, right = [sets[k][side][f // 2] for side in range(2)]
                    out = jnp.where(fits[k][0], pltpu.roll(left, (before - at) % width, 1), out)
                    out = jnp.where(fits[k][1], pltpu.roll(right, (start - at) % width, 1), out)
                    if f == 1:
                        extra = groups * STRIP + (g + 1) * STRIP - 1
                        out = jnp.where(
                            fits[k][2],
                            pltpu.roll(sets[k][0][2], (before - 1 - extra) % width, 1),
                            out,
                        )
                slab[f, 8 * g : 8 * g + 8] = out

        def load_slab():
            return [slab[f] for f in range(3)]

        def store_slab(state):
            for f in range(3):
                slab[f] = state[f]

        aside = substeps([K], [load_slab()])
        store_slab(aside[0])
        next_ghosts(coarse + averages(aside))

        @pl.loop(1, STEPS - 1)
        def _(s):
            states = substeps(range(K + 1), load_own(st) + [load_slab()])
            coarse = averages(states)
            send_averages(s, coarse)
            store_own(states)
            store_slab(states[K])

            @pl.when(s == 1)
            def _():
                given = (sub == 1) | (sub == 5) | (sub == 6)
                for k in range(K):
                    for f, value in enumerate((later[k, 0], 0.0, later[k, 1])):
                        patch[k, f, PH : 2 * PH] = jnp.where(given, value, patch[k, f, PH : 2 * PH])

            next_ghosts(coarse)

        states = substeps(range(K), load_own(st))
        send_averages(STEPS - 1, averages(states))
        for k in range(K):
            live = jnp.full((FINE_ROWS, width), lives[k], jnp.int32) > 0
            for f in range(3):
                out_ref[0, f, slots[k]] = jnp.where(live, states[k][f], state_ref[0, f, slots[k]])

        wait_all(first_in.at[pl.ds(0, tiles - 1)], first_sems.at[2])
        wait_all(bulk_in.at[pl.ds(0, tiles - 1)], bulk_sems.at[2])
        wait_all(strip_in.at[pl.ds(0, n_nest - 1)], strip_sems.at[0])
        wait_all(chosen_in.at[pl.ds(0, n_row - 1)], chosen_sems.at[0])
        for s in range(STEPS):
            wait_all(ret_in.at[s], ret_send.at[s])


def on_device(n_row, n_nest, ocean_state, face_depth, face_open, nest_place, nest_host):
    tiles = n_row * n_nest
    height, width = ocean_state.shape[2:]
    f32 = jnp.float32
    vmem = pl.BlockSpec(memory_space=pltpu.VMEM)
    hbm = pl.BlockSpec(memory_space=pl.ANY)
    smem = pl.BlockSpec(memory_space=pltpu.SMEM)
    dma = pltpu.SemaphoreType.DMA
    return pl.pallas_call(
        functools.partial(kernel, n_row, n_nest),
        out_shape=pltpu.VMEM(ocean_state.shape, f32),
        in_specs=[smem, smem, hbm, hbm, hbm],
        out_specs=vmem,
        scratch_shapes=[
            pltpu.VMEM(ocean_state.shape, f32),
            pltpu.VMEM(face_depth.shape, f32),
            pltpu.VMEM(face_open.shape, jnp.int32),
            dma((3,)),
            pltpu.VMEM((3, height, width), f32),
            pltpu.VMEM((9, height, width), f32),
            pltpu.VMEM((PH, width), f32),
            pltpu.VMEM((tiles, PH, width), f32),
            pltpu.VMEM((3 * K, PH, width), f32),
            pltpu.VMEM((tiles, 3 * K, PH, width), f32),
            pltpu.VMEM((n_nest, K, 2, STRIP_TILES, PH, width), f32),
            pltpu.VMEM((n_row, K, 2, STRIP_TILES, PH, width), f32),
            pltpu.VMEM((n_row, K, 2, STRIP_TILES, PH, width), f32),
            pltpu.VMEM((STEPS, K, PH, width), f32),
            pltpu.VMEM((STEPS, tiles * K, PH, width), f32),
            pltpu.VMEM((height, width), f32),
            pltpu.VMEM((height, width), f32),
            pltpu.VMEM((height, width), f32),
            pltpu.VMEM((5, height + 2 * HALO, 2 * width), f32),
            pltpu.VMEM((height + 2 * HALO, 2 * width), f32),
            pltpu.VMEM((2, K + 1, FINE_ROWS, width), f32),
            pltpu.VMEM((2, K + 1, PH, width), f32),
            pltpu.VMEM((K, 3, 2 * PH, width), f32),
            pltpu.VMEM((K, 2, 2 * PH, width), f32),
            pltpu.VMEM((K, 2, PH, width), f32),
            pltpu.VMEM((5, FINE_ROWS, width), f32),
            pltpu.VMEM((2, height, width), f32),
            pltpu.VMEM((tiles * K, PH, width), f32),
            dma((4,)),
            dma((4,)),
            dma((2,)),
            dma((2,)),
            dma((STEPS,)),
            dma((STEPS,)),
            dma((4,)),
            dma((4,)),
        ],
        compiler_params=pltpu.CompilerParams(collective_id=0, has_side_effects=True),
    )(nest_place, nest_host, ocean_state, face_depth, face_open)


def solution(mesh):
    field = P("sec", None, "row", "nest")
    return jax.shard_map(
        functools.partial(on_device, mesh.shape["row"], mesh.shape["nest"]),
        mesh=mesh,
        in_specs=(field, field, field, P(), P()),
        out_specs=field,
        check_vma=False,
    )
```

```python
import functools

import jax
import jax.numpy as jnp
from jax import lax
from jax.experimental import pallas as pl
from jax.experimental.pallas import tpu as pltpu
from jax.sharding import PartitionSpec as P

PH = 8
PW = 32
RR = 4
K = 2
STEPS = 4
NPOS = K * (RR - 1)
COURANT = 0.3
MESH = pl.DeviceIdType.MESH
FINE_ROWS = RR * PH
TOP = (RR - 1) * PH // 2
LEFT = PW // 2
NEAR = PW
STRIP = 16
STRIP_TILES = 3
BAND = (TOP + PH + STEPS + 7) // 8 * 8
HALO = 8
ROWS_EARLY = ((0, PH), (3, PH + 1), (1, PH), (2, PH), (2, -2), (0, -1), (1, -1), (2, -1))
ROWS_LATE = ((4, PH + 1), (5, -2), (6, -2), (7, PH), (7, -1), (8, PH), (8, -2), (8, -1))
SIDE_FIELDS = (0, 1, 2, 7, 8)


def iota(shape, dim):
    return lax.broadcasted_iota(jnp.int32, shape, dim)


def slab_step(fields, wet, cols, rows, west_at, east_at):
    surface, eastward, southward = fields
    height, width = surface.shape
    sub = iota(surface.shape, 0)
    east_behind = jnp.where(west_at, cols, pltpu.roll(eastward, 1, 1))
    south_behind = jnp.where(sub == 0, rows[0:1], pltpu.roll(southward, 1, 0))
    level = surface - COURANT * ((eastward - east_behind) + (southward - south_behind))
    level_east = jnp.where(east_at, cols, pltpu.roll(level, width - 1, 1))
    level_south = jnp.where(sub == height - 1, rows[1:2], pltpu.roll(level, height - 1, 0))
    east = eastward - COURANT * (wet[0] + 0.5 * (level + level_east)) * (level_east - level)
    south = southward - COURANT * (wet[1] + 0.5 * (level + level_south)) * (level_south - level)
    return [level, jnp.where(wet[0] > 0, east, 0.0), jnp.where(wet[1] > 0, south, 0.0)]


def new_level_ring(surface, eastward, southward, courant):
    east_gap = eastward - pltpu.roll(eastward, 1, 1)
    south_gap = southward - pltpu.roll(southward, 1, 0)
    return surface - courant * (east_gap + south_gap)


def new_fluxes_ring(eastward, southward, level, wet_east, wet_south):
    height, width = level.shape
    level_east = pltpu.roll(level, width - 1, 1)
    level_south = pltpu.roll(level, height - 1, 0)
    east = eastward - COURANT * (wet_east + 0.5 * (level + level_east)) * (level_east - level)
    south = southward - COURANT * (wet_south + 0.5 * (level + level_south)) * (level_south - level)
    return jnp.where(wet_east > 0, east, 0.0), jnp.where(wet_south > 0, south, 0.0)


def parts(x):
    high = x.astype(jnp.bfloat16).astype(jnp.float32)
    rest = x - high
    middle = rest.astype(jnp.bfloat16).astype(jnp.float32)
    return high, middle, rest - middle


def dot_by(x, chosen):
    rows = x.shape[0]
    stacked = jnp.concatenate(parts(x), axis=0).astype(jnp.bfloat16)
    y = jnp.dot(stacked, chosen, preferred_element_type=jnp.float32)
    return y[:rows] + (y[rows : 2 * rows] + y[2 * rows :])


def pack_strips(times):
    width = times[0][0].shape[-1]
    lane, sub = iota((PH, width), 1), iota((PH, width), 0)
    block = jnp.zeros((PH, width), jnp.float32)
    span = (RR - 1) * PW
    inner = (lane >= LEFT) & (lane < LEFT + span)
    for t, fields in enumerate(times):
        surface, eastward, southward = fields
        for band in range(K):
            first = band * FINE_ROWS + TOP
            east8 = eastward[first : first + PH, :]
            level8 = surface[first : first + PH, :]
            for j in range(RR - 1):
                column = LEFT + j * PW
                west_lane = t * (LEFT + span) + band * 2 * (RR - 1) + j
                east_lane = west_lane + RR - 1
                block = jnp.where(
                    lane == west_lane, pltpu.roll(east8, (west_lane - column + 1) % width, 1), block
                )
                block = jnp.where(
                    lane == east_lane, pltpu.roll(level8, (east_lane - column - PW) % width, 1), block
                )
            row = (t * K + band) * 2
            block = jnp.where(inner & (sub == row), southward[first - 1 : first, :], block)
            block = jnp.where(inner & (sub == row + 1), surface[first + PH : first + PH + 1, :], block)
    return block


def pack_sides(free, band):
    width = free.shape[-1]
    lane = iota((PH, width), 1)
    block = jnp.zeros((PH, width), jnp.float32)
    first = band * FINE_ROWS + TOP
    for i, f in enumerate(SIDE_FIELDS):
        values = free[f, first : first + PH, :]
        for j in range(RR - 1):
            column = LEFT + j * PW
            target = j * 8 * len(SIDE_FIELDS) + 8 * i
            for side, source in ((0, column - 4), (4, column + PW - 1)):
                at = target + side
                block = jnp.where(
                    (lane >= at) & (lane < at + 4), pltpu.roll(values, (at - source) % width, 1), block
                )
    return block


def row_sums(x):
    width = x.shape[1]
    sub = iota((8, width), 0)
    out = jnp.zeros((8, width), jnp.float32)
    for v in range(x.shape[0] // 8):
        piece = x[8 * v : 8 * v + 8]
        piece = piece + pltpu.roll(piece, 1, 0)
        piece = piece + pltpu.roll(piece, 2, 0)
        out = jnp.where(sub == 2 * v, piece[3:4], out)
        out = jnp.where(sub == 2 * v + 1, piece[7:8], out)
    return out


def row_picks(x):
    width = x.shape[1]
    sub = iota((8, width), 0)
    out = jnp.zeros((8, width), jnp.float32)
    for v in range(x.shape[0] // 8):
        out = jnp.where(sub == 2 * v, x[8 * v + 3 : 8 * v + 4], out)
        out = jnp.where(sub == 2 * v + 1, x[8 * v + 7 : 8 * v + 8], out)
    return out


def grow_rows(x):
    sub = iota(x.shape, 0)
    return jnp.concatenate(
        [jnp.where(sub < 4, x[2 * v : 2 * v + 1], x[2 * v + 1 : 2 * v + 2]) for v in range(RR)], axis=0
    )


def kernel(
    n_row,
    n_nest,
    place_ref,
    host_ref,
    state_hbm,
    depth_hbm,
    open_hbm,
    out_ref,
    state_ref,
    depth_ref,
    open_ref,
    load_sems,
    st,
    free,
    first_out,
    first_in,
    bulk_out,
    bulk_in,
    low_in,
    low_out,
    low_got,
    high_in,
    high_out,
    high_got,
    near_out,
    near_got,
    ret_out,
    ret_in,
    side_out,
    west_in,
    east_in,
    ext,
    courant_ref,
    ghost_cols,
    ghost_rows,
    patch,
    wet,
    later,
    slab,
    own_wet,
    ret_now,
    first_sems,
    bulk_sems,
    low_sems,
    high_sems,
    near_sems,
    ret_send,
    ret_recv,
    halo_send,
    halo_recv,
):
    tiles = n_row * n_nest
    nests = place_ref.shape[0]
    sec, row, col = lax.axis_index("sec"), lax.axis_index("row"), lax.axis_index("nest")
    tile = row * n_nest + col
    is_outer = sec == 0
    has_west, has_east = col > 0, col < n_nest - 1
    has_north, has_south = row > 0, row < n_row - 1
    west, east = (sec, row, col - 1), (sec, row, col + 1)
    north, south = (sec, row - 1, col), (sec, row + 1, col)
    links = ((has_west, west), (has_east, east), (has_north, north), (has_south, south))
    height, width = state_ref.shape[2], state_ref.shape[3]

    barrier = pltpu.get_barrier_semaphore()

    @pl.when(jnp.logical_not(is_outer))
    def _():
        pl.semaphore_signal(barrier, inc=1, device_id=(0, row, col), device_id_type=MESH)

        @pl.loop(0, tiles - 1)
        def _(i):
            t = lax.rem(tile + i + 1, tiles)
            pl.semaphore_signal(
                barrier, inc=1, device_id=(sec, t // n_nest, lax.rem(t, n_nest)), device_id_type=MESH
            )

    loads = [
        pltpu.make_async_copy(source, target, load_sems.at[i])
        for i, (source, target) in enumerate(
            ((state_hbm, state_ref), (depth_hbm, depth_ref), (open_hbm, open_ref))
        )
    ]
    for load in loads:
        load.start()

    def send_to(section, count, src, dst, send_sem, recv_sem):
        @pl.loop(0, tiles)
        def _(i):
            t = lax.rem(2 * tiles - 1 - tile - i, tiles)

            def go():
                pltpu.make_async_remote_copy(
                    src_ref=src,
                    dst_ref=dst,
                    send_sem=send_sem,
                    recv_sem=recv_sem,
                    device_id=(section, t // n_nest, lax.rem(t, n_nest)),
                    device_id_type=MESH,
                ).start()

            if count == tiles:
                go()
            else:
                pl.when(t != tile)(go)

    def send_all(src, dst, send_sem, recv_sem):
        send_to(1 - sec, tiles, src, dst, send_sem, recv_sem)

    def wait_all(whole, sem):
        pltpu.make_async_copy(whole, whole, sem).wait()

    def relays():
        return [
            pltpu.make_async_remote_copy(
                src_ref=src,
                dst_ref=dst,
                send_sem=sems.at[0],
                recv_sem=sems.at[1],
                device_id=(1, row, col),
                device_id_type=MESH,
            )
            for src, dst, sems in (
                (first_out, first_in.at[tile], first_sems),
                (bulk_out, bulk_in.at[row], bulk_sems),
            )
        ]

    @pl.when(is_outer)
    def _():
        for present, device in links:

            @pl.when(present)
            def _():
                pl.semaphore_signal(barrier, inc=1, device_id=device, device_id_type=MESH)

        slots, covers = [], []
        for p in range(NPOS):
            slot, cover = jnp.int32(0), jnp.int32(0)
            for n in range(nests):
                hit = place_ref[n] == tile * NPOS + p
                slot = jnp.where(hit, host_ref[n], slot)
                cover = jnp.where(hit, 1, cover)
            slots.append(slot)
            covers.append(cover)
        for load in loads:
            load.wait()
        for i in range(2):
            free[7 + i] = jnp.where(open_ref[0, i] > 0, depth_ref[0, i], 0.0)
        levels = []
        for band in range(K):
            lo = band * FINE_ROWS
            hi = lo + BAND
            old = [state_ref[0, f, lo:hi] for f in range(3)]
            level = new_level_ring(old[0], old[1], old[2], COURANT)
            flux_e, flux_s = new_fluxes_ring(old[1], old[2], level, free[7, lo:hi], free[8, lo:hi])
            free[0, lo:hi] = level
            free[1, lo:hi] = flux_e
            free[2, lo:hi] = flux_s
        first_out[...] = pack_strips(
            [[ref.at[f] for f in range(3)] for ref in (state_ref.at[0], free)]
        )
        peers = jnp.int32(1)
        for present, _device in links:
            peers = peers + jnp.where(present, 1, 0)
        pl.semaphore_wait(barrier, peers)
        first_copy, bulk_copy = relays()
        first_copy.start()
        for band in range(K):
            lo = band * FINE_ROWS
            hi = lo + BAND
            level, flux_e, flux_s = [free[f, lo:hi] for f in range(3)]
            for i in range(2):
                east_gap = flux_e - pltpu.roll(flux_e, 1, 1)
                free[3 + i, lo:hi] = level - COURANT * (east_gap + flux_s)
                level = level - COURANT * (east_gap + (flux_s - pltpu.roll(flux_s, 1, 0)))
                if i == 0:
                    flux_e, flux_s = new_fluxes_ring(
                        flux_e, flux_s, level, free[7, lo:hi], free[8, lo:hi]
                    )
            free[5, lo:hi] = level
            free[6, lo:hi] = flux_s
        for band in range(K):
            first = band * FINE_ROWS + TOP
            for part, chosen in enumerate((ROWS_EARLY, ROWS_LATE)):
                for i, (f, shift) in enumerate(chosen):
                    at = first + shift
                    bulk_out[3 * band + part, i : i + 1] = free[f, at : at + 1]
            bulk_out[3 * band + 2] = pack_sides(free, band)

        bulk_copy.start()

        def halo(kind, src, dst, device):
            return pltpu.make_async_remote_copy(
                src_ref=src,
                dst_ref=dst,
                send_sem=halo_send.at[kind],
                recv_sem=halo_recv.at[kind],
                device_id=device,
                device_id_type=MESH,
            )

        fields = [state_ref.at[0, f] for f in range(3)] + [free.at[7 + i] for i in range(2)]
        lane = iota((height, width), 1)
        packed = jnp.zeros((height, width), jnp.float32)
        for i, field in enumerate(fields):
            x = field[...]
            ext[i, 0:height, 0:width] = x
            packed = jnp.where((lane >= 8 * i) & (lane < 8 * i + 4), pltpu.roll(x, 8 * i, 1), packed)
            packed = jnp.where(
                (lane >= 8 * i + 4) & (lane < 8 * i + 8), pltpu.roll(x, 8 * i + 8, 1), packed
            )
        side_out[...] = packed
        to_east = halo(0, side_out, west_in, east)
        to_west = halo(1, side_out, east_in, west)
        top, bottom = pl.ds(0, HALO), pl.ds(height - HALO, HALO)
        below, above = pl.ds(height, HALO), pl.ds(height + HALO, HALO)
        to_south = halo(2, ext.at[:, bottom], ext.at[:, above], south)
        to_north = halo(3, ext.at[:, top], ext.at[:, below], north)

        for present, copy in ((has_east, to_east), (has_west, to_west)):

            @pl.when(present)
            def _():
                copy.start()

        for present, buffer in ((has_west, west_in), (has_east, east_in)):

            @pl.when(jnp.logical_not(present))
            def _():
                buffer[...] = jnp.zeros(buffer.shape, jnp.float32)

        for present, where in ((has_south, below), (has_north, above)):

            @pl.when(jnp.logical_not(present))
            def _():
                ext[:, where] = jnp.zeros((len(fields), HALO, 2 * width), jnp.float32)

        rows, lanes = iota((height + 2 * HALO, 2 * width), 0), iota((height + 2 * HALO, 2 * width), 1)

        def allowed(region, present):
            return jnp.logical_not(region) | (jnp.full(rows.shape, present.astype(jnp.int32)) > 0)

        inside = allowed((rows >= height) & (rows < height + HALO), has_south)
        inside = inside & allowed(rows >= height + HALO, has_north)
        inside = inside & allowed((lanes >= width) & (lanes < width + width // 2), has_east)
        inside = inside & allowed(lanes >= width + width // 2, has_west)
        courant_ref[...] = jnp.where(inside, COURANT, 0.0)

        for present, copy in ((has_west, to_east), (has_east, to_west)):

            @pl.when(present)
            def _():
                copy.wait_recv()

        from_west, from_east = west_in[...], east_in[...]
        for i in range(len(fields)):
            ext[i, 0:height, width:] = jnp.where(
                lane < 4,
                pltpu.roll(from_east, (width - 8 * i) % width, 1),
                jnp.where(lane >= width - 4, pltpu.roll(from_west, width - 8 - 8 * i, 1), 0.0),
            )

        for present, copy in ((has_south, to_south), (has_north, to_north)):

            @pl.when(present)
            def _():
                copy.start()

        for present, copy in ((has_north, to_south), (has_south, to_north)):

            @pl.when(present)
            def _():
                copy.wait_recv()

        for present, copy in (
            (has_east, to_east),
            (has_west, to_west),
            (has_south, to_south),
            (has_north, to_north),
        ):

            @pl.when(present)
            def _():
                copy.wait_send()

        @pl.loop(0, STEPS)
        def _(s):
            surface, eastward, southward = ext[0], ext[1], ext[2]
            level = new_level_ring(surface, eastward, southward, courant_ref[...])
            flux_e, flux_s = new_fluxes_ring(eastward, southward, level, ext[3], ext[4])
            ext[0] = level
            ext[1] = flux_e
            ext[2] = flux_s

            wait_all(ret_in.at[s], ret_recv.at[s])
            ret_now[...] = ret_in[s]
            lane = iota((PH, width), 1)
            for band in range(K):
                first = band * FINE_ROWS + TOP
                merged = [ext[f, first : first + PH, 0:width] for f in range(3)]
                for j in range(RR - 1):
                    p = band * (RR - 1) + j
                    column = LEFT + j * PW
                    block = ret_now[slots[p]]
                    mask = (
                        (lane >= column)
                        & (lane < column + PW)
                        & (jnp.full((PH, width), covers[p], jnp.int32) > 0)
                    )
                    for f in range(3):
                        shifted = pltpu.roll(block, (column - f * PW) % width, 1)
                        merged[f] = jnp.where(mask, shifted, merged[f])
                for f in range(3):
                    ext[f, first : first + PH, 0:width] = merged[f]

        for f in range(3):
            out_ref[0, f] = ext[f, 0:height, 0:width]

        for copy in relays():
            copy.wait_send()

    @pl.when(jnp.logical_not(is_outer))
    def _():
        lane, sub = iota((PH, width), 1), iota((PH, width), 0)
        groups = FINE_ROWS // 8

        def find(keys, wanted, values):
            out = jnp.int32(0)
            for n in range(nests):
                out = jnp.where(keys[n] == wanted, values[n], out)
            return out

        def present(keys, wanted):
            out = jnp.int32(0)
            for n in range(nests):
                out = jnp.where(keys[n] == wanted, 1, out)
            return out

        def owner(slot):
            return slot // (K * n_nest), lax.rem(slot // K, n_nest), lax.rem(slot, K)

        spots, low_wants, high_wants, near_wants = [], [], [], []
        for i in range(n_row):
            at_row = lax.rem(row + i, n_row)
            for k in range(K):
                spot = find(host_ref, (at_row * n_nest + col) * K + k, place_ref)
                if i == 0:
                    spots.append(spot)
                low_wants.append(owner(find(place_ref, spot + 1, host_ref)))
        for i in range(n_nest):
            at_col = lax.rem(col + i, n_nest)
            for k in range(K):
                spot = spots[k] if i == 0 else find(host_ref, (row * n_nest + at_col) * K + k, place_ref)
                high_wants.append(owner(find(place_ref, spot - 1, host_ref)))
                near_wants.append(
                    (spot // (NPOS * n_nest), lax.rem(spot // NPOS, n_nest), lax.rem(spot, NPOS) // (RR - 1))
                )
        lives = [present(host_ref, tile * K + k) for k in range(K)]
        homes = [spot // NPOS for spot in spots]
        bands = [lax.rem(spot, NPOS) // (RR - 1) for spot in spots]
        columns = [lax.rem(spot, RR - 1) for spot in spots]
        near = []
        for k in range(K):
            near.append(
                [
                    jnp.where(
                        (columns[k] + side >= 0) & (columns[k] + side < RR - 1),
                        present(place_ref, spots[k] + side),
                        0,
                    )
                    for side in (-1, 1)
                ]
            )

        gather_from = iota((3 * width, width), 0)
        gather_to = iota((3 * width, width), 1)
        field, lane_in = gather_from // width, lax.rem(gather_from, width)
        weight = jnp.where(
            field == 0,
            1.0 / (RR * RR),
            jnp.where((field == 2) | (lax.rem(lane_in, RR) == RR - 1), 1.0 / RR, 0.0),
        )
        gather = jnp.where(gather_to == field * PW + lane_in // RR, weight, 0.0)
        half = width // K
        fine = iota((width, 2 * width), 1)
        beside = lax.rem(fine, half)
        coarse_lane = jnp.where(
            fine < width,
            NEAR + fine // RR,
            beside // RR + jnp.where(beside < half // 2, NEAR + PW, NEAR - half // RR),
        )
        widen = (iota((width, 2 * width), 0) == coarse_lane).astype(jnp.float32)
        gather, widen = [m.astype(jnp.bfloat16) for m in (gather, widen)]
        own_lanes = (lane >= NEAR) & (lane < NEAR + PW)
        of_first = (lane < half // 2) | (lane >= width - half // 2)

        def by_column(k, choices):
            out = choices[0]
            for j in range(1, len(choices)):
                out = jnp.where(jnp.full(out.shape, columns[k], jnp.int32) == j, choices[j], out)
            return out

        def centred(x, k):
            return by_column(
                k, [pltpu.roll(x, (NEAR - LEFT - j * PW) % width, 1) for j in range(RR - 1)]
            )

        def pick_lane(block, index):
            return jnp.sum(jnp.where(lane == index, block, 0.0), axis=1, keepdims=True)

        def pick_row(block, index):
            return jnp.sum(jnp.where(sub == index, block, 0.0), axis=0, keepdims=True)

        def four(west_0, east_1, west_1, east_0):
            out = jnp.where(lane < half // 2, west_0, east_1)
            out = jnp.where(lane >= half, west_1, out)
            return jnp.where(lane >= width - half // 2, east_0, out)

        def keep_rows(t, lines):
            for k in range(K):
                ghost_rows[t, k, 0:2] = lines[2 * k : 2 * k + 2, 0:width]
            far = lines[:, width:]
            both = jnp.where(sub < 1, far[0:1], far[1:2])
            other = jnp.where(sub < 1, far[2:3], far[3:4])
            ghost_rows[t, K] = jnp.where(of_first, both, other)

        for load in loads:
            load.wait()
        for i in range(2):
            own_wet[i] = jnp.where(open_ref[0, i] > 0, depth_ref[0, i], 0.0)
        sources = [state_ref.at[0, f] for f in range(3)] + [own_wet.at[i] for i in range(2)]
        sources.append(state_ref.at[0, 1])
        for k in range(K):
            for side in (1, 0):
                packed = [jnp.zeros((PH, width), jnp.float32) for _ in range(STRIP_TILES)]
                for f, source in enumerate(sources):
                    if f == 5 and side == 0:
                        continue
                    first = 0 if side == 0 else width - STRIP * (2 if f == 5 else 1)
                    for g in range(groups):
                        at = (f % 2) * groups * STRIP + g * STRIP
                        piece = source[k * FINE_ROWS + 8 * g : k * FINE_ROWS + 8 * g + 8]
                        packed[f // 2] = jnp.where(
                            (lane >= at) & (lane < at + STRIP),
                            pltpu.roll(piece, (at - first) % width, 1),
                            packed[f // 2],
                        )
                for i, x in enumerate(packed):
                    if side == 0:
                        low_in[col, k, i] = x
                    else:
                        high_in[row, k, i] = x

        def to_peer(src, dst, sems, first_sem, device):
            pltpu.make_async_remote_copy(
                src_ref=src,
                dst_ref=dst,
                send_sem=sems.at[first_sem],
                recv_sem=sems.at[first_sem + 1],
                device_id=device,
                device_id_type=MESH,
            ).start()

        def in_plane(i):
            return sec, lax.rem(row + i, n_row), col

        def along_nest(i):
            return sec, row, lax.rem(col + i, n_nest)

        pl.semaphore_wait(barrier, tiles - 1)

        @pl.loop(1, n_row)
        def _(i):
            to_peer(high_in.at[row], high_in.at[row], high_sems, 0, in_plane(n_row - i))

        @pl.loop(1, n_nest)
        def _(i):
            to_peer(low_in.at[col], low_in.at[col], low_sems, 0, along_nest(n_nest - i))

        first_copy, bulk_copy = relays()
        first_copy.wait_recv()
        send_to(1, tiles - 1, first_in.at[tile], first_in.at[tile], first_sems.at[2], first_sems.at[3])
        bulk_copy.wait_recv()

        @pl.loop(1, n_row)
        def _(i):
            to_peer(bulk_in.at[row], bulk_in.at[row], bulk_sems, 2, in_plane(n_row - i))

        def pass_on(count, me, wants, pick, out, got, sems, device):
            for i in range(count):
                for k in range(K):
                    for n, x in enumerate(pick(wants[i * K + k])):
                        if i == 0:
                            got[me, k, n] = x
                        else:
                            out[i - 1, k, n] = x
                if i > 0:
                    to_peer(out.at[i - 1], got.at[me], sems[0], sems[1], device(i))

        wait_all(high_in.at[pl.ds(0, n_row - 1)], high_sems.at[1])
        pass_on(
            n_nest,
            col,
            high_wants,
            lambda w: [high_in[w[0], w[2], n] for n in range(STRIP_TILES)],
            high_out,
            high_got,
            (high_sems, 2),
            along_nest,
        )
        wait_all(low_in.at[pl.ds(0, n_nest - 1)], low_sems.at[1])
        pass_on(
            n_row,
            row,
            low_wants,
            lambda w: [low_in[w[1], w[2], n] for n in range(STRIP_TILES)],
            low_out,
            low_got,
            (low_sems, 2),
            in_plane,
        )
        wait_all(bulk_in.at[pl.ds(0, n_row - 1)], bulk_sems.at[3])
        pass_on(
            n_nest,
            col,
            near_wants,
            lambda w: [bulk_in[w[0], 3 * w[2] + n] for n in range(3)],
            near_out,
            near_got,
            (near_sems, 0),
            along_nest,
        )

        wait_all(first_in.at[pl.ds(0, tiles - 1)], first_sems.at[3])
        blocks = [first_in[homes[k]] for k in range(K)]
        middles = [centred(block, k) for k, block in enumerate(blocks)]
        for t in range(2):
            lines = jnp.zeros((PH, width), jnp.float32)
            ends = []
            for k in range(K):
                at = t * (LEFT + (RR - 1) * PW) + bands[k] * (2 * (RR - 1)) + columns[k]
                to_east = at + RR - 1
                cols = jnp.where(
                    lane < width // 2, pick_lane(blocks[k], at), pick_lane(blocks[k], to_east)
                )
                ghost_cols[t, k] = grow_rows(cols)
                ends.append((pick_lane(blocks[k], at + 1), pick_lane(blocks[k], to_east - 1)))
                for i in range(2):
                    line = pick_row(middles[k], 2 * (t * K + bands[k]) + i)
                    lines = jnp.where(sub == 2 * k + i, line, lines)
            (west_0, east_0), (west_1, east_1) = ends
            ghost_cols[t, K] = grow_rows(four(west_0, east_1, west_1, east_0))
            keep_rows(t, dot_by(lines, widen))

        fine_lane = iota((FINE_ROWS, width), 1)
        own_ends = (fine_lane == 0, fine_lane == width - 1)
        slab_ends = (lax.rem(fine_lane, half) == 0, lax.rem(fine_lane, half) == half - 1)
        slots = [pl.ds(k * FINE_ROWS, FINE_ROWS) for k in range(K)]

        def load_own(source):
            return [[source[f, slot] for f in range(3)] for slot in slots]

        def substeps(which, states):
            wets = [
                [slab[3 + i] if k == K else own_wet[i, slots[k]] for i in range(2)] for k in which
            ]
            old_cols, new_cols = [[ghost_cols[t, k] for k in which] for t in range(2)]
            old_rows, new_rows = [[ghost_rows[t, k] for k in which] for t in range(2)]
            for m in range(1, RR + 1):
                for n, k in enumerate(which):
                    cols = old_cols[n] + (m / RR) * (new_cols[n] - old_cols[n])
                    rows = old_rows[n] + (m / RR) * (new_rows[n] - old_rows[n])
                    ends = slab_ends if k == K else own_ends
                    states[n] = slab_step(states[n], wets[n], cols, rows, *ends)
            return states

        def averages(states):
            sums = dot_by(
                jnp.concatenate(
                    [
                        jnp.concatenate([row_sums(x[0]), row_sums(x[1]), row_picks(x[2])], axis=1)
                        for x in states
                    ],
                    axis=0,
                ),
                gather,
            )
            return [sums[n * PH : (n + 1) * PH] for n in range(len(states))]

        def send_averages(s, coarse):
            for k in range(K):
                ret_out[s, k] = coarse[k]
            send_all(ret_out.at[s], ret_in.at[s, pl.ds(tile * K, K)], ret_send.at[s], ret_recv.at[s])

        def store_own(states):
            for k in range(K):
                for f in range(3):
                    st[f, slots[k]] = states[k][f]

        def next_ghosts(coarse):
            for k in range(K + 1):
                ghost_cols[0, k] = ghost_cols[1, k]
                ghost_rows[0, k] = ghost_rows[1, k]
            lines = jnp.zeros((PH, width), jnp.float32)
            ends = []
            for k in range(K):
                on_left, on_right = [
                    jnp.full((PH, width), cover, jnp.int32) > 0 for cover in near[k]
                ]
                on_left = on_left & (lane >= NEAR - 4) & (lane < NEAR)
                on_right = on_right & (lane >= NEAR + PW) & (lane < NEAR + PW + 4)
                boundary = k * half // RR
                state = []
                for f in range(3):
                    x = patch[k, f, 0:PH]
                    x = jnp.where(own_lanes, pltpu.roll(coarse[k], (NEAR - f * PW) % width, 1), x)
                    low = f * PW + (boundary - 4) % PW
                    x = jnp.where(on_left, pltpu.roll(coarse[K], (NEAR - 4 - low) % width, 1), x)
                    high = f * PW + boundary
                    x = jnp.where(on_right, pltpu.roll(coarse[K], (NEAR + PW - high) % width, 1), x)
                    state.append(jnp.concatenate([x, patch[k, f, PH : 2 * PH]], axis=0))
                level = new_level_ring(state[0], state[1], state[2], COURANT)
                flux_e, flux_s = new_fluxes_ring(state[1], state[2], level, wet[k, 0], wet[k, 1])
                for f, x in enumerate((level, flux_e, flux_s)):
                    patch[k, f] = x
                level8, east8 = level[0:PH], flux_e[0:PH]
                cols = jnp.where(
                    lane < width // 2,
                    pltpu.roll(east8, width - NEAR + 1, 1),
                    pltpu.roll(level8, width - 1 - NEAR - PW, 1),
                )
                ghost_cols[1, k] = grow_rows(cols)
                at = k * half
                ends.append(
                    (
                        pltpu.roll(east8, (at - (NEAR + PW - 1)) % width, 1),
                        pltpu.roll(level8, (at - 1 - NEAR) % width, 1),
                    )
                )
                lines = jnp.where(sub == 2 * k, flux_s[2 * PH - 1 : 2 * PH], lines)
                lines = jnp.where(sub == 2 * k + 1, level[PH : PH + 1], lines)
            (west_0, east_0), (west_1, east_1) = ends
            ghost_cols[1, K] = grow_rows(four(west_0, east_1, west_1, east_0))
            keep_rows(1, dot_by(lines, widen))

        states = substeps(range(K), load_own(state_ref.at[0]))
        store_own(states)
        coarse = averages(states)

        send_averages(0, coarse)

        wait_all(near_got.at[pl.ds(0, n_nest - 1)], near_sems.at[1])
        for k in range(K):
            got = [near_got[near_wants[k][1], k, n] for n in range(3)]
            early, late = [centred(x, k) for x in got[:2]]
            flat = got[2]
            sides = by_column(
                k, [pltpu.roll(flat, (-8 * len(SIDE_FIELDS) * j) % width, 1) for j in range(RR - 1)]
            )

            def tile_of(block, spots):
                out = jnp.zeros((PH, width), jnp.float32)
                for target, source in spots:
                    out = jnp.where(sub == target, block[source : source + 1], out)
                return out

            outside = [
                tile_of(early, ((0, 0), (1, 1), (7, 5))),
                tile_of(early, ((0, 2), (7, 6))),
                tile_of(early, ((0, 3), (6, 4), (7, 7))),
                tile_of(late, ((0, 3), (7, 4))),
                tile_of(late, ((0, 5), (6, 6), (7, 7))),
            ]
            for i in range(5):
                beside = jnp.where(
                    lane < NEAR + PW // 2,
                    pltpu.roll(sides, (NEAR - 4 - 8 * i) % width, 1),
                    pltpu.roll(sides, (NEAR + PW - 5 - 8 * i) % width, 1),
                )
                target = patch.at[k, i] if i < 3 else wet.at[k, i - 3]
                target[0:PH] = beside
                target[PH : 2 * PH] = outside[i]
            later[k, 0] = tile_of(late, ((1, 0), (6, 1)))
            later[k, 1] = tile_of(late, ((5, 2), (6, 2)))

        wait_all(high_got.at[pl.ds(0, n_nest - 1)], high_sems.at[3])
        wait_all(low_got.at[pl.ds(0, n_row - 1)], low_sems.at[3])
        sets = [
            [
                [high_got[high_wants[k][1], k, n] for n in range(STRIP_TILES)],
                [low_got[low_wants[k][0], k, n] for n in range(STRIP_TILES)],
            ]
            for k in range(K)
        ]
        fits = []
        for k in range(K):
            start = k * half
            on_left, on_right = [jnp.full((PH, width), cover, jnp.int32) > 0 for cover in near[k]]
            before = (start - STRIP) % width
            fits.append(
                (
                    on_left & (lane >= before) & (lane < before + STRIP),
                    on_right & (lane >= start) & (lane < start + STRIP),
                    on_left & (lane == before - 1),
                )
            )
        for f in range(5):
            for g in range(groups):
                out = jnp.zeros((PH, width), jnp.float32)
                at = (f % 2) * groups * STRIP + g * STRIP
                for k in range(K):
                    start = k * half
                    before = (start - STRIP) % width
                    left, right = [sets[k][side][f // 2] for side in range(2)]
                    out = jnp.where(fits[k][0], pltpu.roll(left, (before - at) % width, 1), out)
                    out = jnp.where(fits[k][1], pltpu.roll(right, (start - at) % width, 1), out)
                    if f == 1:
                        extra = groups * STRIP + (g + 1) * STRIP - 1
                        out = jnp.where(
                            fits[k][2],
                            pltpu.roll(sets[k][0][2], (before - 1 - extra) % width, 1),
                            out,
                        )
                slab[f, 8 * g : 8 * g + 8] = out

        def load_slab():
            return [slab[f] for f in range(3)]

        def store_slab(state):
            for f in range(3):
                slab[f] = state[f]

        aside = substeps([K], [load_slab()])
        store_slab(aside[0])
        next_ghosts(coarse + averages(aside))

        @pl.loop(1, STEPS - 1)
        def _(s):
            states = substeps(range(K + 1), load_own(st) + [load_slab()])
            coarse = averages(states)
            send_averages(s, coarse)
            store_own(states)
            store_slab(states[K])

            @pl.when(s == 1)
            def _():
                given = (sub == 1) | (sub == 5) | (sub == 6)
                for k in range(K):
                    for f, value in enumerate((later[k, 0], 0.0, later[k, 1])):
                        patch[k, f, PH : 2 * PH] = jnp.where(given, value, patch[k, f, PH : 2 * PH])

            next_ghosts(coarse)

        states = substeps(range(K), load_own(st))
        send_averages(STEPS - 1, averages(states))
        for k in range(K):
            live = jnp.full((FINE_ROWS, width), lives[k], jnp.int32) > 0
            for f in range(3):
                out_ref[0, f, slots[k]] = jnp.where(live, states[k][f], state_ref[0, f, slots[k]])

        wait_all(first_in.at[pl.ds(0, tiles - 1)], first_sems.at[2])
        wait_all(bulk_in.at[pl.ds(0, n_row - 1)], bulk_sems.at[2])
        wait_all(low_in.at[pl.ds(0, n_nest - 1)], low_sems.at[0])
        wait_all(low_got.at[pl.ds(0, n_row - 1)], low_sems.at[2])
        wait_all(high_in.at[pl.ds(0, n_row - 1)], high_sems.at[0])
        wait_all(high_got.at[pl.ds(0, n_nest - 1)], high_sems.at[2])
        wait_all(near_got.at[pl.ds(0, n_nest - 1)], near_sems.at[0])
        for s in range(STEPS):
            wait_all(ret_in.at[s], ret_send.at[s])


def on_device(n_row, n_nest, ocean_state, face_depth, face_open, nest_place, nest_host):
    tiles = n_row * n_nest
    height, width = ocean_state.shape[2:]
    f32 = jnp.float32
    vmem = pl.BlockSpec(memory_space=pltpu.VMEM)
    hbm = pl.BlockSpec(memory_space=pl.ANY)
    smem = pl.BlockSpec(memory_space=pltpu.SMEM)
    dma = pltpu.SemaphoreType.DMA
    return pl.pallas_call(
        functools.partial(kernel, n_row, n_nest),
        out_shape=pltpu.VMEM(ocean_state.shape, f32),
        in_specs=[smem, smem, hbm, hbm, hbm],
        out_specs=vmem,
        scratch_shapes=[
            pltpu.VMEM(ocean_state.shape, f32),
            pltpu.VMEM(face_depth.shape, f32),
            pltpu.VMEM(face_open.shape, jnp.int32),
            dma((3,)),
            pltpu.VMEM((3, height, width), f32),
            pltpu.VMEM((9, height, width), f32),
            pltpu.VMEM((PH, width), f32),
            pltpu.VMEM((tiles, PH, width), f32),
            pltpu.VMEM((3 * K, PH, width), f32),
            pltpu.VMEM((n_row, 3 * K, PH, width), f32),
            pltpu.VMEM((n_nest, K, STRIP_TILES, PH, width), f32),
            pltpu.VMEM((n_row, K, STRIP_TILES, PH, width), f32),
            pltpu.VMEM((n_row, K, STRIP_TILES, PH, width), f32),
            pltpu.VMEM((n_row, K, STRIP_TILES, PH, width), f32),
            pltpu.VMEM((n_nest, K, STRIP_TILES, PH, width), f32),
            pltpu.VMEM((n_nest, K, STRIP_TILES, PH, width), f32),
            pltpu.VMEM((n_nest, K, 3, PH, width), f32),
            pltpu.VMEM((n_nest, K, 3, PH, width), f32),
            pltpu.VMEM((STEPS, K, PH, width), f32),
            pltpu.VMEM((STEPS, tiles * K, PH, width), f32),
            pltpu.VMEM((height, width), f32),
            pltpu.VMEM((height, width), f32),
            pltpu.VMEM((height, width), f32),
            pltpu.VMEM((5, height + 2 * HALO, 2 * width), f32),
            pltpu.VMEM((height + 2 * HALO, 2 * width), f32),
            pltpu.VMEM((2, K + 1, FINE_ROWS, width), f32),
            pltpu.VMEM((2, K + 1, PH, width), f32),
            pltpu.VMEM((K, 3, 2 * PH, width), f32),
            pltpu.VMEM((K, 2, 2 * PH, width), f32),
            pltpu.VMEM((K, 2, PH, width), f32),
            pltpu.VMEM((5, FINE_ROWS, width), f32),
            pltpu.VMEM((2, height, width), f32),
            pltpu.VMEM((tiles * K, PH, width), f32),
            dma((4,)),
            dma((4,)),
            dma((4,)),
            dma((4,)),
            dma((2,)),
            dma((STEPS,)),
            dma((STEPS,)),
            dma((4,)),
            dma((4,)),
        ],
        compiler_params=pltpu.CompilerParams(collective_id=0, has_side_effects=True),
    )(nest_place, nest_host, ocean_state, face_depth, face_open)


def solution(mesh):
    field = P("sec", None, "row", "nest")
    return jax.shard_map(
        functools.partial(on_device, mesh.shape["row"], mesh.shape["nest"]),
        mesh=mesh,
        in_specs=(field, field, field, P(), P()),
        out_specs=field,
        check_vma=False,
    )
```

```python
import functools

import jax
import jax.numpy as jnp
from jax import lax
from jax.experimental import pallas as pl
from jax.experimental.pallas import tpu as pltpu
from jax.sharding import PartitionSpec as P

PH = 8
PW = 32
RR = 4
K = 2
STEPS = 4
NPOS = K * (RR - 1)
COURANT = 0.3
MESH = pl.DeviceIdType.MESH
FINE_ROWS = RR * PH
TOP = (RR - 1) * PH // 2
LEFT = PW // 2
NEAR = PW
BORDER = ((0, 0), (1, 0), (2, 0), (1, PW - 1))
STRIP = 16
STRIP_TILES = 3
BAND = (TOP + PH + STEPS + 7) // 8 * 8
HALO = 8
ROWS_EARLY = ((0, PH), (3, PH + 1), (1, PH), (2, PH), (2, -2), (0, -1), (1, -1), (2, -1))
ROWS_LATE = ((4, PH + 1), (5, -2), (6, -2), (7, PH), (7, -1), (8, PH), (8, -2), (8, -1))
SIDE_FIELDS = (0, 1, 2, 7, 8)


def iota(shape, dim):
    return lax.broadcasted_iota(jnp.int32, shape, dim)


def slab_step(fields, wet, cols, rows, west_at, east_at):
    surface, eastward, southward = fields
    height, width = surface.shape
    sub = iota(surface.shape, 0)
    east_behind = jnp.where(west_at, cols, pltpu.roll(eastward, 1, 1))
    south_behind = jnp.where(sub == 0, rows[0:1], pltpu.roll(southward, 1, 0))
    level = surface - COURANT * ((eastward - east_behind) + (southward - south_behind))
    level_east = jnp.where(east_at, cols, pltpu.roll(level, width - 1, 1))
    level_south = jnp.where(sub == height - 1, rows[1:2], pltpu.roll(level, height - 1, 0))
    east = eastward - COURANT * (wet[0] + 0.5 * (level + level_east)) * (level_east - level)
    south = southward - COURANT * (wet[1] + 0.5 * (level + level_south)) * (level_south - level)
    return [level, jnp.where(wet[0] > 0, east, 0.0), jnp.where(wet[1] > 0, south, 0.0)]


def new_level_ring(surface, eastward, southward, courant):
    east_gap = eastward - pltpu.roll(eastward, 1, 1)
    south_gap = southward - pltpu.roll(southward, 1, 0)
    return surface - courant * (east_gap + south_gap)


def new_fluxes_ring(eastward, southward, level, wet_east, wet_south):
    height, width = level.shape
    level_east = pltpu.roll(level, width - 1, 1)
    level_south = pltpu.roll(level, height - 1, 0)
    east = eastward - COURANT * (wet_east + 0.5 * (level + level_east)) * (level_east - level)
    south = southward - COURANT * (wet_south + 0.5 * (level + level_south)) * (level_south - level)
    return jnp.where(wet_east > 0, east, 0.0), jnp.where(wet_south > 0, south, 0.0)


def parts(x):
    high = x.astype(jnp.bfloat16).astype(jnp.float32)
    rest = x - high
    middle = rest.astype(jnp.bfloat16).astype(jnp.float32)
    return high, middle, rest - middle


def dot_by(x, chosen):
    rows = x.shape[0]
    stacked = jnp.concatenate(parts(x), axis=0).astype(jnp.bfloat16)
    y = jnp.dot(stacked, chosen, preferred_element_type=jnp.float32)
    return y[:rows] + (y[rows : 2 * rows] + y[2 * rows :])


def pack_strips(times):
    width = times[0][0].shape[-1]
    lane, sub = iota((PH, width), 1), iota((PH, width), 0)
    block = jnp.zeros((PH, width), jnp.float32)
    span = (RR - 1) * PW
    inner = (lane >= LEFT) & (lane < LEFT + span)
    for t, fields in enumerate(times):
        surface, eastward, southward = fields
        for band in range(K):
            first = band * FINE_ROWS + TOP
            east8 = eastward[first : first + PH, :]
            level8 = surface[first : first + PH, :]
            for j in range(RR - 1):
                column = LEFT + j * PW
                west_lane = t * (LEFT + span) + band * 2 * (RR - 1) + j
                east_lane = west_lane + RR - 1
                block = jnp.where(
                    lane == west_lane, pltpu.roll(east8, (west_lane - column + 1) % width, 1), block
                )
                block = jnp.where(
                    lane == east_lane, pltpu.roll(level8, (east_lane - column - PW) % width, 1), block
                )
            row = (t * K + band) * 2
            block = jnp.where(inner & (sub == row), southward[first - 1 : first, :], block)
            block = jnp.where(inner & (sub == row + 1), surface[first + PH : first + PH + 1, :], block)
    return block


def pack_sides(free, band):
    width = free.shape[-1]
    lane = iota((PH, width), 1)
    block = jnp.zeros((PH, width), jnp.float32)
    first = band * FINE_ROWS + TOP
    for i, f in enumerate(SIDE_FIELDS):
        values = free[f, first : first + PH, :]
        for j in range(RR - 1):
            column = LEFT + j * PW
            target = j * 8 * len(SIDE_FIELDS) + 8 * i
            for side, source in ((0, column - 4), (4, column + PW - 1)):
                at = target + side
                block = jnp.where(
                    (lane >= at) & (lane < at + 4), pltpu.roll(values, (at - source) % width, 1), block
                )
    return block


def row_sums(x):
    width = x.shape[1]
    sub = iota((8, width), 0)
    out = jnp.zeros((8, width), jnp.float32)
    for v in range(x.shape[0] // 8):
        piece = x[8 * v : 8 * v + 8]
        piece = piece + pltpu.roll(piece, 1, 0)
        piece = piece + pltpu.roll(piece, 2, 0)
        out = jnp.where(sub == 2 * v, piece[3:4], out)
        out = jnp.where(sub == 2 * v + 1, piece[7:8], out)
    return out


def row_picks(x):
    width = x.shape[1]
    sub = iota((8, width), 0)
    out = jnp.zeros((8, width), jnp.float32)
    for v in range(x.shape[0] // 8):
        out = jnp.where(sub == 2 * v, x[8 * v + 3 : 8 * v + 4], out)
        out = jnp.where(sub == 2 * v + 1, x[8 * v + 7 : 8 * v + 8], out)
    return out


def grow_rows(x):
    sub = iota(x.shape, 0)
    return jnp.concatenate(
        [jnp.where(sub < 4, x[2 * v : 2 * v + 1], x[2 * v + 1 : 2 * v + 2]) for v in range(RR)], axis=0
    )


def partner(index, step, count):
    if count & (count - 1) == 0:
        return index ^ step
    return lax.rem(index + step, count)


def kernel(
    n_row,
    n_nest,
    place_ref,
    host_ref,
    state_hbm,
    depth_hbm,
    open_hbm,
    out_ref,
    state_ref,
    depth_ref,
    open_ref,
    load_sems,
    st,
    free,
    first_out,
    first_in,
    bulk_out,
    bulk_in,
    low_in,
    low_out,
    low_got,
    high_in,
    high_out,
    high_got,
    near_out,
    near_got,
    edge_out,
    edge_in,
    ret_out,
    ret_in,
    side_out,
    west_in,
    east_in,
    ext,
    courant_ref,
    ghost_cols,
    ghost_rows,
    patch,
    wet,
    later,
    slab,
    own_wet,
    edge_now,
    first_sems,
    bulk_sems,
    low_sems,
    high_sems,
    near_sems,
    ret_send,
    ret_recv,
    halo_send,
    halo_recv,
):
    tiles = n_row * n_nest
    nests = place_ref.shape[0]
    sec, row, col = lax.axis_index("sec"), lax.axis_index("row"), lax.axis_index("nest")
    tile = row * n_nest + col
    is_outer = sec == 0
    has_west, has_east = col > 0, col < n_nest - 1
    has_north, has_south = row > 0, row < n_row - 1
    west, east = (sec, row, col - 1), (sec, row, col + 1)
    north, south = (sec, row - 1, col), (sec, row + 1, col)
    links = ((has_west, west), (has_east, east), (has_north, north), (has_south, south))
    height, width = state_ref.shape[2], state_ref.shape[3]

    barrier = pltpu.get_barrier_semaphore()

    @pl.when(jnp.logical_not(is_outer))
    def _():
        pl.semaphore_signal(barrier, inc=1, device_id=(0, row, col), device_id_type=MESH)

        @pl.loop(0, tiles - 1)
        def _(i):
            t = lax.rem(tile + i + 1, tiles)
            pl.semaphore_signal(
                barrier, inc=1, device_id=(sec, t // n_nest, lax.rem(t, n_nest)), device_id_type=MESH
            )

    loads = [
        pltpu.make_async_copy(source, target, load_sems.at[i])
        for i, (source, target) in enumerate(
            ((state_hbm, state_ref), (depth_hbm, depth_ref), (open_hbm, open_ref))
        )
    ]
    for load in loads:
        load.start()

    def send_to(section, count, src, dst, send_sem, recv_sem):
        for far in range(tiles - 1, tiles - 1 - count, -1):
            pltpu.make_async_remote_copy(
                src_ref=src,
                dst_ref=dst,
                send_sem=send_sem,
                recv_sem=recv_sem,
                device_id=(
                    section,
                    partner(row, far % n_row, n_row),
                    partner(col, far // n_row, n_nest),
                ),
                device_id_type=MESH,
            ).start()

    def send_all(src, dst, send_sem, recv_sem):
        send_to(1 - sec, tiles, src, dst, send_sem, recv_sem)

    def wait_all(whole, sem):
        pltpu.make_async_copy(whole, whole, sem).wait()

    def relays():
        return [
            pltpu.make_async_remote_copy(
                src_ref=src,
                dst_ref=dst,
                send_sem=sems.at[0],
                recv_sem=sems.at[1],
                device_id=(1, row, col),
                device_id_type=MESH,
            )
            for src, dst, sems in (
                (first_out, first_in.at[tile], first_sems),
                (bulk_out, bulk_in.at[row], bulk_sems),
            )
        ]

    @pl.when(is_outer)
    def _():
        for present, device in links:

            @pl.when(present)
            def _():
                pl.semaphore_signal(barrier, inc=1, device_id=device, device_id_type=MESH)

        slots, covers = [], []
        for p in range(NPOS):
            slot, cover = jnp.int32(0), jnp.int32(0)
            for n in range(nests):
                hit = place_ref[n] == tile * NPOS + p
                slot = jnp.where(hit, host_ref[n], slot)
                cover = jnp.where(hit, 1, cover)
            slots.append(slot)
            covers.append(cover)
        for load in loads:
            load.wait()
        for i in range(2):
            free[7 + i] = jnp.where(open_ref[0, i] > 0, depth_ref[0, i], 0.0)
        levels = []
        for band in range(K):
            lo = band * FINE_ROWS
            hi = lo + BAND
            old = [state_ref[0, f, lo:hi] for f in range(3)]
            level = new_level_ring(old[0], old[1], old[2], COURANT)
            flux_e, flux_s = new_fluxes_ring(old[1], old[2], level, free[7, lo:hi], free[8, lo:hi])
            free[0, lo:hi] = level
            free[1, lo:hi] = flux_e
            free[2, lo:hi] = flux_s
        first_out[...] = pack_strips(
            [[ref.at[f] for f in range(3)] for ref in (state_ref.at[0], free)]
        )
        peers = jnp.int32(1)
        for present, _device in links:
            peers = peers + jnp.where(present, 1, 0)
        pl.semaphore_wait(barrier, peers)
        first_copy, bulk_copy = relays()
        first_copy.start()
        for band in range(K):
            lo = band * FINE_ROWS
            hi = lo + BAND
            level, flux_e, flux_s = [free[f, lo:hi] for f in range(3)]
            for i in range(2):
                east_gap = flux_e - pltpu.roll(flux_e, 1, 1)
                free[3 + i, lo:hi] = level - COURANT * (east_gap + flux_s)
                level = level - COURANT * (east_gap + (flux_s - pltpu.roll(flux_s, 1, 0)))
                if i == 0:
                    flux_e, flux_s = new_fluxes_ring(
                        flux_e, flux_s, level, free[7, lo:hi], free[8, lo:hi]
                    )
            free[5, lo:hi] = level
            free[6, lo:hi] = flux_s
        for band in range(K):
            first = band * FINE_ROWS + TOP
            for part, chosen in enumerate((ROWS_EARLY, ROWS_LATE)):
                for i, (f, shift) in enumerate(chosen):
                    at = first + shift
                    bulk_out[3 * band + part, i : i + 1] = free[f, at : at + 1]
            bulk_out[3 * band + 2] = pack_sides(free, band)

        bulk_copy.start()

        def halo(kind, src, dst, device):
            return pltpu.make_async_remote_copy(
                src_ref=src,
                dst_ref=dst,
                send_sem=halo_send.at[kind],
                recv_sem=halo_recv.at[kind],
                device_id=device,
                device_id_type=MESH,
            )

        fields = [state_ref.at[0, f] for f in range(3)] + [free.at[7 + i] for i in range(2)]
        lane = iota((height, width), 1)
        packed = jnp.zeros((height, width), jnp.float32)
        for i, field in enumerate(fields):
            x = field[...]
            ext[i, 0:height, 0:width] = x
            packed = jnp.where((lane >= 8 * i) & (lane < 8 * i + 4), pltpu.roll(x, 8 * i, 1), packed)
            packed = jnp.where(
                (lane >= 8 * i + 4) & (lane < 8 * i + 8), pltpu.roll(x, 8 * i + 8, 1), packed
            )
        side_out[...] = packed
        to_east = halo(0, side_out, west_in, east)
        to_west = halo(1, side_out, east_in, west)
        top, bottom = pl.ds(0, HALO), pl.ds(height - HALO, HALO)
        below, above = pl.ds(height, HALO), pl.ds(height + HALO, HALO)
        to_south = halo(2, ext.at[:, bottom], ext.at[:, above], south)
        to_north = halo(3, ext.at[:, top], ext.at[:, below], north)

        for present, copy in ((has_east, to_east), (has_west, to_west)):

            @pl.when(present)
            def _():
                copy.start()

        for present, buffer in ((has_west, west_in), (has_east, east_in)):

            @pl.when(jnp.logical_not(present))
            def _():
                buffer[...] = jnp.zeros(buffer.shape, jnp.float32)

        for present, where in ((has_south, below), (has_north, above)):

            @pl.when(jnp.logical_not(present))
            def _():
                ext[:, where] = jnp.zeros((len(fields), HALO, 2 * width), jnp.float32)

        rows, lanes = iota((height + 2 * HALO, 2 * width), 0), iota((height + 2 * HALO, 2 * width), 1)

        def allowed(region, present):
            return jnp.logical_not(region) | (jnp.full(rows.shape, present.astype(jnp.int32)) > 0)

        inside = allowed((rows >= height) & (rows < height + HALO), has_south)
        inside = inside & allowed(rows >= height + HALO, has_north)
        inside = inside & allowed((lanes >= width) & (lanes < width + width // 2), has_east)
        inside = inside & allowed(lanes >= width + width // 2, has_west)
        courant_ref[...] = jnp.where(inside, COURANT, 0.0)

        for present, copy in ((has_west, to_east), (has_east, to_west)):

            @pl.when(present)
            def _():
                copy.wait_recv()

        from_west, from_east = west_in[...], east_in[...]
        for i in range(len(fields)):
            ext[i, 0:height, width:] = jnp.where(
                lane < 4,
                pltpu.roll(from_east, (width - 8 * i) % width, 1),
                jnp.where(lane >= width - 4, pltpu.roll(from_west, width - 8 - 8 * i, 1), 0.0),
            )

        for present, copy in ((has_south, to_south), (has_north, to_north)):

            @pl.when(present)
            def _():
                copy.start()

        for present, copy in ((has_north, to_south), (has_south, to_north)):

            @pl.when(present)
            def _():
                copy.wait_recv()

        for present, copy in (
            (has_east, to_east),
            (has_west, to_west),
            (has_south, to_south),
            (has_north, to_north),
        ):

            @pl.when(present)
            def _():
                copy.wait_send()

        def advance():
            surface, eastward, southward = ext[0], ext[1], ext[2]
            level = new_level_ring(surface, eastward, southward, courant_ref[...])
            flux_e, flux_s = new_fluxes_ring(eastward, southward, level, ext[3], ext[4])
            ext[0] = level
            ext[1] = flux_e
            ext[2] = flux_s

        lane, sub = iota((PH, width), 1), iota((PH, width), 0)

        def covered(p):
            return jnp.full((PH, width), covers[p], jnp.int32) > 0

        def merge(parts_of, keep):
            for band in range(K):
                first = band * FINE_ROWS + TOP
                merged = [ext[f, first : first + PH, 0:width] for f in range(3)]
                for j in range(RR - 1):
                    p = band * (RR - 1) + j
                    column = LEFT + j * PW
                    here = covered(p)
                    for f, mask, values in parts_of(p, column):
                        merged[f] = jnp.where(here & mask, values, merged[f])
                for f in range(3):
                    keep(f, first, merged[f])

        def whole_parts(p, column):
            block = ret_in[slots[p]]
            mask = (lane >= column) & (lane < column + PW)
            return [(f, mask, pltpu.roll(block, (column - f * PW) % width, 1)) for f in range(3)]

        def border_parts(p, column):
            device, k = slots[p] // K, lax.rem(slots[p], K)
            line, ends = [
                jnp.broadcast_to(edge_now[device, pl.ds(2 * k + i, 1)], (PH, width)) for i in range(2)
            ]
            items = ends
            for r in range(1, PH):
                items = jnp.where(sub == r, pltpu.roll(ends, width - 16 * r, 1), items)
            inside = (lane >= column) & (lane < column + PW)
            out = []
            for f in range(3):
                out.append((f, inside & (sub == 0), pltpu.roll(line, (column - f * PW) % width, 1)))
            out.append((2, inside & (sub == PH - 1), pltpu.roll(line, (column - 3 * PW) % width, 1)))
            for i, (f, c) in enumerate(BORDER):
                at = column + c
                out.append((f, lane == at, pltpu.roll(items, (at - i) % width, 1)))
            return out

        def keep_inside(f, first, x):
            ext[f, first : first + PH, 0:width] = x

        def keep_result(f, first, x):
            out_ref[0, f, first : first + PH] = x

        @pl.loop(0, STEPS - 1)
        def _(s):
            advance()
            lines = pl.ds(0, 2 * K)
            wait_all(edge_in.at[s, :, lines], ret_recv.at[s])
            edge_now[:, 0 : 2 * K] = edge_in[s, :, 0 : 2 * K]
            merge(border_parts, keep_inside)

        advance()
        for f in range(3):
            out_ref[0, f] = ext[f, 0:height, 0:width]
        for copy in relays():
            copy.wait_send()
        wait_all(ret_in, ret_recv.at[STEPS - 1])
        merge(whole_parts, keep_result)

    @pl.when(jnp.logical_not(is_outer))
    def _():
        lane, sub = iota((PH, width), 1), iota((PH, width), 0)
        groups = FINE_ROWS // 8

        def find(keys, wanted, values):
            out = jnp.int32(0)
            for n in range(nests):
                out = jnp.where(keys[n] == wanted, values[n], out)
            return out

        def present(keys, wanted):
            out = jnp.int32(0)
            for n in range(nests):
                out = jnp.where(keys[n] == wanted, 1, out)
            return out

        def owner(slot):
            return slot // (K * n_nest), lax.rem(slot // K, n_nest), lax.rem(slot, K)

        spots, low_wants, high_wants, near_wants = [], [], [], []
        for i in range(n_row):
            at_row = lax.rem(row + i, n_row)
            for k in range(K):
                spot = find(host_ref, (at_row * n_nest + col) * K + k, place_ref)
                if i == 0:
                    spots.append(spot)
                low_wants.append(owner(find(place_ref, spot + 1, host_ref)))
        for i in range(n_nest):
            at_col = lax.rem(col + i, n_nest)
            for k in range(K):
                spot = spots[k] if i == 0 else find(host_ref, (row * n_nest + at_col) * K + k, place_ref)
                high_wants.append(owner(find(place_ref, spot - 1, host_ref)))
                near_wants.append(
                    (spot // (NPOS * n_nest), lax.rem(spot // NPOS, n_nest), lax.rem(spot, NPOS) // (RR - 1))
                )
        lives = [present(host_ref, tile * K + k) for k in range(K)]
        homes = [spot // NPOS for spot in spots]
        bands = [lax.rem(spot, NPOS) // (RR - 1) for spot in spots]
        columns = [lax.rem(spot, RR - 1) for spot in spots]
        near = []
        for k in range(K):
            near.append(
                [
                    jnp.where(
                        (columns[k] + side >= 0) & (columns[k] + side < RR - 1),
                        present(place_ref, spots[k] + side),
                        0,
                    )
                    for side in (-1, 1)
                ]
            )

        gather_from = iota((3 * width, 2 * width), 0)
        gather_to = iota((3 * width, 2 * width), 1)
        field, lane_in = gather_from // width, lax.rem(gather_from, width)
        weight = jnp.where(
            field == 0,
            1.0 / (RR * RR),
            jnp.where((field == 2) | (lax.rem(lane_in, RR) == RR - 1), 1.0 / RR, 0.0),
        )
        gather = jnp.where(gather_to == field * PW + lane_in // RR, weight, 0.0)
        for i, (f, c) in enumerate(BORDER):
            gather = gather + jnp.where(
                (gather_to >= width)
                & (lax.rem(gather_to, 16) == i)
                & (field == f)
                & (lane_in // RR == c),
                weight,
                0.0,
            )
        half = width // K
        fine = iota((width, 2 * width), 1)
        beside = lax.rem(fine, half)
        coarse_lane = jnp.where(
            fine < width,
            NEAR + fine // RR,
            beside // RR + jnp.where(beside < half // 2, NEAR + PW, NEAR - half // RR),
        )
        widen = (iota((width, 2 * width), 0) == coarse_lane).astype(jnp.float32)
        gather, widen = [m.astype(jnp.bfloat16) for m in (gather, widen)]
        own_lanes = (lane >= NEAR) & (lane < NEAR + PW)
        of_first = (lane < half // 2) | (lane >= width - half // 2)

        def by_column(k, choices):
            out = choices[0]
            for j in range(1, len(choices)):
                out = jnp.where(jnp.full(out.shape, columns[k], jnp.int32) == j, choices[j], out)
            return out

        def centred(x, k):
            return by_column(
                k, [pltpu.roll(x, (NEAR - LEFT - j * PW) % width, 1) for j in range(RR - 1)]
            )

        def pick_lane(block, index):
            return jnp.sum(jnp.where(lane == index, block, 0.0), axis=1, keepdims=True)

        def pick_row(block, index):
            return jnp.sum(jnp.where(sub == index, block, 0.0), axis=0, keepdims=True)

        def four(west_0, east_1, west_1, east_0):
            out = jnp.where(lane < half // 2, west_0, east_1)
            out = jnp.where(lane >= half, west_1, out)
            return jnp.where(lane >= width - half // 2, east_0, out)

        def keep_rows(t, lines):
            for k in range(K):
                ghost_rows[t, k, 0:2] = lines[2 * k : 2 * k + 2, 0:width]
            far = lines[:, width:]
            both = jnp.where(sub < 1, far[0:1], far[1:2])
            other = jnp.where(sub < 1, far[2:3], far[3:4])
            ghost_rows[t, K] = jnp.where(of_first, both, other)

        for load in loads:
            load.wait()
        for i in range(2):
            own_wet[i] = jnp.where(open_ref[0, i] > 0, depth_ref[0, i], 0.0)
        sources = [state_ref.at[0, f] for f in range(3)] + [own_wet.at[i] for i in range(2)]
        sources.append(state_ref.at[0, 1])
        for k in range(K):
            for side in (1, 0):
                packed = [jnp.zeros((PH, width), jnp.float32) for _ in range(STRIP_TILES)]
                for f, source in enumerate(sources):
                    if f == 5 and side == 0:
                        continue
                    first = 0 if side == 0 else width - STRIP * (2 if f == 5 else 1)
                    for g in range(groups):
                        at = (f % 2) * groups * STRIP + g * STRIP
                        piece = source[k * FINE_ROWS + 8 * g : k * FINE_ROWS + 8 * g + 8]
                        packed[f // 2] = jnp.where(
                            (lane >= at) & (lane < at + STRIP),
                            pltpu.roll(piece, (at - first) % width, 1),
                            packed[f // 2],
                        )
                for i, x in enumerate(packed):
                    if side == 0:
                        low_in[col, k, i] = x
                    else:
                        high_in[row, k, i] = x

        def to_peer(src, dst, sems, first_sem, device):
            pltpu.make_async_remote_copy(
                src_ref=src,
                dst_ref=dst,
                send_sem=sems.at[first_sem],
                recv_sem=sems.at[first_sem + 1],
                device_id=device,
                device_id_type=MESH,
            ).start()

        def in_plane(i):
            return sec, lax.rem(row + i, n_row), col

        def along_nest(i):
            return sec, row, lax.rem(col + i, n_nest)

        pl.semaphore_wait(barrier, tiles - 1)

        @pl.loop(1, n_row)
        def _(i):
            to_peer(high_in.at[row], high_in.at[row], high_sems, 0, in_plane(n_row - i))

        @pl.loop(1, n_nest)
        def _(i):
            to_peer(low_in.at[col], low_in.at[col], low_sems, 0, along_nest(n_nest - i))

        first_copy, bulk_copy = relays()
        first_copy.wait_recv()
        send_to(1, tiles - 1, first_in.at[tile], first_in.at[tile], first_sems.at[2], first_sems.at[3])
        bulk_copy.wait_recv()

        @pl.loop(1, n_row)
        def _(i):
            to_peer(bulk_in.at[row], bulk_in.at[row], bulk_sems, 2, in_plane(n_row - i))

        def pass_on(count, me, wants, pick, out, got, sems, device):
            for i in range(count):
                for k in range(K):
                    for n, x in enumerate(pick(wants[i * K + k])):
                        if i == 0:
                            got[me, k, n] = x
                        else:
                            out[i - 1, k, n] = x
                if i > 0:
                    to_peer(out.at[i - 1], got.at[me], sems[0], sems[1], device(i))

        wait_all(high_in.at[pl.ds(0, n_row - 1)], high_sems.at[1])
        pass_on(
            n_nest,
            col,
            high_wants,
            lambda w: [high_in[w[0], w[2], n] for n in range(STRIP_TILES)],
            high_out,
            high_got,
            (high_sems, 2),
            along_nest,
        )
        wait_all(low_in.at[pl.ds(0, n_nest - 1)], low_sems.at[1])
        pass_on(
            n_row,
            row,
            low_wants,
            lambda w: [low_in[w[1], w[2], n] for n in range(STRIP_TILES)],
            low_out,
            low_got,
            (low_sems, 2),
            in_plane,
        )
        wait_all(bulk_in.at[pl.ds(0, n_row - 1)], bulk_sems.at[3])
        pass_on(
            n_nest,
            col,
            near_wants,
            lambda w: [bulk_in[w[0], 3 * w[2] + n] for n in range(3)],
            near_out,
            near_got,
            (near_sems, 0),
            along_nest,
        )

        wait_all(first_in.at[pl.ds(0, tiles - 1)], first_sems.at[3])
        blocks = [first_in[homes[k]] for k in range(K)]
        middles = [centred(block, k) for k, block in enumerate(blocks)]
        for t in range(2):
            lines = jnp.zeros((PH, width), jnp.float32)
            ends = []
            for k in range(K):
                at = t * (LEFT + (RR - 1) * PW) + bands[k] * (2 * (RR - 1)) + columns[k]
                to_east = at + RR - 1
                cols = jnp.where(
                    lane < width // 2, pick_lane(blocks[k], at), pick_lane(blocks[k], to_east)
                )
                ghost_cols[t, k] = grow_rows(cols)
                ends.append((pick_lane(blocks[k], at + 1), pick_lane(blocks[k], to_east - 1)))
                for i in range(2):
                    line = pick_row(middles[k], 2 * (t * K + bands[k]) + i)
                    lines = jnp.where(sub == 2 * k + i, line, lines)
            (west_0, east_0), (west_1, east_1) = ends
            ghost_cols[t, K] = grow_rows(four(west_0, east_1, west_1, east_0))
            keep_rows(t, dot_by(lines, widen))

        fine_lane = iota((FINE_ROWS, width), 1)
        own_ends = (fine_lane == 0, fine_lane == width - 1)
        slab_ends = (lax.rem(fine_lane, half) == 0, lax.rem(fine_lane, half) == half - 1)
        slots = [pl.ds(k * FINE_ROWS, FINE_ROWS) for k in range(K)]

        def load_own(source):
            return [[source[f, slot] for f in range(3)] for slot in slots]

        def substeps(which, states):
            wets = [
                [slab[3 + i] if k == K else own_wet[i, slots[k]] for i in range(2)] for k in which
            ]
            old_cols, new_cols = [[ghost_cols[t, k] for k in which] for t in range(2)]
            old_rows, new_rows = [[ghost_rows[t, k] for k in which] for t in range(2)]
            for m in range(1, RR + 1):
                for n, k in enumerate(which):
                    cols = old_cols[n] + (m / RR) * (new_cols[n] - old_cols[n])
                    rows = old_rows[n] + (m / RR) * (new_rows[n] - old_rows[n])
                    ends = slab_ends if k == K else own_ends
                    states[n] = slab_step(states[n], wets[n], cols, rows, *ends)
            return states

        def averages(states):
            sums = dot_by(
                jnp.concatenate(
                    [
                        jnp.concatenate([row_sums(x[0]), row_sums(x[1]), row_picks(x[2])], axis=1)
                        for x in states
                    ],
                    axis=0,
                ),
                gather,
            )
            sums = [sums[n * PH : (n + 1) * PH] for n in range(len(states))]
            return [x[:, 0:width] for x in sums], [x[:, width:] for x in sums]

        def send_border(s, coarse, border):
            for k in range(K):
                last = pltpu.roll(coarse[k], PW, 1)
                edge_out[s, 2 * k : 2 * k + 1] = jnp.where(
                    lane[0:1] < 3 * PW, coarse[k][0:1], last[PH - 1 : PH]
                )
                edge_out[s, 2 * k + 1 : 2 * k + 2] = jnp.sum(
                    jnp.where(lane // 16 == sub, border[k], 0.0), axis=0, keepdims=True
                )
            lines = pl.ds(0, 2 * K)
            send_all(edge_out.at[s, lines], edge_in.at[s, tile, lines], ret_send.at[s], ret_recv.at[s])

        def store_own(states):
            for k in range(K):
                for f in range(3):
                    st[f, slots[k]] = states[k][f]

        def next_ghosts(coarse):
            for k in range(K + 1):
                ghost_cols[0, k] = ghost_cols[1, k]
                ghost_rows[0, k] = ghost_rows[1, k]
            lines = jnp.zeros((PH, width), jnp.float32)
            ends = []
            for k in range(K):
                on_left, on_right = [
                    jnp.full((PH, width), cover, jnp.int32) > 0 for cover in near[k]
                ]
                on_left = on_left & (lane >= NEAR - 4) & (lane < NEAR)
                on_right = on_right & (lane >= NEAR + PW) & (lane < NEAR + PW + 4)
                boundary = k * half // RR
                state = []
                for f in range(3):
                    x = patch[k, f, 0:PH]
                    x = jnp.where(own_lanes, pltpu.roll(coarse[k], (NEAR - f * PW) % width, 1), x)
                    low = f * PW + (boundary - 4) % PW
                    x = jnp.where(on_left, pltpu.roll(coarse[K], (NEAR - 4 - low) % width, 1), x)
                    high = f * PW + boundary
                    x = jnp.where(on_right, pltpu.roll(coarse[K], (NEAR + PW - high) % width, 1), x)
                    state.append(jnp.concatenate([x, patch[k, f, PH : 2 * PH]], axis=0))
                level = new_level_ring(state[0], state[1], state[2], COURANT)
                flux_e, flux_s = new_fluxes_ring(state[1], state[2], level, wet[k, 0], wet[k, 1])
                for f, x in enumerate((level, flux_e, flux_s)):
                    patch[k, f] = x
                level8, east8 = level[0:PH], flux_e[0:PH]
                cols = jnp.where(
                    lane < width // 2,
                    pltpu.roll(east8, width - NEAR + 1, 1),
                    pltpu.roll(level8, width - 1 - NEAR - PW, 1),
                )
                ghost_cols[1, k] = grow_rows(cols)
                at = k * half
                ends.append(
                    (
                        pltpu.roll(east8, (at - (NEAR + PW - 1)) % width, 1),
                        pltpu.roll(level8, (at - 1 - NEAR) % width, 1),
                    )
                )
                lines = jnp.where(sub == 2 * k, flux_s[2 * PH - 1 : 2 * PH], lines)
                lines = jnp.where(sub == 2 * k + 1, level[PH : PH + 1], lines)
            (west_0, east_0), (west_1, east_1) = ends
            ghost_cols[1, K] = grow_rows(four(west_0, east_1, west_1, east_0))
            keep_rows(1, dot_by(lines, widen))

        states = substeps(range(K), load_own(state_ref.at[0]))
        store_own(states)
        coarse, border = averages(states)


        send_border(0, coarse, border)

        wait_all(near_got.at[pl.ds(0, n_nest - 1)], near_sems.at[1])
        for k in range(K):
            got = [near_got[near_wants[k][1], k, n] for n in range(3)]
            early, late = [centred(x, k) for x in got[:2]]
            flat = got[2]
            sides = by_column(
                k, [pltpu.roll(flat, (-8 * len(SIDE_FIELDS) * j) % width, 1) for j in range(RR - 1)]
            )

            def tile_of(block, spots):
                out = jnp.zeros((PH, width), jnp.float32)
                for target, source in spots:
                    out = jnp.where(sub == target, block[source : source + 1], out)
                return out

            outside = [
                tile_of(early, ((0, 0), (1, 1), (7, 5))),
                tile_of(early, ((0, 2), (7, 6))),
                tile_of(early, ((0, 3), (6, 4), (7, 7))),
                tile_of(late, ((0, 3), (7, 4))),
                tile_of(late, ((0, 5), (6, 6), (7, 7))),
            ]
            for i in range(5):
                beside = jnp.where(
                    lane < NEAR + PW // 2,
                    pltpu.roll(sides, (NEAR - 4 - 8 * i) % width, 1),
                    pltpu.roll(sides, (NEAR + PW - 5 - 8 * i) % width, 1),
                )
                target = patch.at[k, i] if i < 3 else wet.at[k, i - 3]
                target[0:PH] = beside
                target[PH : 2 * PH] = outside[i]
            later[k, 0] = tile_of(late, ((1, 0), (6, 1)))
            later[k, 1] = tile_of(late, ((5, 2), (6, 2)))

        wait_all(high_got.at[pl.ds(0, n_nest - 1)], high_sems.at[3])
        wait_all(low_got.at[pl.ds(0, n_row - 1)], low_sems.at[3])
        sets = [
            [
                [high_got[high_wants[k][1], k, n] for n in range(STRIP_TILES)],
                [low_got[low_wants[k][0], k, n] for n in range(STRIP_TILES)],
            ]
            for k in range(K)
        ]
        fits = []
        for k in range(K):
            start = k * half
            on_left, on_right = [jnp.full((PH, width), cover, jnp.int32) > 0 for cover in near[k]]
            before = (start - STRIP) % width
            fits.append(
                (
                    on_left & (lane >= before) & (lane < before + STRIP),
                    on_right & (lane >= start) & (lane < start + STRIP),
                    on_left & (lane == before - 1),
                )
            )
        for f in range(5):
            for g in range(groups):
                out = jnp.zeros((PH, width), jnp.float32)
                at = (f % 2) * groups * STRIP + g * STRIP
                for k in range(K):
                    start = k * half
                    before = (start - STRIP) % width
                    left, right = [sets[k][side][f // 2] for side in range(2)]
                    out = jnp.where(fits[k][0], pltpu.roll(left, (before - at) % width, 1), out)
                    out = jnp.where(fits[k][1], pltpu.roll(right, (start - at) % width, 1), out)
                    if f == 1:
                        extra = groups * STRIP + (g + 1) * STRIP - 1
                        out = jnp.where(
                            fits[k][2],
                            pltpu.roll(sets[k][0][2], (before - 1 - extra) % width, 1),
                            out,
                        )
                slab[f, 8 * g : 8 * g + 8] = out

        def load_slab():
            return [slab[f] for f in range(3)]

        def store_slab(state):
            for f in range(3):
                slab[f] = state[f]

        aside = substeps([K], [load_slab()])
        store_slab(aside[0])
        next_ghosts(coarse + averages(aside)[0])

        @pl.loop(1, STEPS - 1)
        def _(s):
            states = substeps(range(K + 1), load_own(st) + [load_slab()])
            coarse, border = averages(states)
            send_border(s, coarse, border)
            store_own(states)
            store_slab(states[K])

            @pl.when(s == 1)
            def _():
                given = (sub == 1) | (sub == 5) | (sub == 6)
                for k in range(K):
                    for f, value in enumerate((later[k, 0], 0.0, later[k, 1])):
                        patch[k, f, PH : 2 * PH] = jnp.where(given, value, patch[k, f, PH : 2 * PH])

            next_ghosts(coarse)

        states = substeps(range(K), load_own(st))
        coarse, _ = averages(states)
        for k in range(K):
            ret_out[k] = coarse[k]
        send_all(ret_out, ret_in.at[pl.ds(tile * K, K)], ret_send.at[STEPS - 1], ret_recv.at[STEPS - 1])
        for k in range(K):
            live = jnp.full((FINE_ROWS, width), lives[k], jnp.int32) > 0
            for f in range(3):
                out_ref[0, f, slots[k]] = jnp.where(live, states[k][f], state_ref[0, f, slots[k]])

        wait_all(first_in.at[pl.ds(0, tiles - 1)], first_sems.at[2])
        wait_all(bulk_in.at[pl.ds(0, n_row - 1)], bulk_sems.at[2])
        wait_all(low_in.at[pl.ds(0, n_nest - 1)], low_sems.at[0])
        wait_all(low_got.at[pl.ds(0, n_row - 1)], low_sems.at[2])
        wait_all(high_in.at[pl.ds(0, n_row - 1)], high_sems.at[0])
        wait_all(high_got.at[pl.ds(0, n_nest - 1)], high_sems.at[2])
        wait_all(near_got.at[pl.ds(0, n_nest - 1)], near_sems.at[0])
        for s in range(STEPS - 1):
            wait_all(edge_in.at[s, :, pl.ds(0, 2 * K)], ret_send.at[s])
        wait_all(ret_in, ret_send.at[STEPS - 1])


def on_device(n_row, n_nest, ocean_state, face_depth, face_open, nest_place, nest_host):
    tiles = n_row * n_nest
    height, width = ocean_state.shape[2:]
    f32 = jnp.float32
    vmem = pl.BlockSpec(memory_space=pltpu.VMEM)
    hbm = pl.BlockSpec(memory_space=pl.ANY)
    smem = pl.BlockSpec(memory_space=pltpu.SMEM)
    dma = pltpu.SemaphoreType.DMA
    return pl.pallas_call(
        functools.partial(kernel, n_row, n_nest),
        out_shape=pltpu.VMEM(ocean_state.shape, f32),
        in_specs=[smem, smem, hbm, hbm, hbm],
        out_specs=vmem,
        scratch_shapes=[
            pltpu.VMEM(ocean_state.shape, f32),
            pltpu.VMEM(face_depth.shape, f32),
            pltpu.VMEM(face_open.shape, jnp.int32),
            dma((3,)),
            pltpu.VMEM((3, height, width), f32),
            pltpu.VMEM((9, height, width), f32),
            pltpu.VMEM((PH, width), f32),
            pltpu.VMEM((tiles, PH, width), f32),
            pltpu.VMEM((3 * K, PH, width), f32),
            pltpu.VMEM((n_row, 3 * K, PH, width), f32),
            pltpu.VMEM((n_nest, K, STRIP_TILES, PH, width), f32),
            pltpu.VMEM((n_row, K, STRIP_TILES, PH, width), f32),
            pltpu.VMEM((n_row, K, STRIP_TILES, PH, width), f32),
            pltpu.VMEM((n_row, K, STRIP_TILES, PH, width), f32),
            pltpu.VMEM((n_nest, K, STRIP_TILES, PH, width), f32),
            pltpu.VMEM((n_nest, K, STRIP_TILES, PH, width), f32),
            pltpu.VMEM((n_nest, K, 3, PH, width), f32),
            pltpu.VMEM((n_nest, K, 3, PH, width), f32),
            pltpu.VMEM((STEPS - 1, PH, width), f32),
            pltpu.VMEM((STEPS - 1, tiles, PH, width), f32),
            pltpu.VMEM((K, PH, width), f32),
            pltpu.VMEM((tiles * K, PH, width), f32),
            pltpu.VMEM((height, width), f32),
            pltpu.VMEM((height, width), f32),
            pltpu.VMEM((height, width), f32),
            pltpu.VMEM((5, height + 2 * HALO, 2 * width), f32),
            pltpu.VMEM((height + 2 * HALO, 2 * width), f32),
            pltpu.VMEM((2, K + 1, FINE_ROWS, width), f32),
            pltpu.VMEM((2, K + 1, PH, width), f32),
            pltpu.VMEM((K, 3, 2 * PH, width), f32),
            pltpu.VMEM((K, 2, 2 * PH, width), f32),
            pltpu.VMEM((K, 2, PH, width), f32),
            pltpu.VMEM((5, FINE_ROWS, width), f32),
            pltpu.VMEM((2, height, width), f32),
            pltpu.VMEM((tiles, PH, width), f32),
            dma((4,)),
            dma((4,)),
            dma((4,)),
            dma((4,)),
            dma((2,)),
            dma((STEPS,)),
            dma((STEPS,)),
            dma((4,)),
            dma((4,)),
        ],
        compiler_params=pltpu.CompilerParams(collective_id=0, has_side_effects=True),
    )(nest_place, nest_host, ocean_state, face_depth, face_open)


def solution(mesh):
    field = P("sec", None, "row", "nest")
    return jax.shard_map(
        functools.partial(on_device, mesh.shape["row"], mesh.shape["nest"]),
        mesh=mesh,
        in_specs=(field, field, field, P(), P()),
        out_specs=field,
        check_vma=False,
    )
```

```python
import functools

import jax
import jax.numpy as jnp
from jax import lax
from jax.experimental import pallas as pl
from jax.experimental.pallas import tpu as pltpu
from jax.sharding import PartitionSpec as P

PH = 8
PW = 32
RR = 4
K = 2
STEPS = 4
NPOS = K * (RR - 1)
COURANT = 0.3
MESH = pl.DeviceIdType.MESH
FINE_ROWS = RR * PH
TOP = (RR - 1) * PH // 2
LEFT = PW // 2
NEAR = PW
BORDER = ((0, 0), (1, 0), (2, 0), (1, PW - 1))
STRIP = 16
STRIP_TILES = 3
BAND = (TOP + PH + STEPS + 7) // 8 * 8
HALO = 8
ROWS_EARLY = ((0, PH), (3, PH + 1), (1, PH), (2, PH), (2, -2), (0, -1), (1, -1), (2, -1))
ROWS_LATE = ((4, PH + 1), (5, -2), (6, -2), (7, PH), (7, -1), (8, PH), (8, -2), (8, -1))
SIDE_FIELDS = (0, 1, 2, 7, 8)


def iota(shape, dim):
    return lax.broadcasted_iota(jnp.int32, shape, dim)


def slab_step(fields, wet, cols, rows, west_at, east_at):
    surface, eastward, southward = fields
    height, width = surface.shape
    sub = iota(surface.shape, 0)
    east_behind = jnp.where(west_at, cols, pltpu.roll(eastward, 1, 1))
    south_behind = jnp.where(sub == 0, rows[0:1], pltpu.roll(southward, 1, 0))
    level = surface - COURANT * ((eastward - east_behind) + (southward - south_behind))
    level_east = jnp.where(east_at, cols, pltpu.roll(level, width - 1, 1))
    level_south = jnp.where(sub == height - 1, rows[1:2], pltpu.roll(level, height - 1, 0))
    east = eastward - COURANT * (wet[0] + 0.5 * (level + level_east)) * (level_east - level)
    south = southward - COURANT * (wet[1] + 0.5 * (level + level_south)) * (level_south - level)
    return [level, jnp.where(wet[0] > 0, east, 0.0), jnp.where(wet[1] > 0, south, 0.0)]


def new_level_ring(surface, eastward, southward, courant):
    east_gap = eastward - pltpu.roll(eastward, 1, 1)
    south_gap = southward - pltpu.roll(southward, 1, 0)
    return surface - courant * (east_gap + south_gap)


def new_fluxes_ring(eastward, southward, level, wet_east, wet_south):
    height, width = level.shape
    level_east = pltpu.roll(level, width - 1, 1)
    level_south = pltpu.roll(level, height - 1, 0)
    east = eastward - COURANT * (wet_east + 0.5 * (level + level_east)) * (level_east - level)
    south = southward - COURANT * (wet_south + 0.5 * (level + level_south)) * (level_south - level)
    return jnp.where(wet_east > 0, east, 0.0), jnp.where(wet_south > 0, south, 0.0)


def parts(x):
    high = x.astype(jnp.bfloat16).astype(jnp.float32)
    rest = x - high
    middle = rest.astype(jnp.bfloat16).astype(jnp.float32)
    return high, middle, rest - middle


def dot_by(x, chosen):
    rows = x.shape[0]
    stacked = jnp.concatenate(parts(x), axis=0).astype(jnp.bfloat16)
    y = jnp.dot(stacked, chosen, preferred_element_type=jnp.float32)
    return y[:rows] + (y[rows : 2 * rows] + y[2 * rows :])


def pack_strips(times):
    width = times[0][0].shape[-1]
    lane, sub = iota((PH, width), 1), iota((PH, width), 0)
    block = jnp.zeros((PH, width), jnp.float32)
    span = (RR - 1) * PW
    inner = (lane >= LEFT) & (lane < LEFT + span)
    for t, fields in enumerate(times):
        surface, eastward, southward = fields
        for band in range(K):
            first = band * FINE_ROWS + TOP
            east8 = eastward[first : first + PH, :]
            level8 = surface[first : first + PH, :]
            for j in range(RR - 1):
                column = LEFT + j * PW
                west_lane = t * (LEFT + span) + band * 2 * (RR - 1) + j
                east_lane = west_lane + RR - 1
                block = jnp.where(
                    lane == west_lane, pltpu.roll(east8, (west_lane - column + 1) % width, 1), block
                )
                block = jnp.where(
                    lane == east_lane, pltpu.roll(level8, (east_lane - column - PW) % width, 1), block
                )
            row = (t * K + band) * 2
            block = jnp.where(inner & (sub == row), southward[first - 1 : first, :], block)
            block = jnp.where(inner & (sub == row + 1), surface[first + PH : first + PH + 1, :], block)
    return block


def pack_sides(free, band):
    width = free.shape[-1]
    lane = iota((PH, width), 1)
    block = jnp.zeros((PH, width), jnp.float32)
    first = band * FINE_ROWS + TOP
    for i, f in enumerate(SIDE_FIELDS):
        values = free[f, first : first + PH, :]
        for j in range(RR - 1):
            column = LEFT + j * PW
            target = j * 8 * len(SIDE_FIELDS) + 8 * i
            for side, source in ((0, column - 4), (4, column + PW - 1)):
                at = target + side
                block = jnp.where(
                    (lane >= at) & (lane < at + 4), pltpu.roll(values, (at - source) % width, 1), block
                )
    return block


def row_sums(x):
    width = x.shape[1]
    sub = iota((8, width), 0)
    out = jnp.zeros((8, width), jnp.float32)
    for v in range(x.shape[0] // 8):
        piece = x[8 * v : 8 * v + 8]
        piece = piece + pltpu.roll(piece, 1, 0)
        piece = piece + pltpu.roll(piece, 2, 0)
        out = jnp.where(sub == 2 * v, piece[3:4], out)
        out = jnp.where(sub == 2 * v + 1, piece[7:8], out)
    return out


def row_picks(x):
    width = x.shape[1]
    sub = iota((8, width), 0)
    out = jnp.zeros((8, width), jnp.float32)
    for v in range(x.shape[0] // 8):
        out = jnp.where(sub == 2 * v, x[8 * v + 3 : 8 * v + 4], out)
        out = jnp.where(sub == 2 * v + 1, x[8 * v + 7 : 8 * v + 8], out)
    return out


def grow_rows(x):
    sub = iota(x.shape, 0)
    return jnp.concatenate(
        [jnp.where(sub < 4, x[2 * v : 2 * v + 1], x[2 * v + 1 : 2 * v + 2]) for v in range(RR)], axis=0
    )


def partner(index, step, count):
    if count & (count - 1) == 0:
        return index ^ step
    return lax.rem(index + step, count)


def kernel(
    n_row,
    n_nest,
    place_ref,
    host_ref,
    state_hbm,
    depth_hbm,
    open_hbm,
    out_ref,
    state_ref,
    depth_ref,
    open_ref,
    load_sems,
    st,
    free,
    first_out,
    first_in,
    bulk_out,
    bulk_in,
    low_in,
    low_out,
    low_got,
    high_in,
    high_out,
    high_got,
    near_out,
    near_got,
    edge_out,
    edge_in,
    ret_out,
    ret_in,
    side_out,
    west_in,
    east_in,
    ext,
    courant_ref,
    ghost_cols,
    ghost_rows,
    patch,
    wet,
    later,
    slab,
    own_wet,
    edge_now,
    first_sems,
    bulk_sems,
    low_sems,
    high_sems,
    near_sems,
    ret_send,
    ret_recv,
    halo_send,
    halo_recv,
):
    tiles = n_row * n_nest
    nests = place_ref.shape[0]
    sec, row, col = lax.axis_index("sec"), lax.axis_index("row"), lax.axis_index("nest")
    tile = row * n_nest + col
    is_outer = sec == 0
    has_west, has_east = col > 0, col < n_nest - 1
    has_north, has_south = row > 0, row < n_row - 1
    west, east = (sec, row, col - 1), (sec, row, col + 1)
    north, south = (sec, row - 1, col), (sec, row + 1, col)
    links = ((has_west, west), (has_east, east), (has_north, north), (has_south, south))
    height, width = state_ref.shape[2], state_ref.shape[3]

    barrier = pltpu.get_barrier_semaphore()

    @pl.when(jnp.logical_not(is_outer))
    def _():
        pl.semaphore_signal(barrier, inc=1, device_id=(0, row, col), device_id_type=MESH)

        @pl.loop(0, tiles - 1)
        def _(i):
            t = lax.rem(tile + i + 1, tiles)
            pl.semaphore_signal(
                barrier, inc=1, device_id=(sec, t // n_nest, lax.rem(t, n_nest)), device_id_type=MESH
            )

    loads = [
        pltpu.make_async_copy(source, target, load_sems.at[i])
        for i, (source, target) in enumerate(
            ((state_hbm, state_ref), (depth_hbm, depth_ref), (open_hbm, open_ref))
        )
    ]
    for load in loads:
        load.start()

    def send_to(section, count, src, dst, send_sem, recv_sem):
        for far in range(tiles - 1, tiles - 1 - count, -1):
            pltpu.make_async_remote_copy(
                src_ref=src,
                dst_ref=dst,
                send_sem=send_sem,
                recv_sem=recv_sem,
                device_id=(
                    section,
                    partner(row, far % n_row, n_row),
                    partner(col, far // n_row, n_nest),
                ),
                device_id_type=MESH,
            ).start()

    def send_all(src, dst, send_sem, recv_sem):
        send_to(1 - sec, tiles, src, dst, send_sem, recv_sem)

    def wait_all(whole, sem):
        pltpu.make_async_copy(whole, whole, sem).wait()

    def relays():
        return [
            pltpu.make_async_remote_copy(
                src_ref=src,
                dst_ref=dst,
                send_sem=sems.at[0],
                recv_sem=sems.at[1],
                device_id=(1, row, col),
                device_id_type=MESH,
            )
            for src, dst, sems in (
                (first_out, first_in.at[tile], first_sems),
                (bulk_out, bulk_in.at[row], bulk_sems),
            )
        ]

    @pl.when(is_outer)
    def _():
        for present, device in links:

            @pl.when(present)
            def _():
                pl.semaphore_signal(barrier, inc=1, device_id=device, device_id_type=MESH)

        slots, covers = [], []
        for p in range(NPOS):
            slot, cover = jnp.int32(0), jnp.int32(0)
            for n in range(nests):
                hit = place_ref[n] == tile * NPOS + p
                slot = jnp.where(hit, host_ref[n], slot)
                cover = jnp.where(hit, 1, cover)
            slots.append(slot)
            covers.append(cover)
        for load in loads:
            load.wait()
        for i in range(2):
            free[7 + i] = jnp.where(open_ref[0, i] > 0, depth_ref[0, i], 0.0)
        levels = []
        for band in range(K):
            lo = band * FINE_ROWS
            hi = lo + BAND
            old = [state_ref[0, f, lo:hi] for f in range(3)]
            level = new_level_ring(old[0], old[1], old[2], COURANT)
            flux_e, flux_s = new_fluxes_ring(old[1], old[2], level, free[7, lo:hi], free[8, lo:hi])
            free[0, lo:hi] = level
            free[1, lo:hi] = flux_e
            free[2, lo:hi] = flux_s
        first_out[...] = pack_strips(
            [[ref.at[f] for f in range(3)] for ref in (state_ref.at[0], free)]
        )
        peers = jnp.int32(1)
        for present, _device in links:
            peers = peers + jnp.where(present, 1, 0)
        pl.semaphore_wait(barrier, peers)
        first_copy, bulk_copy = relays()
        first_copy.start()
        for band in range(K):
            lo = band * FINE_ROWS
            hi = lo + BAND
            level, flux_e, flux_s = [free[f, lo:hi] for f in range(3)]
            for i in range(2):
                east_gap = flux_e - pltpu.roll(flux_e, 1, 1)
                free[3 + i, lo:hi] = level - COURANT * (east_gap + flux_s)
                level = level - COURANT * (east_gap + (flux_s - pltpu.roll(flux_s, 1, 0)))
                if i == 0:
                    flux_e, flux_s = new_fluxes_ring(
                        flux_e, flux_s, level, free[7, lo:hi], free[8, lo:hi]
                    )
            free[5, lo:hi] = level
            free[6, lo:hi] = flux_s
        for band in range(K):
            first = band * FINE_ROWS + TOP
            for part, chosen in enumerate((ROWS_EARLY, ROWS_LATE)):
                for i, (f, shift) in enumerate(chosen):
                    at = first + shift
                    bulk_out[3 * band + part, i : i + 1] = free[f, at : at + 1]
            bulk_out[3 * band + 2] = pack_sides(free, band)

        bulk_copy.start()

        def halo(kind, src, dst, device):
            return pltpu.make_async_remote_copy(
                src_ref=src,
                dst_ref=dst,
                send_sem=halo_send.at[kind],
                recv_sem=halo_recv.at[kind],
                device_id=device,
                device_id_type=MESH,
            )

        fields = [state_ref.at[0, f] for f in range(3)] + [free.at[7 + i] for i in range(2)]
        lane = iota((height, width), 1)
        packed = jnp.zeros((height, width), jnp.float32)
        for i, field in enumerate(fields):
            x = field[...]
            ext[i, 0:height, 0:width] = x
            packed = jnp.where((lane >= 8 * i) & (lane < 8 * i + 4), pltpu.roll(x, 8 * i, 1), packed)
            packed = jnp.where(
                (lane >= 8 * i + 4) & (lane < 8 * i + 8), pltpu.roll(x, 8 * i + 8, 1), packed
            )
        side_out[...] = packed
        to_east = halo(0, side_out, west_in, east)
        to_west = halo(1, side_out, east_in, west)
        top, bottom = pl.ds(0, HALO), pl.ds(height - HALO, HALO)
        below, above = pl.ds(height, HALO), pl.ds(height + HALO, HALO)
        to_south = halo(2, ext.at[:, bottom], ext.at[:, above], south)
        to_north = halo(3, ext.at[:, top], ext.at[:, below], north)

        for present, copy in ((has_east, to_east), (has_west, to_west)):

            @pl.when(present)
            def _():
                copy.start()

        for present, buffer in ((has_west, west_in), (has_east, east_in)):

            @pl.when(jnp.logical_not(present))
            def _():
                buffer[...] = jnp.zeros(buffer.shape, jnp.float32)

        for present, where in ((has_south, below), (has_north, above)):

            @pl.when(jnp.logical_not(present))
            def _():
                ext[:, where] = jnp.zeros((len(fields), HALO, 2 * width), jnp.float32)

        rows, lanes = iota((height + 2 * HALO, 2 * width), 0), iota((height + 2 * HALO, 2 * width), 1)

        def allowed(region, present):
            return jnp.logical_not(region) | (jnp.full(rows.shape, present.astype(jnp.int32)) > 0)

        inside = allowed((rows >= height) & (rows < height + HALO), has_south)
        inside = inside & allowed(rows >= height + HALO, has_north)
        inside = inside & allowed((lanes >= width) & (lanes < width + width // 2), has_east)
        inside = inside & allowed(lanes >= width + width // 2, has_west)
        courant_ref[...] = jnp.where(inside, COURANT, 0.0)

        for present, copy in ((has_west, to_east), (has_east, to_west)):

            @pl.when(present)
            def _():
                copy.wait_recv()

        from_west, from_east = west_in[...], east_in[...]
        for i in range(len(fields)):
            ext[i, 0:height, width:] = jnp.where(
                lane < 4,
                pltpu.roll(from_east, (width - 8 * i) % width, 1),
                jnp.where(lane >= width - 4, pltpu.roll(from_west, width - 8 - 8 * i, 1), 0.0),
            )

        for present, copy in ((has_south, to_south), (has_north, to_north)):

            @pl.when(present)
            def _():
                copy.start()

        for present, copy in ((has_north, to_south), (has_south, to_north)):

            @pl.when(present)
            def _():
                copy.wait_recv()

        for present, copy in (
            (has_east, to_east),
            (has_west, to_west),
            (has_south, to_south),
            (has_north, to_north),
        ):

            @pl.when(present)
            def _():
                copy.wait_send()

        def advance():
            surface, eastward, southward = ext[0], ext[1], ext[2]
            level = new_level_ring(surface, eastward, southward, courant_ref[...])
            flux_e, flux_s = new_fluxes_ring(eastward, southward, level, ext[3], ext[4])
            ext[0] = level
            ext[1] = flux_e
            ext[2] = flux_s

        lane, sub = iota((PH, width), 1), iota((PH, width), 0)

        def covered(p):
            return jnp.full((PH, width), covers[p], jnp.int32) > 0

        def merge(parts_of, keep):
            for band in range(K):
                first = band * FINE_ROWS + TOP
                merged = [ext[f, first : first + PH, 0:width] for f in range(3)]
                for j in range(RR - 1):
                    p = band * (RR - 1) + j
                    column = LEFT + j * PW
                    here = covered(p)
                    for f, mask, values in parts_of(p, column):
                        merged[f] = jnp.where(here & mask, values, merged[f])
                for f in range(3):
                    keep(f, first, merged[f])

        def whole_parts(p, column):
            block = ret_in[slots[p]]
            mask = (lane >= column) & (lane < column + PW)
            return [(f, mask, pltpu.roll(block, (column - f * PW) % width, 1)) for f in range(3)]

        def border_parts(p, column):
            device, k = slots[p] // K, lax.rem(slots[p], K)
            line, ends = [
                jnp.broadcast_to(edge_now[device, pl.ds(2 * k + i, 1)], (PH, width)) for i in range(2)
            ]
            items = ends
            for r in range(1, PH):
                items = jnp.where(sub == r, pltpu.roll(ends, width - 16 * r, 1), items)
            inside = (lane >= column) & (lane < column + PW)
            out = []
            for f in range(3):
                out.append((f, inside & (sub == 0), pltpu.roll(line, (column - f * PW) % width, 1)))
            out.append((2, inside & (sub == PH - 1), pltpu.roll(line, (column - 3 * PW) % width, 1)))
            for i, (f, c) in enumerate(BORDER):
                at = column + c
                out.append((f, lane == at, pltpu.roll(items, (at - i) % width, 1)))
            return out

        def keep_inside(f, first, x):
            ext[f, first : first + PH, 0:width] = x

        def keep_result(f, first, x):
            out_ref[0, f, first : first + PH] = x

        @pl.loop(0, STEPS - 1)
        def _(s):
            advance()
            lines = pl.ds(0, 2 * K)
            wait_all(edge_in.at[s, :, lines], ret_recv.at[s])
            edge_now[:, 0 : 2 * K] = edge_in[s, :, 0 : 2 * K]
            merge(border_parts, keep_inside)

        advance()
        for f in range(3):
            out_ref[0, f] = ext[f, 0:height, 0:width]
        for copy in relays():
            copy.wait_send()
        wait_all(ret_in, ret_recv.at[STEPS - 1])
        merge(whole_parts, keep_result)

    @pl.when(jnp.logical_not(is_outer))
    def _():
        lane, sub = iota((PH, width), 1), iota((PH, width), 0)
        groups = FINE_ROWS // 8

        def find(keys, wanted, values):
            out = jnp.int32(0)
            for n in range(nests):
                out = jnp.where(keys[n] == wanted, values[n], out)
            return out

        def present(keys, wanted):
            out = jnp.int32(0)
            for n in range(nests):
                out = jnp.where(keys[n] == wanted, 1, out)
            return out

        def owner(slot):
            return slot // (K * n_nest), lax.rem(slot // K, n_nest), lax.rem(slot, K)

        spots, low_wants, high_wants, near_wants = [], [], [], []
        for i in range(n_row):
            at_row = lax.rem(row + i, n_row)
            for k in range(K):
                spot = find(host_ref, (at_row * n_nest + col) * K + k, place_ref)
                if i == 0:
                    spots.append(spot)
                low_wants.append(owner(find(place_ref, spot + 1, host_ref)))
        for i in range(n_nest):
            at_col = lax.rem(col + i, n_nest)
            for k in range(K):
                spot = spots[k] if i == 0 else find(host_ref, (row * n_nest + at_col) * K + k, place_ref)
                high_wants.append(owner(find(place_ref, spot - 1, host_ref)))
                near_wants.append(
                    (
                        spot // (NPOS * n_nest),
                        lax.rem(spot // NPOS, n_nest),
                        lax.rem(spot, NPOS) // (RR - 1),
                        lax.rem(spot, RR - 1),
                    )
                )
        lives = [present(host_ref, tile * K + k) for k in range(K)]
        homes = [spot // NPOS for spot in spots]
        bands = [lax.rem(spot, NPOS) // (RR - 1) for spot in spots]
        columns = [lax.rem(spot, RR - 1) for spot in spots]
        near = []
        for k in range(K):
            near.append(
                [
                    jnp.where(
                        (columns[k] + side >= 0) & (columns[k] + side < RR - 1),
                        present(place_ref, spots[k] + side),
                        0,
                    )
                    for side in (-1, 1)
                ]
            )

        gather_from = iota((3 * width, 2 * width), 0)
        gather_to = iota((3 * width, 2 * width), 1)
        field, lane_in = gather_from // width, lax.rem(gather_from, width)
        weight = jnp.where(
            field == 0,
            1.0 / (RR * RR),
            jnp.where((field == 2) | (lax.rem(lane_in, RR) == RR - 1), 1.0 / RR, 0.0),
        )
        gather = jnp.where(gather_to == field * PW + lane_in // RR, weight, 0.0)
        for i, (f, c) in enumerate(BORDER):
            gather = gather + jnp.where(
                (gather_to >= width)
                & (lax.rem(gather_to, 16) == i)
                & (field == f)
                & (lane_in // RR == c),
                weight,
                0.0,
            )
        half = width // K
        fine = iota((width, 2 * width), 1)
        beside = lax.rem(fine, half)
        coarse_lane = jnp.where(
            fine < width,
            NEAR + fine // RR,
            beside // RR + jnp.where(beside < half // 2, NEAR + PW, NEAR - half // RR),
        )
        widen = (iota((width, 2 * width), 0) == coarse_lane).astype(jnp.float32)
        gather, widen = [m.astype(jnp.bfloat16) for m in (gather, widen)]
        own_lanes = (lane >= NEAR) & (lane < NEAR + PW)
        of_first = (lane < half // 2) | (lane >= width - half // 2)

        def by_column(column, choices):
            out = choices[0]
            for j in range(1, len(choices)):
                out = jnp.where(jnp.full(out.shape, column, jnp.int32) == j, choices[j], out)
            return out

        def centred(x, k):
            return by_column(
                columns[k], [pltpu.roll(x, (NEAR - LEFT - j * PW) % width, 1) for j in range(RR - 1)]
            )

        span = 8 * len(SIDE_FIELDS)

        def around(want):
            early, late, sides = [bulk_in[want[0], 3 * want[2] + n] for n in range(3)]
            choices = []
            for j in range(RR - 1):
                first = LEFT + j * PW - 4
                x = jnp.where(
                    lane < 2 * span,
                    pltpu.roll(late, (span - first) % width, 1),
                    pltpu.roll(sides, (2 * span - span * j) % width, 1),
                )
                choices.append(jnp.where(lane < span, pltpu.roll(early, (-first) % width, 1), x))
            return [by_column(want[3], choices)]

        def pick_lane(block, index):
            return jnp.sum(jnp.where(lane == index, block, 0.0), axis=1, keepdims=True)

        def pick_row(block, index):
            return jnp.sum(jnp.where(sub == index, block, 0.0), axis=0, keepdims=True)

        def four(west_0, east_1, west_1, east_0):
            out = jnp.where(lane < half // 2, west_0, east_1)
            out = jnp.where(lane >= half, west_1, out)
            return jnp.where(lane >= width - half // 2, east_0, out)

        def keep_rows(t, lines):
            for k in range(K):
                ghost_rows[t, k, 0:2] = lines[2 * k : 2 * k + 2, 0:width]
            far = lines[:, width:]
            both = jnp.where(sub < 1, far[0:1], far[1:2])
            other = jnp.where(sub < 1, far[2:3], far[3:4])
            ghost_rows[t, K] = jnp.where(of_first, both, other)

        for load in loads:
            load.wait()
        for i in range(2):
            own_wet[i] = jnp.where(open_ref[0, i] > 0, depth_ref[0, i], 0.0)
        sources = [state_ref.at[0, f] for f in range(3)] + [own_wet.at[i] for i in range(2)]
        sources.append(state_ref.at[0, 1])
        for k in range(K):
            for side in (1, 0):
                packed = [jnp.zeros((PH, width), jnp.float32) for _ in range(STRIP_TILES)]
                for f, source in enumerate(sources):
                    if f == 5 and side == 0:
                        continue
                    first = 0 if side == 0 else width - STRIP * (2 if f == 5 else 1)
                    for g in range(groups):
                        at = (f % 2) * groups * STRIP + g * STRIP
                        piece = source[k * FINE_ROWS + 8 * g : k * FINE_ROWS + 8 * g + 8]
                        packed[f // 2] = jnp.where(
                            (lane >= at) & (lane < at + STRIP),
                            pltpu.roll(piece, (at - first) % width, 1),
                            packed[f // 2],
                        )
                for i, x in enumerate(packed):
                    if side == 0:
                        low_in[col, k, i] = x
                    else:
                        high_in[row, k, i] = x

        def to_peer(src, dst, sems, first_sem, device):
            pltpu.make_async_remote_copy(
                src_ref=src,
                dst_ref=dst,
                send_sem=sems.at[first_sem],
                recv_sem=sems.at[first_sem + 1],
                device_id=device,
                device_id_type=MESH,
            ).start()

        def in_plane(i):
            return sec, lax.rem(row + i, n_row), col

        def along_nest(i):
            return sec, row, lax.rem(col + i, n_nest)

        pl.semaphore_wait(barrier, tiles - 1)

        @pl.loop(1, n_row)
        def _(i):
            to_peer(high_in.at[row], high_in.at[row], high_sems, 0, in_plane(n_row - i))

        @pl.loop(1, n_nest)
        def _(i):
            to_peer(low_in.at[col], low_in.at[col], low_sems, 0, along_nest(n_nest - i))

        first_copy, bulk_copy = relays()
        first_copy.wait_recv()
        send_to(1, tiles - 1, first_in.at[tile], first_in.at[tile], first_sems.at[2], first_sems.at[3])
        bulk_copy.wait_recv()

        @pl.loop(1, n_row)
        def _(i):
            to_peer(bulk_in.at[row], bulk_in.at[row], bulk_sems, 2, in_plane(n_row - i))

        def pass_on(count, me, wants, pick, out, got, sems, device):
            for i in range(count):
                for k in range(K):
                    for n, x in enumerate(pick(wants[i * K + k])):
                        if i == 0:
                            got[me, k, n] = x
                        else:
                            out[i - 1, k, n] = x
                if i > 0:
                    to_peer(out.at[i - 1], got.at[me], sems[0], sems[1], device(i))

        wait_all(high_in.at[pl.ds(0, n_row - 1)], high_sems.at[1])
        pass_on(
            n_nest,
            col,
            high_wants,
            lambda w: [high_in[w[0], w[2], n] for n in range(STRIP_TILES)],
            high_out,
            high_got,
            (high_sems, 2),
            along_nest,
        )
        wait_all(low_in.at[pl.ds(0, n_nest - 1)], low_sems.at[1])
        pass_on(
            n_row,
            row,
            low_wants,
            lambda w: [low_in[w[1], w[2], n] for n in range(STRIP_TILES)],
            low_out,
            low_got,
            (low_sems, 2),
            in_plane,
        )
        wait_all(bulk_in.at[pl.ds(0, n_row - 1)], bulk_sems.at[3])
        pass_on(
            n_nest,
            col,
            near_wants,
            around,
            near_out,
            near_got,
            (near_sems, 0),
            along_nest,
        )

        wait_all(first_in.at[pl.ds(0, tiles - 1)], first_sems.at[3])
        blocks = [first_in[homes[k]] for k in range(K)]
        middles = [centred(block, k) for k, block in enumerate(blocks)]
        for t in range(2):
            lines = jnp.zeros((PH, width), jnp.float32)
            ends = []
            for k in range(K):
                at = t * (LEFT + (RR - 1) * PW) + bands[k] * (2 * (RR - 1)) + columns[k]
                to_east = at + RR - 1
                cols = jnp.where(
                    lane < width // 2, pick_lane(blocks[k], at), pick_lane(blocks[k], to_east)
                )
                ghost_cols[t, k] = grow_rows(cols)
                ends.append((pick_lane(blocks[k], at + 1), pick_lane(blocks[k], to_east - 1)))
                for i in range(2):
                    line = pick_row(middles[k], 2 * (t * K + bands[k]) + i)
                    lines = jnp.where(sub == 2 * k + i, line, lines)
            (west_0, east_0), (west_1, east_1) = ends
            ghost_cols[t, K] = grow_rows(four(west_0, east_1, west_1, east_0))
            keep_rows(t, dot_by(lines, widen))

        fine_lane = iota((FINE_ROWS, width), 1)
        own_ends = (fine_lane == 0, fine_lane == width - 1)
        slab_ends = (lax.rem(fine_lane, half) == 0, lax.rem(fine_lane, half) == half - 1)
        slots = [pl.ds(k * FINE_ROWS, FINE_ROWS) for k in range(K)]

        def load_own(source):
            return [[source[f, slot] for f in range(3)] for slot in slots]

        def substeps(which, states):
            wets = [
                [slab[3 + i] if k == K else own_wet[i, slots[k]] for i in range(2)] for k in which
            ]
            old_cols, new_cols = [[ghost_cols[t, k] for k in which] for t in range(2)]
            old_rows, new_rows = [[ghost_rows[t, k] for k in which] for t in range(2)]
            for m in range(1, RR + 1):
                for n, k in enumerate(which):
                    cols = old_cols[n] + (m / RR) * (new_cols[n] - old_cols[n])
                    rows = old_rows[n] + (m / RR) * (new_rows[n] - old_rows[n])
                    ends = slab_ends if k == K else own_ends
                    states[n] = slab_step(states[n], wets[n], cols, rows, *ends)
            return states

        def averages(states):
            sums = dot_by(
                jnp.concatenate(
                    [
                        jnp.concatenate([row_sums(x[0]), row_sums(x[1]), row_picks(x[2])], axis=1)
                        for x in states
                    ],
                    axis=0,
                ),
                gather,
            )
            sums = [sums[n * PH : (n + 1) * PH] for n in range(len(states))]
            return [x[:, 0:width] for x in sums], [x[:, width:] for x in sums]

        def send_border(s, coarse, border):
            for k in range(K):
                last = pltpu.roll(coarse[k], PW, 1)
                edge_out[s, 2 * k : 2 * k + 1] = jnp.where(
                    lane[0:1] < 3 * PW, coarse[k][0:1], last[PH - 1 : PH]
                )
                edge_out[s, 2 * k + 1 : 2 * k + 2] = jnp.sum(
                    jnp.where(lane // 16 == sub, border[k], 0.0), axis=0, keepdims=True
                )
            lines = pl.ds(0, 2 * K)
            send_all(edge_out.at[s, lines], edge_in.at[s, tile, lines], ret_send.at[s], ret_recv.at[s])

        def store_own(states):
            for k in range(K):
                for f in range(3):
                    st[f, slots[k]] = states[k][f]

        def next_ghosts(coarse):
            for k in range(K + 1):
                ghost_cols[0, k] = ghost_cols[1, k]
                ghost_rows[0, k] = ghost_rows[1, k]
            lines = jnp.zeros((PH, width), jnp.float32)
            ends = []
            for k in range(K):
                on_left, on_right = [
                    jnp.full((PH, width), cover, jnp.int32) > 0 for cover in near[k]
                ]
                on_left = on_left & (lane >= NEAR - 4) & (lane < NEAR)
                on_right = on_right & (lane >= NEAR + PW) & (lane < NEAR + PW + 4)
                boundary = k * half // RR
                state = []
                for f in range(3):
                    x = patch[k, f, 0:PH]
                    x = jnp.where(own_lanes, pltpu.roll(coarse[k], (NEAR - f * PW) % width, 1), x)
                    low = f * PW + (boundary - 4) % PW
                    x = jnp.where(on_left, pltpu.roll(coarse[K], (NEAR - 4 - low) % width, 1), x)
                    high = f * PW + boundary
                    x = jnp.where(on_right, pltpu.roll(coarse[K], (NEAR + PW - high) % width, 1), x)
                    state.append(jnp.concatenate([x, patch[k, f, PH : 2 * PH]], axis=0))
                level = new_level_ring(state[0], state[1], state[2], COURANT)
                flux_e, flux_s = new_fluxes_ring(state[1], state[2], level, wet[k, 0], wet[k, 1])
                for f, x in enumerate((level, flux_e, flux_s)):
                    patch[k, f] = x
                level8, east8 = level[0:PH], flux_e[0:PH]
                cols = jnp.where(
                    lane < width // 2,
                    pltpu.roll(east8, width - NEAR + 1, 1),
                    pltpu.roll(level8, width - 1 - NEAR - PW, 1),
                )
                ghost_cols[1, k] = grow_rows(cols)
                at = k * half
                ends.append(
                    (
                        pltpu.roll(east8, (at - (NEAR + PW - 1)) % width, 1),
                        pltpu.roll(level8, (at - 1 - NEAR) % width, 1),
                    )
                )
                lines = jnp.where(sub == 2 * k, flux_s[2 * PH - 1 : 2 * PH], lines)
                lines = jnp.where(sub == 2 * k + 1, level[PH : PH + 1], lines)
            (west_0, east_0), (west_1, east_1) = ends
            ghost_cols[1, K] = grow_rows(four(west_0, east_1, west_1, east_0))
            keep_rows(1, dot_by(lines, widen))

        states = substeps(range(K), load_own(state_ref.at[0]))
        store_own(states)
        coarse, border = averages(states)


        send_border(0, coarse, border)

        wait_all(near_got.at[pl.ds(0, n_nest - 1)], near_sems.at[1])
        for k in range(K):
            got = near_got[near_wants[k][1], k, 0]
            early, late, sides = [
                pltpu.roll(got, shift % width, 1) for shift in (NEAR - 4, NEAR - 4 - span, -2 * span)
            ]

            def tile_of(block, spots):
                out = jnp.zeros((PH, width), jnp.float32)
                for target, source in spots:
                    out = jnp.where(sub == target, block[source : source + 1], out)
                return out

            outside = [
                tile_of(early, ((0, 0), (1, 1), (7, 5))),
                tile_of(early, ((0, 2), (7, 6))),
                tile_of(early, ((0, 3), (6, 4), (7, 7))),
                tile_of(late, ((0, 3), (7, 4))),
                tile_of(late, ((0, 5), (6, 6), (7, 7))),
            ]
            for i in range(5):
                beside = jnp.where(
                    lane < NEAR + PW // 2,
                    pltpu.roll(sides, (NEAR - 4 - 8 * i) % width, 1),
                    pltpu.roll(sides, (NEAR + PW - 5 - 8 * i) % width, 1),
                )
                target = patch.at[k, i] if i < 3 else wet.at[k, i - 3]
                target[0:PH] = beside
                target[PH : 2 * PH] = outside[i]
            later[k, 0] = tile_of(late, ((1, 0), (6, 1)))
            later[k, 1] = tile_of(late, ((5, 2), (6, 2)))

        wait_all(high_got.at[pl.ds(0, n_nest - 1)], high_sems.at[3])
        wait_all(low_got.at[pl.ds(0, n_row - 1)], low_sems.at[3])
        sets = [
            [
                [high_got[high_wants[k][1], k, n] for n in range(STRIP_TILES)],
                [low_got[low_wants[k][0], k, n] for n in range(STRIP_TILES)],
            ]
            for k in range(K)
        ]
        fits = []
        for k in range(K):
            start = k * half
            on_left, on_right = [jnp.full((PH, width), cover, jnp.int32) > 0 for cover in near[k]]
            before = (start - STRIP) % width
            fits.append(
                (
                    on_left & (lane >= before) & (lane < before + STRIP),
                    on_right & (lane >= start) & (lane < start + STRIP),
                    on_left & (lane == before - 1),
                )
            )
        for f in range(5):
            for g in range(groups):
                out = jnp.zeros((PH, width), jnp.float32)
                at = (f % 2) * groups * STRIP + g * STRIP
                for k in range(K):
                    start = k * half
                    before = (start - STRIP) % width
                    left, right = [sets[k][side][f // 2] for side in range(2)]
                    out = jnp.where(fits[k][0], pltpu.roll(left, (before - at) % width, 1), out)
                    out = jnp.where(fits[k][1], pltpu.roll(right, (start - at) % width, 1), out)
                    if f == 1:
                        extra = groups * STRIP + (g + 1) * STRIP - 1
                        out = jnp.where(
                            fits[k][2],
                            pltpu.roll(sets[k][0][2], (before - 1 - extra) % width, 1),
                            out,
                        )
                slab[f, 8 * g : 8 * g + 8] = out

        def load_slab():
            return [slab[f] for f in range(3)]

        def store_slab(state):
            for f in range(3):
                slab[f] = state[f]

        aside = substeps([K], [load_slab()])
        store_slab(aside[0])
        next_ghosts(coarse + averages(aside)[0])

        @pl.loop(1, STEPS - 1)
        def _(s):
            states = substeps(range(K + 1), load_own(st) + [load_slab()])
            coarse, border = averages(states)
            send_border(s, coarse, border)
            store_own(states)
            store_slab(states[K])

            @pl.when(s == 1)
            def _():
                given = (sub == 1) | (sub == 5) | (sub == 6)
                for k in range(K):
                    for f, value in enumerate((later[k, 0], 0.0, later[k, 1])):
                        patch[k, f, PH : 2 * PH] = jnp.where(given, value, patch[k, f, PH : 2 * PH])

            next_ghosts(coarse)

        states = substeps(range(K), load_own(st))
        coarse, _ = averages(states)
        for k in range(K):
            ret_out[k] = coarse[k]
        send_all(ret_out, ret_in.at[pl.ds(tile * K, K)], ret_send.at[STEPS - 1], ret_recv.at[STEPS - 1])
        for k in range(K):
            live = jnp.full((FINE_ROWS, width), lives[k], jnp.int32) > 0
            for f in range(3):
                out_ref[0, f, slots[k]] = jnp.where(live, states[k][f], state_ref[0, f, slots[k]])

        wait_all(first_in.at[pl.ds(0, tiles - 1)], first_sems.at[2])
        wait_all(bulk_in.at[pl.ds(0, n_row - 1)], bulk_sems.at[2])
        wait_all(low_in.at[pl.ds(0, n_nest - 1)], low_sems.at[0])
        wait_all(low_got.at[pl.ds(0, n_row - 1)], low_sems.at[2])
        wait_all(high_in.at[pl.ds(0, n_row - 1)], high_sems.at[0])
        wait_all(high_got.at[pl.ds(0, n_nest - 1)], high_sems.at[2])
        wait_all(near_got.at[pl.ds(0, n_nest - 1)], near_sems.at[0])
        for s in range(STEPS - 1):
            wait_all(edge_in.at[s, :, pl.ds(0, 2 * K)], ret_send.at[s])
        wait_all(ret_in, ret_send.at[STEPS - 1])


def on_device(n_row, n_nest, ocean_state, face_depth, face_open, nest_place, nest_host):
    tiles = n_row * n_nest
    height, width = ocean_state.shape[2:]
    f32 = jnp.float32
    vmem = pl.BlockSpec(memory_space=pltpu.VMEM)
    hbm = pl.BlockSpec(memory_space=pl.ANY)
    smem = pl.BlockSpec(memory_space=pltpu.SMEM)
    dma = pltpu.SemaphoreType.DMA
    return pl.pallas_call(
        functools.partial(kernel, n_row, n_nest),
        out_shape=pltpu.VMEM(ocean_state.shape, f32),
        in_specs=[smem, smem, hbm, hbm, hbm],
        out_specs=vmem,
        scratch_shapes=[
            pltpu.VMEM(ocean_state.shape, f32),
            pltpu.VMEM(face_depth.shape, f32),
            pltpu.VMEM(face_open.shape, jnp.int32),
            dma((3,)),
            pltpu.VMEM((3, height, width), f32),
            pltpu.VMEM((9, height, width), f32),
            pltpu.VMEM((PH, width), f32),
            pltpu.VMEM((tiles, PH, width), f32),
            pltpu.VMEM((3 * K, PH, width), f32),
            pltpu.VMEM((n_row, 3 * K, PH, width), f32),
            pltpu.VMEM((n_nest, K, STRIP_TILES, PH, width), f32),
            pltpu.VMEM((n_row, K, STRIP_TILES, PH, width), f32),
            pltpu.VMEM((n_row, K, STRIP_TILES, PH, width), f32),
            pltpu.VMEM((n_row, K, STRIP_TILES, PH, width), f32),
            pltpu.VMEM((n_nest, K, STRIP_TILES, PH, width), f32),
            pltpu.VMEM((n_nest, K, STRIP_TILES, PH, width), f32),
            pltpu.VMEM((n_nest, K, 1, PH, width), f32),
            pltpu.VMEM((n_nest, K, 1, PH, width), f32),
            pltpu.VMEM((STEPS - 1, PH, width), f32),
            pltpu.VMEM((STEPS - 1, tiles, PH, width), f32),
            pltpu.VMEM((K, PH, width), f32),
            pltpu.VMEM((tiles * K, PH, width), f32),
            pltpu.VMEM((height, width), f32),
            pltpu.VMEM((height, width), f32),
            pltpu.VMEM((height, width), f32),
            pltpu.VMEM((5, height + 2 * HALO, 2 * width), f32),
            pltpu.VMEM((height + 2 * HALO, 2 * width), f32),
            pltpu.VMEM((2, K + 1, FINE_ROWS, width), f32),
            pltpu.VMEM((2, K + 1, PH, width), f32),
            pltpu.VMEM((K, 3, 2 * PH, width), f32),
            pltpu.VMEM((K, 2, 2 * PH, width), f32),
            pltpu.VMEM((K, 2, PH, width), f32),
            pltpu.VMEM((5, FINE_ROWS, width), f32),
            pltpu.VMEM((2, height, width), f32),
            pltpu.VMEM((tiles, PH, width), f32),
            dma((4,)),
            dma((4,)),
            dma((4,)),
            dma((4,)),
            dma((2,)),
            dma((STEPS,)),
            dma((STEPS,)),
            dma((4,)),
            dma((4,)),
        ],
        compiler_params=pltpu.CompilerParams(collective_id=0, has_side_effects=True),
    )(nest_place, nest_host, ocean_state, face_depth, face_open)


def solution(mesh):
    field = P("sec", None, "row", "nest")
    return jax.shard_map(
        functools.partial(on_device, mesh.shape["row"], mesh.shape["nest"]),
        mesh=mesh,
        in_specs=(field, field, field, P(), P()),
        out_specs=field,
        check_vma=False,
    )
```

```python
import functools

import jax
import jax.numpy as jnp
from jax import lax
from jax.experimental import pallas as pl
from jax.experimental.pallas import tpu as pltpu
from jax.sharding import PartitionSpec as P

PH = 8
PW = 32
RR = 4
K = 2
STEPS = 4
NPOS = K * (RR - 1)
COURANT = 0.3
MESH = pl.DeviceIdType.MESH
FINE_ROWS = RR * PH
TOP = (RR - 1) * PH // 2
LEFT = PW // 2
NEAR = PW
BORDER = ((0, 0), (1, 0), (2, 0), (1, PW - 1))
STRIP = 16
STRIP_TILES = 3
BAND = (TOP + PH + STEPS + 7) // 8 * 8
HALO = 8
ROWS_EARLY = ((0, PH), (3, PH + 1), (1, PH), (2, PH), (2, -2), (0, -1), (1, -1), (2, -1))
ROWS_LATE = ((4, PH + 1), (5, -2), (6, -2), (7, PH), (7, -1), (8, PH), (8, -2), (8, -1))
SIDE_FIELDS = (0, 1, 2, 7, 8)


def iota(shape, dim):
    return lax.broadcasted_iota(jnp.int32, shape, dim)


def slab_step(fields, wet, cols, rows, west_at, east_at):
    surface, eastward, southward = fields
    height, width = surface.shape
    sub = iota(surface.shape, 0)
    east_behind = jnp.where(west_at, cols, pltpu.roll(eastward, 1, 1))
    south_behind = jnp.where(sub == 0, rows[0:1], pltpu.roll(southward, 1, 0))
    level = surface - COURANT * ((eastward - east_behind) + (southward - south_behind))
    level_east = jnp.where(east_at, cols, pltpu.roll(level, width - 1, 1))
    level_south = jnp.where(sub == height - 1, rows[1:2], pltpu.roll(level, height - 1, 0))
    east = eastward - COURANT * (wet[0] + 0.5 * (level + level_east)) * (level_east - level)
    south = southward - COURANT * (wet[1] + 0.5 * (level + level_south)) * (level_south - level)
    return [level, jnp.where(wet[0] > 0, east, 0.0), jnp.where(wet[1] > 0, south, 0.0)]


def new_level_ring(surface, eastward, southward, courant):
    east_gap = eastward - pltpu.roll(eastward, 1, 1)
    south_gap = southward - pltpu.roll(southward, 1, 0)
    return surface - courant * (east_gap + south_gap)


def new_fluxes_ring(eastward, southward, level, wet_east, wet_south):
    height, width = level.shape
    level_east = pltpu.roll(level, width - 1, 1)
    level_south = pltpu.roll(level, height - 1, 0)
    east = eastward - COURANT * (wet_east + 0.5 * (level + level_east)) * (level_east - level)
    south = southward - COURANT * (wet_south + 0.5 * (level + level_south)) * (level_south - level)
    return jnp.where(wet_east > 0, east, 0.0), jnp.where(wet_south > 0, south, 0.0)


def parts(x):
    high = x.astype(jnp.bfloat16).astype(jnp.float32)
    rest = x - high
    middle = rest.astype(jnp.bfloat16).astype(jnp.float32)
    return high, middle, rest - middle


def dot_by(x, chosen):
    rows = x.shape[0]
    stacked = jnp.concatenate(parts(x), axis=0).astype(jnp.bfloat16)
    y = jnp.dot(stacked, chosen, preferred_element_type=jnp.float32)
    return y[:rows] + (y[rows : 2 * rows] + y[2 * rows :])


def pack_strips(times):
    width = times[0][0].shape[-1]
    lane, sub = iota((PH, width), 1), iota((PH, width), 0)
    block = jnp.zeros((PH, width), jnp.float32)
    span = (RR - 1) * PW
    inner = (lane >= LEFT) & (lane < LEFT + span)
    for t, fields in enumerate(times):
        surface, eastward, southward = fields
        for band in range(K):
            first = band * FINE_ROWS + TOP
            east8 = eastward[first : first + PH, :]
            level8 = surface[first : first + PH, :]
            for j in range(RR - 1):
                column = LEFT + j * PW
                west_lane = t * (LEFT + span) + band * 2 * (RR - 1) + j
                east_lane = west_lane + RR - 1
                block = jnp.where(
                    lane == west_lane, pltpu.roll(east8, (west_lane - column + 1) % width, 1), block
                )
                block = jnp.where(
                    lane == east_lane, pltpu.roll(level8, (east_lane - column - PW) % width, 1), block
                )
            row = (t * K + band) * 2
            block = jnp.where(inner & (sub == row), southward[first - 1 : first, :], block)
            block = jnp.where(inner & (sub == row + 1), surface[first + PH : first + PH + 1, :], block)
    return block


def pack_sides(free, band):
    width = free.shape[-1]
    lane = iota((PH, width), 1)
    block = jnp.zeros((PH, width), jnp.float32)
    first = band * FINE_ROWS + TOP
    for i, f in enumerate(SIDE_FIELDS):
        values = free[f, first : first + PH, :]
        for j in range(RR - 1):
            column = LEFT + j * PW
            target = j * 8 * len(SIDE_FIELDS) + 8 * i
            for side, source in ((0, column - 4), (4, column + PW - 1)):
                at = target + side
                block = jnp.where(
                    (lane >= at) & (lane < at + 4), pltpu.roll(values, (at - source) % width, 1), block
                )
    return block


def row_sums(x):
    width = x.shape[1]
    sub = iota((8, width), 0)
    out = jnp.zeros((8, width), jnp.float32)
    for v in range(x.shape[0] // 8):
        piece = x[8 * v : 8 * v + 8]
        piece = piece + pltpu.roll(piece, 1, 0)
        piece = piece + pltpu.roll(piece, 2, 0)
        out = jnp.where(sub == 2 * v, piece[3:4], out)
        out = jnp.where(sub == 2 * v + 1, piece[7:8], out)
    return out


def row_picks(x):
    width = x.shape[1]
    sub = iota((8, width), 0)
    out = jnp.zeros((8, width), jnp.float32)
    for v in range(x.shape[0] // 8):
        out = jnp.where(sub == 2 * v, x[8 * v + 3 : 8 * v + 4], out)
        out = jnp.where(sub == 2 * v + 1, x[8 * v + 7 : 8 * v + 8], out)
    return out


def grow_rows(x):
    sub = iota(x.shape, 0)
    return jnp.concatenate(
        [jnp.where(sub < 4, x[2 * v : 2 * v + 1], x[2 * v + 1 : 2 * v + 2]) for v in range(RR)], axis=0
    )


def partner(index, step, count):
    if count & (count - 1) == 0:
        return index ^ step
    return lax.rem(index + step, count)


def kernel(
    n_row,
    n_nest,
    place_ref,
    host_ref,
    state_hbm,
    depth_hbm,
    open_hbm,
    out_ref,
    state_ref,
    depth_ref,
    open_ref,
    load_sems,
    st,
    free,
    first_out,
    first_in,
    bulk_out,
    bulk_in,
    low_in,
    low_out,
    low_got,
    high_in,
    high_out,
    high_got,
    near_out,
    near_got,
    edge_out,
    edge_in,
    ret_out,
    ret_in,
    side_out,
    west_in,
    east_in,
    ext,
    courant_ref,
    ghost_cols,
    ghost_rows,
    patch,
    wet,
    later,
    slab,
    own_wet,
    edge_now,
    first_sems,
    bulk_sems,
    low_sems,
    high_sems,
    near_sems,
    ret_send,
    ret_recv,
    halo_send,
    halo_recv,
):
    tiles = n_row * n_nest
    nests = place_ref.shape[0]
    sec, row, col = lax.axis_index("sec"), lax.axis_index("row"), lax.axis_index("nest")
    tile = row * n_nest + col
    is_outer = sec == 0
    has_west, has_east = col > 0, col < n_nest - 1
    has_north, has_south = row > 0, row < n_row - 1
    west, east = (sec, row, col - 1), (sec, row, col + 1)
    north, south = (sec, row - 1, col), (sec, row + 1, col)
    links = ((has_west, west), (has_east, east), (has_north, north), (has_south, south))
    height, width = state_ref.shape[2], state_ref.shape[3]

    barrier = pltpu.get_barrier_semaphore()

    @pl.when(jnp.logical_not(is_outer))
    def _():
        pl.semaphore_signal(barrier, inc=1, device_id=(0, row, col), device_id_type=MESH)

        @pl.loop(0, tiles - 1)
        def _(i):
            t = lax.rem(tile + i + 1, tiles)
            pl.semaphore_signal(
                barrier, inc=1, device_id=(sec, t // n_nest, lax.rem(t, n_nest)), device_id_type=MESH
            )

    loads = [
        pltpu.make_async_copy(source, target, load_sems.at[i])
        for i, (source, target) in enumerate(
            ((state_hbm, state_ref), (depth_hbm, depth_ref), (open_hbm, open_ref))
        )
    ]
    for load in loads:
        load.start()

    def send_to(section, count, src, dst, send_sem, recv_sem):
        for far in range(tiles - 1, tiles - 1 - count, -1):
            pltpu.make_async_remote_copy(
                src_ref=src,
                dst_ref=dst,
                send_sem=send_sem,
                recv_sem=recv_sem,
                device_id=(
                    section,
                    partner(row, far % n_row, n_row),
                    partner(col, far // n_row, n_nest),
                ),
                device_id_type=MESH,
            ).start()

    def send_all(src, dst, send_sem, recv_sem):
        send_to(1 - sec, tiles, src, dst, send_sem, recv_sem)

    def wait_all(whole, sem):
        pltpu.make_async_copy(whole, whole, sem).wait()

    def relays():
        return [
            pltpu.make_async_remote_copy(
                src_ref=src,
                dst_ref=dst,
                send_sem=sems.at[0],
                recv_sem=sems.at[1],
                device_id=(1, row, col),
                device_id_type=MESH,
            )
            for src, dst, sems in (
                (first_out, first_in.at[tile], first_sems),
                (bulk_out, bulk_in.at[row], bulk_sems),
            )
        ]

    @pl.when(is_outer)
    def _():
        for present, device in links:

            @pl.when(present)
            def _():
                pl.semaphore_signal(barrier, inc=1, device_id=device, device_id_type=MESH)

        slots, covers = [], []
        for p in range(NPOS):
            slot, cover = jnp.int32(0), jnp.int32(0)
            for n in range(nests):
                hit = place_ref[n] == tile * NPOS + p
                slot = jnp.where(hit, host_ref[n], slot)
                cover = jnp.where(hit, 1, cover)
            slots.append(slot)
            covers.append(cover)
        for load in loads:
            load.wait()
        for i in range(2):
            free[7 + i] = jnp.where(open_ref[0, i] > 0, depth_ref[0, i], 0.0)
        levels = []
        for band in range(K):
            lo = band * FINE_ROWS
            hi = lo + BAND
            old = [state_ref[0, f, lo:hi] for f in range(3)]
            level = new_level_ring(old[0], old[1], old[2], COURANT)
            flux_e, flux_s = new_fluxes_ring(old[1], old[2], level, free[7, lo:hi], free[8, lo:hi])
            free[0, lo:hi] = level
            free[1, lo:hi] = flux_e
            free[2, lo:hi] = flux_s
        first_out[...] = pack_strips(
            [[ref.at[f] for f in range(3)] for ref in (state_ref.at[0], free)]
        )
        peers = jnp.int32(1)
        for present, _device in links:
            peers = peers + jnp.where(present, 1, 0)
        pl.semaphore_wait(barrier, peers)
        first_copy, bulk_copy = relays()
        first_copy.start()
        for band in range(K):
            lo = band * FINE_ROWS
            hi = lo + BAND
            level, flux_e, flux_s = [free[f, lo:hi] for f in range(3)]
            for i in range(2):
                east_gap = flux_e - pltpu.roll(flux_e, 1, 1)
                free[3 + i, lo:hi] = level - COURANT * (east_gap + flux_s)
                level = level - COURANT * (east_gap + (flux_s - pltpu.roll(flux_s, 1, 0)))
                if i == 0:
                    flux_e, flux_s = new_fluxes_ring(
                        flux_e, flux_s, level, free[7, lo:hi], free[8, lo:hi]
                    )
            free[5, lo:hi] = level
            free[6, lo:hi] = flux_s
        for band in range(K):
            first = band * FINE_ROWS + TOP
            for part, chosen in enumerate((ROWS_EARLY, ROWS_LATE)):
                for i, (f, shift) in enumerate(chosen):
                    at = first + shift
                    bulk_out[3 * band + part, i : i + 1] = free[f, at : at + 1]
            bulk_out[3 * band + 2] = pack_sides(free, band)

        bulk_copy.start()

        def halo(kind, src, dst, device):
            return pltpu.make_async_remote_copy(
                src_ref=src,
                dst_ref=dst,
                send_sem=halo_send.at[kind],
                recv_sem=halo_recv.at[kind],
                device_id=device,
                device_id_type=MESH,
            )

        fields = [state_ref.at[0, f] for f in range(3)] + [free.at[7 + i] for i in range(2)]
        lane = iota((height, width), 1)
        packed = jnp.zeros((height, width), jnp.float32)
        for i, field in enumerate(fields):
            x = field[...]
            ext[i, 0:height, 0:width] = x
            packed = jnp.where((lane >= 8 * i) & (lane < 8 * i + 4), pltpu.roll(x, 8 * i, 1), packed)
            packed = jnp.where(
                (lane >= 8 * i + 4) & (lane < 8 * i + 8), pltpu.roll(x, 8 * i + 8, 1), packed
            )
        side_out[...] = packed
        to_east = halo(0, side_out, west_in, east)
        to_west = halo(1, side_out, east_in, west)
        top, bottom = pl.ds(0, HALO), pl.ds(height - HALO, HALO)
        below, above = pl.ds(height, HALO), pl.ds(height + HALO, HALO)
        to_south = halo(2, ext.at[:, bottom], ext.at[:, above], south)
        to_north = halo(3, ext.at[:, top], ext.at[:, below], north)

        for present, copy in ((has_east, to_east), (has_west, to_west)):

            @pl.when(present)
            def _():
                copy.start()

        for present, buffer in ((has_west, west_in), (has_east, east_in)):

            @pl.when(jnp.logical_not(present))
            def _():
                buffer[...] = jnp.zeros(buffer.shape, jnp.float32)

        for present, where in ((has_south, below), (has_north, above)):

            @pl.when(jnp.logical_not(present))
            def _():
                ext[:, where] = jnp.zeros((len(fields), HALO, 2 * width), jnp.float32)

        rows, lanes = iota((height + 2 * HALO, 2 * width), 0), iota((height + 2 * HALO, 2 * width), 1)

        def allowed(region, present):
            return jnp.logical_not(region) | (jnp.full(rows.shape, present.astype(jnp.int32)) > 0)

        inside = allowed((rows >= height) & (rows < height + HALO), has_south)
        inside = inside & allowed(rows >= height + HALO, has_north)
        inside = inside & allowed((lanes >= width) & (lanes < width + width // 2), has_east)
        inside = inside & allowed(lanes >= width + width // 2, has_west)
        courant_ref[...] = jnp.where(inside, COURANT, 0.0)

        for present, copy in ((has_west, to_east), (has_east, to_west)):

            @pl.when(present)
            def _():
                copy.wait_recv()

        from_west, from_east = west_in[...], east_in[...]
        for i in range(len(fields)):
            ext[i, 0:height, width:] = jnp.where(
                lane < 4,
                pltpu.roll(from_east, (width - 8 * i) % width, 1),
                jnp.where(lane >= width - 4, pltpu.roll(from_west, width - 8 - 8 * i, 1), 0.0),
            )

        for present, copy in ((has_south, to_south), (has_north, to_north)):

            @pl.when(present)
            def _():
                copy.start()

        for present, copy in ((has_north, to_south), (has_south, to_north)):

            @pl.when(present)
            def _():
                copy.wait_recv()

        for present, copy in (
            (has_east, to_east),
            (has_west, to_west),
            (has_south, to_south),
            (has_north, to_north),
        ):

            @pl.when(present)
            def _():
                copy.wait_send()

        def advance():
            surface, eastward, southward = ext[0], ext[1], ext[2]
            level = new_level_ring(surface, eastward, southward, courant_ref[...])
            flux_e, flux_s = new_fluxes_ring(eastward, southward, level, ext[3], ext[4])
            ext[0] = level
            ext[1] = flux_e
            ext[2] = flux_s

        lane, sub = iota((PH, width), 1), iota((PH, width), 0)

        def covered(p):
            return jnp.full((PH, width), covers[p], jnp.int32) > 0

        def merge(parts_of, keep):
            for band in range(K):
                first = band * FINE_ROWS + TOP
                merged = [ext[f, first : first + PH, 0:width] for f in range(3)]
                for j in range(RR - 1):
                    p = band * (RR - 1) + j
                    column = LEFT + j * PW
                    here = covered(p)
                    for f, mask, values in parts_of(p, column):
                        merged[f] = jnp.where(here & mask, values, merged[f])
                for f in range(3):
                    keep(f, first, merged[f])

        def whole_parts(p, column):
            block = ret_in[slots[p]]
            mask = (lane >= column) & (lane < column + PW)
            return [(f, mask, pltpu.roll(block, (column - f * PW) % width, 1)) for f in range(3)]

        def border_parts(p, column):
            device, k = slots[p] // K, lax.rem(slots[p], K)
            line, ends = [
                jnp.broadcast_to(edge_now[device, pl.ds(2 * k + i, 1)], (PH, width)) for i in range(2)
            ]
            items = ends
            for r in range(1, PH):
                items = jnp.where(sub == r, pltpu.roll(ends, width - 16 * r, 1), items)
            inside = (lane >= column) & (lane < column + PW)
            out = []
            for f in range(3):
                out.append((f, inside & (sub == 0), pltpu.roll(line, (column - f * PW) % width, 1)))
            out.append((2, inside & (sub == PH - 1), pltpu.roll(line, (column - 3 * PW) % width, 1)))
            for i, (f, c) in enumerate(BORDER):
                at = column + c
                out.append((f, lane == at, pltpu.roll(items, (at - i) % width, 1)))
            return out

        def keep_inside(f, first, x):
            ext[f, first : first + PH, 0:width] = x

        def keep_result(f, first, x):
            out_ref[0, f, first : first + PH] = x

        @pl.loop(0, STEPS - 1)
        def _(s):
            advance()
            lines = pl.ds(0, 2 * K)
            wait_all(edge_in.at[s, :, lines], ret_recv.at[s])
            edge_now[:, 0 : 2 * K] = edge_in[s, :, 0 : 2 * K]
            merge(border_parts, keep_inside)

        advance()
        for f in range(3):
            out_ref[0, f] = ext[f, 0:height, 0:width]
        for copy in relays():
            copy.wait_send()
        wait_all(ret_in, ret_recv.at[STEPS - 1])
        merge(whole_parts, keep_result)

    @pl.when(jnp.logical_not(is_outer))
    def _():
        lane, sub = iota((PH, width), 1), iota((PH, width), 0)
        groups = FINE_ROWS // 8

        def find(keys, wanted, values):
            out = jnp.int32(0)
            for n in range(nests):
                out = jnp.where(keys[n] == wanted, values[n], out)
            return out

        def present(keys, wanted):
            out = jnp.int32(0)
            for n in range(nests):
                out = jnp.where(keys[n] == wanted, 1, out)
            return out

        def owner(slot):
            return slot // (K * n_nest), lax.rem(slot // K, n_nest), lax.rem(slot, K)

        spots, low_wants, high_wants, near_wants = [], [], [], []
        for i in range(n_row):
            at_row = lax.rem(row + i, n_row)
            for k in range(K):
                spot = find(host_ref, (at_row * n_nest + col) * K + k, place_ref)
                if i == 0:
                    spots.append(spot)
                low_wants.append(owner(find(place_ref, spot + 1, host_ref)))
        for i in range(n_nest):
            at_col = lax.rem(col + i, n_nest)
            for k in range(K):
                spot = spots[k] if i == 0 else find(host_ref, (row * n_nest + at_col) * K + k, place_ref)
                high_wants.append(owner(find(place_ref, spot - 1, host_ref)))
                near_wants.append(
                    (
                        spot // (NPOS * n_nest),
                        lax.rem(spot // NPOS, n_nest),
                        lax.rem(spot, NPOS) // (RR - 1),
                        lax.rem(spot, RR - 1),
                    )
                )
        lives = [present(host_ref, tile * K + k) for k in range(K)]
        homes = [spot // NPOS for spot in spots]
        bands = [lax.rem(spot, NPOS) // (RR - 1) for spot in spots]
        columns = [lax.rem(spot, RR - 1) for spot in spots]
        near = []
        for k in range(K):
            near.append(
                [
                    jnp.where(
                        (columns[k] + side >= 0) & (columns[k] + side < RR - 1),
                        present(place_ref, spots[k] + side),
                        0,
                    )
                    for side in (-1, 1)
                ]
            )

        gather_from = iota((3 * width, 2 * width), 0)
        gather_to = iota((3 * width, 2 * width), 1)
        field, lane_in = gather_from // width, lax.rem(gather_from, width)
        weight = jnp.where(
            field == 0,
            1.0 / (RR * RR),
            jnp.where((field == 2) | (lax.rem(lane_in, RR) == RR - 1), 1.0 / RR, 0.0),
        )
        gather = jnp.where(gather_to == field * PW + lane_in // RR, weight, 0.0)
        for i, (f, c) in enumerate(BORDER):
            gather = gather + jnp.where(
                (gather_to >= width)
                & (lax.rem(gather_to, 16) == i)
                & (field == f)
                & (lane_in // RR == c),
                weight,
                0.0,
            )
        half = width // K
        fine = iota((width, 2 * width), 1)
        beside = lax.rem(fine, half)
        coarse_lane = jnp.where(
            fine < width,
            NEAR + fine // RR,
            beside // RR + jnp.where(beside < half // 2, NEAR + PW, NEAR - half // RR),
        )
        widen = (iota((width, 2 * width), 0) == coarse_lane).astype(jnp.float32)
        gather, widen = [m.astype(jnp.bfloat16) for m in (gather, widen)]
        own_lanes = (lane >= NEAR) & (lane < NEAR + PW)
        of_first = (lane < half // 2) | (lane >= width - half // 2)

        def by_column(column, choices):
            out = choices[0]
            for j in range(1, len(choices)):
                out = jnp.where(jnp.full(out.shape, column, jnp.int32) == j, choices[j], out)
            return out

        def centred(x, k):
            return by_column(
                columns[k], [pltpu.roll(x, (NEAR - LEFT - j * PW) % width, 1) for j in range(RR - 1)]
            )

        span = 8 * len(SIDE_FIELDS)

        def around(want):
            early, late, sides = [bulk_in[want[0], 3 * want[2] + n] for n in range(3)]
            choices = []
            for j in range(RR - 1):
                first = LEFT + j * PW - 4
                x = jnp.where(
                    lane < 2 * span,
                    pltpu.roll(late, (span - first) % width, 1),
                    pltpu.roll(sides, (2 * span - span * j) % width, 1),
                )
                choices.append(jnp.where(lane < span, pltpu.roll(early, (-first) % width, 1), x))
            return [by_column(want[3], choices)]

        def pick_lane(block, index):
            return jnp.sum(jnp.where(lane == index, block, 0.0), axis=1, keepdims=True)

        def pick_row(block, index):
            return jnp.sum(jnp.where(sub == index, block, 0.0), axis=0, keepdims=True)

        def four(west_0, east_1, west_1, east_0):
            out = jnp.where(lane < half // 2, west_0, east_1)
            out = jnp.where(lane >= half, west_1, out)
            return jnp.where(lane >= width - half // 2, east_0, out)

        def keep_rows(t, lines):
            for k in range(K):
                ghost_rows[t, k, 0:2] = lines[2 * k : 2 * k + 2, 0:width]
            far = lines[:, width:]
            both = jnp.where(sub < 1, far[0:1], far[1:2])
            other = jnp.where(sub < 1, far[2:3], far[3:4])
            ghost_rows[t, K] = jnp.where(of_first, both, other)

        for load in loads:
            load.wait()
        for i in range(2):
            own_wet[i] = jnp.where(open_ref[0, i] > 0, depth_ref[0, i], 0.0)
        sources = [state_ref.at[0, f] for f in range(3)] + [own_wet.at[i] for i in range(2)]
        sources.append(state_ref.at[0, 1])
        for k in range(K):
            for side in (1, 0):
                packed = [jnp.zeros((PH, width), jnp.float32) for _ in range(STRIP_TILES)]
                for f, source in enumerate(sources):
                    if f == 5 and side == 0:
                        continue
                    first = 0 if side == 0 else width - STRIP * (2 if f == 5 else 1)
                    for g in range(groups):
                        at = (f % 2) * groups * STRIP + g * STRIP
                        piece = source[k * FINE_ROWS + 8 * g : k * FINE_ROWS + 8 * g + 8]
                        packed[f // 2] = jnp.where(
                            (lane >= at) & (lane < at + STRIP),
                            pltpu.roll(piece, (at - first) % width, 1),
                            packed[f // 2],
                        )
                for i, x in enumerate(packed):
                    if side == 0:
                        low_in[col, k, i] = x
                    else:
                        high_in[row, k, i] = x

        def to_peer(src, dst, sems, first_sem, device):
            pltpu.make_async_remote_copy(
                src_ref=src,
                dst_ref=dst,
                send_sem=sems.at[first_sem],
                recv_sem=sems.at[first_sem + 1],
                device_id=device,
                device_id_type=MESH,
            ).start()

        def in_plane(i):
            return sec, lax.rem(row + i, n_row), col

        def along_nest(i):
            return sec, row, lax.rem(col + i, n_nest)

        pl.semaphore_wait(barrier, tiles - 1)

        @pl.loop(1, n_row)
        def _(i):
            to_peer(high_in.at[row], high_in.at[row], high_sems, 0, in_plane(n_row - i))

        @pl.loop(1, n_nest)
        def _(i):
            to_peer(low_in.at[col], low_in.at[col], low_sems, 0, along_nest(n_nest - i))

        first_copy, bulk_copy = relays()
        first_copy.wait_recv()
        send_to(1, tiles - 1, first_in.at[tile], first_in.at[tile], first_sems.at[2], first_sems.at[3])
        bulk_copy.wait_recv()

        @pl.loop(1, n_row)
        def _(i):
            to_peer(bulk_in.at[row], bulk_in.at[row], bulk_sems, 2, in_plane(n_row - i))

        def pass_on(count, me, wants, pick, out, got, sems, device):
            for i in range(count):
                for k in range(K):
                    for n, x in enumerate(pick(wants[i * K + k])):
                        if i == 0:
                            got[me, k, n] = x
                        else:
                            out[i - 1, k, n] = x
                if i > 0:
                    to_peer(out.at[i - 1], got.at[me], sems[0], sems[1], device(i))

        wait_all(high_in.at[pl.ds(0, n_row - 1)], high_sems.at[1])
        pass_on(
            n_nest,
            col,
            high_wants,
            lambda w: [high_in[w[0], w[2], n] for n in range(STRIP_TILES)],
            high_out,
            high_got,
            (high_sems, 2),
            along_nest,
        )
        wait_all(low_in.at[pl.ds(0, n_nest - 1)], low_sems.at[1])
        pass_on(
            n_row,
            row,
            low_wants,
            lambda w: [low_in[w[1], w[2], n] for n in range(STRIP_TILES)],
            low_out,
            low_got,
            (low_sems, 2),
            in_plane,
        )
        wait_all(bulk_in.at[pl.ds(0, n_row - 1)], bulk_sems.at[3])
        pass_on(
            n_nest,
            col,
            near_wants,
            around,
            near_out,
            near_got,
            (near_sems, 0),
            along_nest,
        )

        wait_all(first_in.at[pl.ds(0, tiles - 1)], first_sems.at[3])
        blocks = [first_in[homes[k]] for k in range(K)]
        middles = [centred(block, k) for k, block in enumerate(blocks)]
        for t in range(2):
            lines = jnp.zeros((PH, width), jnp.float32)
            ends = []
            for k in range(K):
                at = t * (LEFT + (RR - 1) * PW) + bands[k] * (2 * (RR - 1)) + columns[k]
                to_east = at + RR - 1
                cols = jnp.where(
                    lane < width // 2, pick_lane(blocks[k], at), pick_lane(blocks[k], to_east)
                )
                ghost_cols[t, k] = grow_rows(cols)
                ends.append((pick_lane(blocks[k], at + 1), pick_lane(blocks[k], to_east - 1)))
                for i in range(2):
                    line = pick_row(middles[k], 2 * (t * K + bands[k]) + i)
                    lines = jnp.where(sub == 2 * k + i, line, lines)
            (west_0, east_0), (west_1, east_1) = ends
            ghost_cols[t, K] = grow_rows(four(west_0, east_1, west_1, east_0))
            keep_rows(t, dot_by(lines, widen))

        fine_lane = iota((FINE_ROWS, width), 1)
        own_ends = (fine_lane == 0, fine_lane == width - 1)
        slab_ends = (lax.rem(fine_lane, half) == 0, lax.rem(fine_lane, half) == half - 1)
        slots = [pl.ds(k * FINE_ROWS, FINE_ROWS) for k in range(K)]

        def load_own(source):
            return [[source[f, slot] for f in range(3)] for slot in slots]

        def substeps(which, states):
            wets = [
                [slab[3 + i] if k == K else own_wet[i, slots[k]] for i in range(2)] for k in which
            ]
            old_cols, new_cols = [[ghost_cols[t, k] for k in which] for t in range(2)]
            old_rows, new_rows = [[ghost_rows[t, k] for k in which] for t in range(2)]
            for m in range(1, RR + 1):
                for n, k in enumerate(which):
                    cols = old_cols[n] + (m / RR) * (new_cols[n] - old_cols[n])
                    rows = old_rows[n] + (m / RR) * (new_rows[n] - old_rows[n])
                    ends = slab_ends if k == K else own_ends
                    states[n] = slab_step(states[n], wets[n], cols, rows, *ends)
            return states

        def averages(states):
            sums = dot_by(
                jnp.concatenate(
                    [
                        jnp.concatenate([row_sums(x[0]), row_sums(x[1]), row_picks(x[2])], axis=1)
                        for x in states
                    ],
                    axis=0,
                ),
                gather,
            )
            sums = [sums[n * PH : (n + 1) * PH] for n in range(len(states))]
            return [x[:, 0:width] for x in sums], [x[:, width:] for x in sums]

        def send_border(s, coarse, border):
            for k in range(K):
                last = pltpu.roll(coarse[k], PW, 1)
                edge_out[s, 2 * k : 2 * k + 1] = jnp.where(
                    lane[0:1] < 3 * PW, coarse[k][0:1], last[PH - 1 : PH]
                )
                edge_out[s, 2 * k + 1 : 2 * k + 2] = jnp.sum(
                    jnp.where(lane // 16 == sub, border[k], 0.0), axis=0, keepdims=True
                )
            lines = pl.ds(0, 2 * K)
            send_all(edge_out.at[s, lines], edge_in.at[s, tile, lines], ret_send.at[s], ret_recv.at[s])

        def store_own(states):
            for k in range(K):
                for f in range(3):
                    st[f, slots[k]] = states[k][f]

        def next_ghosts(coarse):
            for k in range(K + 1):
                ghost_cols[0, k] = ghost_cols[1, k]
                ghost_rows[0, k] = ghost_rows[1, k]
            lines = jnp.zeros((PH, width), jnp.float32)
            ends = []
            for k in range(K):
                on_left, on_right = [
                    jnp.full((PH, width), cover, jnp.int32) > 0 for cover in near[k]
                ]
                on_left = on_left & (lane >= NEAR - 4) & (lane < NEAR)
                on_right = on_right & (lane >= NEAR + PW) & (lane < NEAR + PW + 4)
                boundary = k * half // RR
                state = []
                for f in range(3):
                    x = patch[k, f, 0:PH]
                    x = jnp.where(own_lanes, pltpu.roll(coarse[k], (NEAR - f * PW) % width, 1), x)
                    low = f * PW + (boundary - 4) % PW
                    x = jnp.where(on_left, pltpu.roll(coarse[K], (NEAR - 4 - low) % width, 1), x)
                    high = f * PW + boundary
                    x = jnp.where(on_right, pltpu.roll(coarse[K], (NEAR + PW - high) % width, 1), x)
                    state.append(jnp.concatenate([x, patch[k, f, PH : 2 * PH]], axis=0))
                level = new_level_ring(state[0], state[1], state[2], COURANT)
                flux_e, flux_s = new_fluxes_ring(state[1], state[2], level, wet[k, 0], wet[k, 1])
                for f, x in enumerate((level, flux_e, flux_s)):
                    patch[k, f] = x
                level8, east8 = level[0:PH], flux_e[0:PH]
                cols = jnp.where(
                    lane < width // 2,
                    pltpu.roll(east8, width - NEAR + 1, 1),
                    pltpu.roll(level8, width - 1 - NEAR - PW, 1),
                )
                ghost_cols[1, k] = grow_rows(cols)
                at = k * half
                ends.append(
                    (
                        pltpu.roll(east8, (at - (NEAR + PW - 1)) % width, 1),
                        pltpu.roll(level8, (at - 1 - NEAR) % width, 1),
                    )
                )
                lines = jnp.where(sub == 2 * k, flux_s[2 * PH - 1 : 2 * PH], lines)
                lines = jnp.where(sub == 2 * k + 1, level[PH : PH + 1], lines)
            (west_0, east_0), (west_1, east_1) = ends
            ghost_cols[1, K] = grow_rows(four(west_0, east_1, west_1, east_0))
            keep_rows(1, dot_by(lines, widen))

        states = substeps(range(K), load_own(state_ref.at[0]))
        store_own(states)
        coarse, border = averages(states)


        send_border(0, coarse, border)

        wait_all(high_got.at[pl.ds(0, n_nest - 1)], high_sems.at[3])
        wait_all(low_got.at[pl.ds(0, n_row - 1)], low_sems.at[3])
        sets = [
            [
                [high_got[high_wants[k][1], k, n] for n in range(STRIP_TILES)],
                [low_got[low_wants[k][0], k, n] for n in range(STRIP_TILES)],
            ]
            for k in range(K)
        ]
        fits = []
        for k in range(K):
            start = k * half
            on_left, on_right = [jnp.full((PH, width), cover, jnp.int32) > 0 for cover in near[k]]
            before = (start - STRIP) % width
            fits.append(
                (
                    on_left & (lane >= before) & (lane < before + STRIP),
                    on_right & (lane >= start) & (lane < start + STRIP),
                    on_left & (lane == before - 1),
                )
            )
        for f in range(5):
            for g in range(groups):
                out = jnp.zeros((PH, width), jnp.float32)
                at = (f % 2) * groups * STRIP + g * STRIP
                for k in range(K):
                    start = k * half
                    before = (start - STRIP) % width
                    left, right = [sets[k][side][f // 2] for side in range(2)]
                    out = jnp.where(fits[k][0], pltpu.roll(left, (before - at) % width, 1), out)
                    out = jnp.where(fits[k][1], pltpu.roll(right, (start - at) % width, 1), out)
                    if f == 1:
                        extra = groups * STRIP + (g + 1) * STRIP - 1
                        out = jnp.where(
                            fits[k][2],
                            pltpu.roll(sets[k][0][2], (before - 1 - extra) % width, 1),
                            out,
                        )
                slab[f, 8 * g : 8 * g + 8] = out

        def load_slab():
            return [slab[f] for f in range(3)]

        def store_slab(state):
            for f in range(3):
                slab[f] = state[f]

        aside = substeps([K], [load_slab()])
        store_slab(aside[0])
        beside_own, _ = averages(aside)

        wait_all(near_got.at[pl.ds(0, n_nest - 1)], near_sems.at[1])
        for k in range(K):
            got = near_got[near_wants[k][1], k, 0]
            early, late, sides = [
                pltpu.roll(got, shift % width, 1) for shift in (NEAR - 4, NEAR - 4 - span, -2 * span)
            ]

            def tile_of(block, spots):
                out = jnp.zeros((PH, width), jnp.float32)
                for target, source in spots:
                    out = jnp.where(sub == target, block[source : source + 1], out)
                return out

            outside = [
                tile_of(early, ((0, 0), (1, 1), (7, 5))),
                tile_of(early, ((0, 2), (7, 6))),
                tile_of(early, ((0, 3), (6, 4), (7, 7))),
                tile_of(late, ((0, 3), (7, 4))),
                tile_of(late, ((0, 5), (6, 6), (7, 7))),
            ]
            for i in range(5):
                beside = jnp.where(
                    lane < NEAR + PW // 2,
                    pltpu.roll(sides, (NEAR - 4 - 8 * i) % width, 1),
                    pltpu.roll(sides, (NEAR + PW - 5 - 8 * i) % width, 1),
                )
                target = patch.at[k, i] if i < 3 else wet.at[k, i - 3]
                target[0:PH] = beside
                target[PH : 2 * PH] = outside[i]
            later[k, 0] = tile_of(late, ((1, 0), (6, 1)))
            later[k, 1] = tile_of(late, ((5, 2), (6, 2)))

        next_ghosts(coarse + beside_own)

        @pl.loop(1, STEPS - 1)
        def _(s):
            states = substeps(range(K + 1), load_own(st) + [load_slab()])
            coarse, border = averages(states)
            send_border(s, coarse, border)
            store_own(states)
            store_slab(states[K])

            @pl.when(s == 1)
            def _():
                given = (sub == 1) | (sub == 5) | (sub == 6)
                for k in range(K):
                    for f, value in enumerate((later[k, 0], 0.0, later[k, 1])):
                        patch[k, f, PH : 2 * PH] = jnp.where(given, value, patch[k, f, PH : 2 * PH])

            next_ghosts(coarse)

        states = substeps(range(K), load_own(st))
        coarse, _ = averages(states)
        for k in range(K):
            ret_out[k] = coarse[k]
        send_all(ret_out, ret_in.at[pl.ds(tile * K, K)], ret_send.at[STEPS - 1], ret_recv.at[STEPS - 1])
        for k in range(K):
            live = jnp.full((FINE_ROWS, width), lives[k], jnp.int32) > 0
            for f in range(3):
                out_ref[0, f, slots[k]] = jnp.where(live, states[k][f], state_ref[0, f, slots[k]])

        wait_all(first_in.at[pl.ds(0, tiles - 1)], first_sems.at[2])
        wait_all(bulk_in.at[pl.ds(0, n_row - 1)], bulk_sems.at[2])
        wait_all(low_in.at[pl.ds(0, n_nest - 1)], low_sems.at[0])
        wait_all(low_got.at[pl.ds(0, n_row - 1)], low_sems.at[2])
        wait_all(high_in.at[pl.ds(0, n_row - 1)], high_sems.at[0])
        wait_all(high_got.at[pl.ds(0, n_nest - 1)], high_sems.at[2])
        wait_all(near_got.at[pl.ds(0, n_nest - 1)], near_sems.at[0])
        for s in range(STEPS - 1):
            wait_all(edge_in.at[s, :, pl.ds(0, 2 * K)], ret_send.at[s])
        wait_all(ret_in, ret_send.at[STEPS - 1])


def on_device(n_row, n_nest, ocean_state, face_depth, face_open, nest_place, nest_host):
    tiles = n_row * n_nest
    height, width = ocean_state.shape[2:]
    f32 = jnp.float32
    vmem = pl.BlockSpec(memory_space=pltpu.VMEM)
    hbm = pl.BlockSpec(memory_space=pl.ANY)
    smem = pl.BlockSpec(memory_space=pltpu.SMEM)
    dma = pltpu.SemaphoreType.DMA
    return pl.pallas_call(
        functools.partial(kernel, n_row, n_nest),
        out_shape=pltpu.VMEM(ocean_state.shape, f32),
        in_specs=[smem, smem, hbm, hbm, hbm],
        out_specs=vmem,
        scratch_shapes=[
            pltpu.VMEM(ocean_state.shape, f32),
            pltpu.VMEM(face_depth.shape, f32),
            pltpu.VMEM(face_open.shape, jnp.int32),
            dma((3,)),
            pltpu.VMEM((3, height, width), f32),
            pltpu.VMEM((9, height, width), f32),
            pltpu.VMEM((PH, width), f32),
            pltpu.VMEM((tiles, PH, width), f32),
            pltpu.VMEM((3 * K, PH, width), f32),
            pltpu.VMEM((n_row, 3 * K, PH, width), f32),
            pltpu.VMEM((n_nest, K, STRIP_TILES, PH, width), f32),
            pltpu.VMEM((n_row, K, STRIP_TILES, PH, width), f32),
            pltpu.VMEM((n_row, K, STRIP_TILES, PH, width), f32),
            pltpu.VMEM((n_row, K, STRIP_TILES, PH, width), f32),
            pltpu.VMEM((n_nest, K, STRIP_TILES, PH, width), f32),
            pltpu.VMEM((n_nest, K, STRIP_TILES, PH, width), f32),
            pltpu.VMEM((n_nest, K, 1, PH, width), f32),
            pltpu.VMEM((n_nest, K, 1, PH, width), f32),
            pltpu.VMEM((STEPS - 1, PH, width), f32),
            pltpu.VMEM((STEPS - 1, tiles, PH, width), f32),
            pltpu.VMEM((K, PH, width), f32),
            pltpu.VMEM((tiles * K, PH, width), f32),
            pltpu.VMEM((height, width), f32),
            pltpu.VMEM((height, width), f32),
            pltpu.VMEM((height, width), f32),
            pltpu.VMEM((5, height + 2 * HALO, 2 * width), f32),
            pltpu.VMEM((height + 2 * HALO, 2 * width), f32),
            pltpu.VMEM((2, K + 1, FINE_ROWS, width), f32),
            pltpu.VMEM((2, K + 1, PH, width), f32),
            pltpu.VMEM((K, 3, 2 * PH, width), f32),
            pltpu.VMEM((K, 2, 2 * PH, width), f32),
            pltpu.VMEM((K, 2, PH, width), f32),
            pltpu.VMEM((5, FINE_ROWS, width), f32),
            pltpu.VMEM((2, height, width), f32),
            pltpu.VMEM((tiles, PH, width), f32),
            dma((4,)),
            dma((4,)),
            dma((4,)),
            dma((4,)),
            dma((2,)),
            dma((STEPS,)),
            dma((STEPS,)),
            dma((4,)),
            dma((4,)),
        ],
        compiler_params=pltpu.CompilerParams(collective_id=0, has_side_effects=True),
    )(nest_place, nest_host, ocean_state, face_depth, face_open)


def solution(mesh):
    field = P("sec", None, "row", "nest")
    return jax.shard_map(
        functools.partial(on_device, mesh.shape["row"], mesh.shape["nest"]),
        mesh=mesh,
        in_specs=(field, field, field, P(), P()),
        out_specs=field,
        check_vma=False,
    )
```

```python
import functools

import jax
import jax.numpy as jnp
from jax import lax
from jax.experimental import pallas as pl
from jax.experimental.pallas import tpu as pltpu
from jax.sharding import PartitionSpec as P

PH = 8
PW = 32
RR = 4
K = 2
STEPS = 4
NPOS = K * (RR - 1)
COURANT = 0.3
MESH = pl.DeviceIdType.MESH
FINE_ROWS = RR * PH
TOP = (RR - 1) * PH // 2
LEFT = PW // 2
NEAR = PW
BORDER = ((0, 0), (1, 0), (2, 0), (1, PW - 1))
STRIP = 16
STRIP_TILES = 3
BAND = (TOP + PH + STEPS + 7) // 8 * 8
HALO = 8
ROWS_EARLY = ((0, PH), (3, PH + 1), (1, PH), (2, PH), (2, -2), (0, -1), (1, -1), (2, -1))
ROWS_LATE = ((4, PH + 1), (5, -2), (6, -2), (7, PH), (7, -1), (8, PH), (8, -2), (8, -1))
SIDE_FIELDS = (0, 1, 2, 7, 8)


def iota(shape, dim):
    return lax.broadcasted_iota(jnp.int32, shape, dim)


def slab_step(fields, wet, cols, rows, west_at, east_at):
    surface, eastward, southward = fields
    height, width = surface.shape
    sub = iota(surface.shape, 0)
    east_behind = jnp.where(west_at, cols, pltpu.roll(eastward, 1, 1))
    south_behind = jnp.where(sub == 0, rows[0:1], pltpu.roll(southward, 1, 0))
    level = surface - COURANT * ((eastward - east_behind) + (southward - south_behind))
    level_east = jnp.where(east_at, cols, pltpu.roll(level, width - 1, 1))
    level_south = jnp.where(sub == height - 1, rows[1:2], pltpu.roll(level, height - 1, 0))
    east = eastward - COURANT * (wet[0] + 0.5 * (level + level_east)) * (level_east - level)
    south = southward - COURANT * (wet[1] + 0.5 * (level + level_south)) * (level_south - level)
    return [level, jnp.where(wet[0] > 0, east, 0.0), jnp.where(wet[1] > 0, south, 0.0)]


def new_level_ring(surface, eastward, southward, courant):
    east_gap = eastward - pltpu.roll(eastward, 1, 1)
    south_gap = southward - pltpu.roll(southward, 1, 0)
    return surface - courant * (east_gap + south_gap)


def new_fluxes_ring(eastward, southward, level, wet_east, wet_south):
    height, width = level.shape
    level_east = pltpu.roll(level, width - 1, 1)
    level_south = pltpu.roll(level, height - 1, 0)
    east = eastward - COURANT * (wet_east + 0.5 * (level + level_east)) * (level_east - level)
    south = southward - COURANT * (wet_south + 0.5 * (level + level_south)) * (level_south - level)
    return jnp.where(wet_east > 0, east, 0.0), jnp.where(wet_south > 0, south, 0.0)


def parts(x):
    high = x.astype(jnp.bfloat16).astype(jnp.float32)
    rest = x - high
    middle = rest.astype(jnp.bfloat16).astype(jnp.float32)
    return high, middle, rest - middle


def dot_by(x, chosen):
    rows = x.shape[0]
    stacked = jnp.concatenate(parts(x), axis=0).astype(jnp.bfloat16)
    y = jnp.dot(stacked, chosen, preferred_element_type=jnp.float32)
    return y[:rows] + (y[rows : 2 * rows] + y[2 * rows :])


def pack_strips(times):
    width = times[0][0].shape[-1]
    lane, sub = iota((PH, width), 1), iota((PH, width), 0)
    block = jnp.zeros((PH, width), jnp.float32)
    span = (RR - 1) * PW
    inner = (lane >= LEFT) & (lane < LEFT + span)
    for t, fields in enumerate(times):
        surface, eastward, southward = fields
        for band in range(K):
            first = band * FINE_ROWS + TOP
            east8 = eastward[first : first + PH, :]
            level8 = surface[first : first + PH, :]
            for j in range(RR - 1):
                column = LEFT + j * PW
                west_lane = t * (LEFT + span) + band * 2 * (RR - 1) + j
                east_lane = west_lane + RR - 1
                block = jnp.where(
                    lane == west_lane, pltpu.roll(east8, (west_lane - column + 1) % width, 1), block
                )
                block = jnp.where(
                    lane == east_lane, pltpu.roll(level8, (east_lane - column - PW) % width, 1), block
                )
            row = (t * K + band) * 2
            block = jnp.where(inner & (sub == row), southward[first - 1 : first, :], block)
            block = jnp.where(inner & (sub == row + 1), surface[first + PH : first + PH + 1, :], block)
    return block


def pack_sides(free, band):
    width = free.shape[-1]
    lane = iota((PH, width), 1)
    block = jnp.zeros((PH, width), jnp.float32)
    first = band * FINE_ROWS + TOP
    for i, f in enumerate(SIDE_FIELDS):
        values = free[f, first : first + PH, :]
        for j in range(RR - 1):
            column = LEFT + j * PW
            target = j * 8 * len(SIDE_FIELDS) + 8 * i
            for side, source in ((0, column - 4), (4, column + PW - 1)):
                at = target + side
                block = jnp.where(
                    (lane >= at) & (lane < at + 4), pltpu.roll(values, (at - source) % width, 1), block
                )
    return block


def row_sums(x):
    width = x.shape[1]
    sub = iota((8, width), 0)
    out = jnp.zeros((8, width), jnp.float32)
    for v in range(x.shape[0] // 8):
        piece = x[8 * v : 8 * v + 8]
        piece = piece + pltpu.roll(piece, 1, 0)
        piece = piece + pltpu.roll(piece, 2, 0)
        out = jnp.where(sub == 2 * v, piece[3:4], out)
        out = jnp.where(sub == 2 * v + 1, piece[7:8], out)
    return out


def row_picks(x):
    width = x.shape[1]
    sub = iota((8, width), 0)
    out = jnp.zeros((8, width), jnp.float32)
    for v in range(x.shape[0] // 8):
        out = jnp.where(sub == 2 * v, x[8 * v + 3 : 8 * v + 4], out)
        out = jnp.where(sub == 2 * v + 1, x[8 * v + 7 : 8 * v + 8], out)
    return out


def grow_rows(x):
    sub = iota(x.shape, 0)
    return jnp.concatenate(
        [jnp.where(sub < 4, x[2 * v : 2 * v + 1], x[2 * v + 1 : 2 * v + 2]) for v in range(RR)], axis=0
    )


def partner(index, step, count):
    if count & (count - 1) == 0:
        return index ^ step
    return lax.rem(index + step, count)


def kernel(
    n_row,
    n_nest,
    place_ref,
    host_ref,
    state_hbm,
    depth_hbm,
    open_hbm,
    out_ref,
    state_ref,
    depth_ref,
    open_ref,
    load_sems,
    st,
    free,
    first_out,
    first_in,
    bulk_out,
    bulk_in,
    low_in,
    low_out,
    low_got,
    high_in,
    high_out,
    high_got,
    near_out,
    near_got,
    edge_out,
    edge_in,
    ret_out,
    ret_in,
    side_out,
    west_in,
    east_in,
    ext,
    courant_ref,
    ghost_cols,
    ghost_rows,
    patch,
    wet,
    later,
    slab,
    own_wet,
    edge_now,
    first_sems,
    bulk_sems,
    low_sems,
    high_sems,
    near_sems,
    ret_send,
    ret_recv,
    halo_send,
    halo_recv,
):
    tiles = n_row * n_nest
    nests = place_ref.shape[0]
    sec, row, col = lax.axis_index("sec"), lax.axis_index("row"), lax.axis_index("nest")
    tile = row * n_nest + col
    is_outer = sec == 0
    has_west, has_east = col > 0, col < n_nest - 1
    has_north, has_south = row > 0, row < n_row - 1
    west, east = (sec, row, col - 1), (sec, row, col + 1)
    north, south = (sec, row - 1, col), (sec, row + 1, col)
    links = ((has_west, west), (has_east, east), (has_north, north), (has_south, south))
    height, width = state_ref.shape[2], state_ref.shape[3]

    barrier = pltpu.get_barrier_semaphore()

    @pl.when(jnp.logical_not(is_outer))
    def _():
        pl.semaphore_signal(barrier, inc=1, device_id=(0, row, col), device_id_type=MESH)

        @pl.loop(0, tiles - 1)
        def _(i):
            t = lax.rem(tile + i + 1, tiles)
            pl.semaphore_signal(
                barrier, inc=1, device_id=(sec, t // n_nest, lax.rem(t, n_nest)), device_id_type=MESH
            )

    loads = [
        pltpu.make_async_copy(source, target, load_sems.at[i])
        for i, (source, target) in enumerate(
            ((state_hbm, state_ref), (depth_hbm, depth_ref), (open_hbm, open_ref))
        )
    ]
    for load in loads:
        load.start()

    def send_to(section, count, src, dst, send_sem, recv_sem):
        for far in range(tiles - 1, tiles - 1 - count, -1):
            pltpu.make_async_remote_copy(
                src_ref=src,
                dst_ref=dst,
                send_sem=send_sem,
                recv_sem=recv_sem,
                device_id=(
                    section,
                    partner(row, far % n_row, n_row),
                    partner(col, far // n_row, n_nest),
                ),
                device_id_type=MESH,
            ).start()

    def send_all(src, dst, send_sem, recv_sem):
        send_to(1 - sec, tiles, src, dst, send_sem, recv_sem)

    def wait_all(whole, sem):
        pltpu.make_async_copy(whole, whole, sem).wait()

    def relays():
        return [
            pltpu.make_async_remote_copy(
                src_ref=src,
                dst_ref=dst,
                send_sem=sems.at[0],
                recv_sem=sems.at[1],
                device_id=(1, row, col),
                device_id_type=MESH,
            )
            for src, dst, sems in (
                (first_out, first_in.at[tile], first_sems),
                (bulk_out, bulk_in.at[row], bulk_sems),
            )
        ]

    @pl.when(is_outer)
    def _():
        for present, device in links:

            @pl.when(present)
            def _():
                pl.semaphore_signal(barrier, inc=1, device_id=device, device_id_type=MESH)

        slots, covers = [], []
        for p in range(NPOS):
            slot, cover = jnp.int32(0), jnp.int32(0)
            for n in range(nests):
                hit = place_ref[n] == tile * NPOS + p
                slot = jnp.where(hit, host_ref[n], slot)
                cover = jnp.where(hit, 1, cover)
            slots.append(slot)
            covers.append(cover)
        for load in loads:
            load.wait()
        for i in range(2):
            free[7 + i] = jnp.where(open_ref[0, i] > 0, depth_ref[0, i], 0.0)
        levels = []
        for band in range(K):
            lo = band * FINE_ROWS
            hi = lo + BAND
            old = [state_ref[0, f, lo:hi] for f in range(3)]
            level = new_level_ring(old[0], old[1], old[2], COURANT)
            flux_e, flux_s = new_fluxes_ring(old[1], old[2], level, free[7, lo:hi], free[8, lo:hi])
            free[0, lo:hi] = level
            free[1, lo:hi] = flux_e
            free[2, lo:hi] = flux_s
        first_out[...] = pack_strips(
            [[ref.at[f] for f in range(3)] for ref in (state_ref.at[0], free)]
        )
        peers = jnp.int32(1)
        for present, _device in links:
            peers = peers + jnp.where(present, 1, 0)
        pl.semaphore_wait(barrier, peers)
        first_copy, bulk_copy = relays()
        first_copy.start()
        for band in range(K):
            lo = band * FINE_ROWS
            hi = lo + BAND
            level, flux_e, flux_s = [free[f, lo:hi] for f in range(3)]
            for i in range(2):
                east_gap = flux_e - pltpu.roll(flux_e, 1, 1)
                free[3 + i, lo:hi] = level - COURANT * (east_gap + flux_s)
                level = level - COURANT * (east_gap + (flux_s - pltpu.roll(flux_s, 1, 0)))
                if i == 0:
                    flux_e, flux_s = new_fluxes_ring(
                        flux_e, flux_s, level, free[7, lo:hi], free[8, lo:hi]
                    )
            free[5, lo:hi] = level
            free[6, lo:hi] = flux_s
        for band in range(K):
            first = band * FINE_ROWS + TOP
            for part, chosen in enumerate((ROWS_EARLY, ROWS_LATE)):
                for i, (f, shift) in enumerate(chosen):
                    at = first + shift
                    bulk_out[3 * band + part, i : i + 1] = free[f, at : at + 1]
            bulk_out[3 * band + 2] = pack_sides(free, band)

        bulk_copy.start()

        def halo(kind, src, dst, device):
            return pltpu.make_async_remote_copy(
                src_ref=src,
                dst_ref=dst,
                send_sem=halo_send.at[kind],
                recv_sem=halo_recv.at[kind],
                device_id=device,
                device_id_type=MESH,
            )

        fields = [state_ref.at[0, f] for f in range(3)] + [free.at[7 + i] for i in range(2)]
        lane = iota((height, width), 1)
        packed = jnp.zeros((height, width), jnp.float32)
        for i, field in enumerate(fields):
            x = field[...]
            ext[i, 0:height, 0:width] = x
            packed = jnp.where((lane >= 8 * i) & (lane < 8 * i + 4), pltpu.roll(x, 8 * i, 1), packed)
            packed = jnp.where(
                (lane >= 8 * i + 4) & (lane < 8 * i + 8), pltpu.roll(x, 8 * i + 8, 1), packed
            )
        side_out[...] = packed
        to_east = halo(0, side_out, west_in, east)
        to_west = halo(1, side_out, east_in, west)
        top, bottom = pl.ds(0, HALO), pl.ds(height - HALO, HALO)
        below, above = pl.ds(height, HALO), pl.ds(height + HALO, HALO)
        to_south = halo(2, ext.at[:, bottom], ext.at[:, above], south)
        to_north = halo(3, ext.at[:, top], ext.at[:, below], north)

        for present, copy in ((has_east, to_east), (has_west, to_west)):

            @pl.when(present)
            def _():
                copy.start()

        for present, buffer in ((has_west, west_in), (has_east, east_in)):

            @pl.when(jnp.logical_not(present))
            def _():
                buffer[...] = jnp.zeros(buffer.shape, jnp.float32)

        for present, where in ((has_south, below), (has_north, above)):

            @pl.when(jnp.logical_not(present))
            def _():
                ext[:, where] = jnp.zeros((len(fields), HALO, 2 * width), jnp.float32)

        rows, lanes = iota((height + 2 * HALO, 2 * width), 0), iota((height + 2 * HALO, 2 * width), 1)

        def allowed(region, present):
            return jnp.logical_not(region) | (jnp.full(rows.shape, present.astype(jnp.int32)) > 0)

        inside = allowed((rows >= height) & (rows < height + HALO), has_south)
        inside = inside & allowed(rows >= height + HALO, has_north)
        inside = inside & allowed((lanes >= width) & (lanes < width + width // 2), has_east)
        inside = inside & allowed(lanes >= width + width // 2, has_west)
        courant_ref[...] = jnp.where(inside, COURANT, 0.0)

        for present, copy in ((has_west, to_east), (has_east, to_west)):

            @pl.when(present)
            def _():
                copy.wait_recv()

        from_west, from_east = west_in[...], east_in[...]
        for i in range(len(fields)):
            ext[i, 0:height, width:] = jnp.where(
                lane < 4,
                pltpu.roll(from_east, (width - 8 * i) % width, 1),
                jnp.where(lane >= width - 4, pltpu.roll(from_west, width - 8 - 8 * i, 1), 0.0),
            )

        for present, copy in ((has_south, to_south), (has_north, to_north)):

            @pl.when(present)
            def _():
                copy.start()

        for present, copy in ((has_north, to_south), (has_south, to_north)):

            @pl.when(present)
            def _():
                copy.wait_recv()

        for present, copy in (
            (has_east, to_east),
            (has_west, to_west),
            (has_south, to_south),
            (has_north, to_north),
        ):

            @pl.when(present)
            def _():
                copy.wait_send()

        def advance():
            surface, eastward, southward = ext[0], ext[1], ext[2]
            level = new_level_ring(surface, eastward, southward, courant_ref[...])
            flux_e, flux_s = new_fluxes_ring(eastward, southward, level, ext[3], ext[4])
            ext[0] = level
            ext[1] = flux_e
            ext[2] = flux_s

        lane, sub = iota((PH, width), 1), iota((PH, width), 0)

        def covered(p):
            return jnp.full((PH, width), covers[p], jnp.int32) > 0

        def merge(parts_of, keep):
            for band in range(K):
                first = band * FINE_ROWS + TOP
                merged = [ext[f, first : first + PH, 0:width] for f in range(3)]
                for j in range(RR - 1):
                    p = band * (RR - 1) + j
                    column = LEFT + j * PW
                    here = covered(p)
                    for f, mask, values in parts_of(p, column):
                        merged[f] = jnp.where(here & mask, values, merged[f])
                for f in range(3):
                    keep(f, first, merged[f])

        def whole_parts(p, column):
            block = ret_in[slots[p]]
            mask = (lane >= column) & (lane < column + PW)
            return [(f, mask, pltpu.roll(block, (column - f * PW) % width, 1)) for f in range(3)]

        def border_parts(p, column):
            device, k = slots[p] // K, lax.rem(slots[p], K)
            line, ends = [
                jnp.broadcast_to(edge_now[device, pl.ds(2 * k + i, 1)], (PH, width)) for i in range(2)
            ]
            items = ends
            for r in range(1, PH):
                items = jnp.where(sub == r, pltpu.roll(ends, width - 16 * r, 1), items)
            inside = (lane >= column) & (lane < column + PW)
            out = []
            for f in range(3):
                out.append((f, inside & (sub == 0), pltpu.roll(line, (column - f * PW) % width, 1)))
            out.append((2, inside & (sub == PH - 1), pltpu.roll(line, (column - 3 * PW) % width, 1)))
            for i, (f, c) in enumerate(BORDER):
                at = column + c
                out.append((f, lane == at, pltpu.roll(items, (at - i) % width, 1)))
            return out

        def keep_inside(f, first, x):
            ext[f, first : first + PH, 0:width] = x

        def keep_result(f, first, x):
            out_ref[0, f, first : first + PH] = x

        @pl.loop(0, STEPS - 1)
        def _(s):
            advance()
            lines = pl.ds(0, 2 * K)
            wait_all(edge_in.at[s, :, lines], ret_recv.at[s])
            edge_now[:, 0 : 2 * K] = edge_in[s, :, 0 : 2 * K]
            merge(border_parts, keep_inside)

        advance()
        for f in range(3):
            out_ref[0, f] = ext[f, 0:height, 0:width]
        for copy in relays():
            copy.wait_send()
        wait_all(ret_in, ret_recv.at[STEPS - 1])
        merge(whole_parts, keep_result)

    @pl.when(jnp.logical_not(is_outer))
    def _():
        lane, sub = iota((PH, width), 1), iota((PH, width), 0)
        groups = FINE_ROWS // 8

        def find(keys, wanted, values):
            out = jnp.int32(0)
            for n in range(nests):
                out = jnp.where(keys[n] == wanted, values[n], out)
            return out

        def present(keys, wanted):
            out = jnp.int32(0)
            for n in range(nests):
                out = jnp.where(keys[n] == wanted, 1, out)
            return out

        def owner(slot):
            return slot // (K * n_nest), lax.rem(slot // K, n_nest), lax.rem(slot, K)

        spots, low_wants, high_wants, near_wants = [], [], [], []
        for i in range(n_row):
            at_row = lax.rem(row + i, n_row)
            for k in range(K):
                spot = find(host_ref, (at_row * n_nest + col) * K + k, place_ref)
                if i == 0:
                    spots.append(spot)
                low_wants.append(owner(find(place_ref, spot + 1, host_ref)))
        for i in range(n_nest):
            at_col = lax.rem(col + i, n_nest)
            for k in range(K):
                spot = spots[k] if i == 0 else find(host_ref, (row * n_nest + at_col) * K + k, place_ref)
                high_wants.append(owner(find(place_ref, spot - 1, host_ref)))
                near_wants.append(
                    (
                        spot // (NPOS * n_nest),
                        lax.rem(spot // NPOS, n_nest),
                        lax.rem(spot, NPOS) // (RR - 1),
                        lax.rem(spot, RR - 1),
                    )
                )
        lives = [present(host_ref, tile * K + k) for k in range(K)]
        homes = [spot // NPOS for spot in spots]
        bands = [lax.rem(spot, NPOS) // (RR - 1) for spot in spots]
        columns = [lax.rem(spot, RR - 1) for spot in spots]
        near = []
        for k in range(K):
            near.append(
                [
                    jnp.where(
                        (columns[k] + side >= 0) & (columns[k] + side < RR - 1),
                        present(place_ref, spots[k] + side),
                        0,
                    )
                    for side in (-1, 1)
                ]
            )

        gather_from = iota((3 * width, 2 * width), 0)
        gather_to = iota((3 * width, 2 * width), 1)
        field, lane_in = gather_from // width, lax.rem(gather_from, width)
        weight = jnp.where(
            field == 0,
            1.0 / (RR * RR),
            jnp.where((field == 2) | (lax.rem(lane_in, RR) == RR - 1), 1.0 / RR, 0.0),
        )
        gather = jnp.where(gather_to == field * PW + lane_in // RR, weight, 0.0)
        for i, (f, c) in enumerate(BORDER):
            gather = gather + jnp.where(
                (gather_to >= width)
                & (lax.rem(gather_to, 16) == i)
                & (field == f)
                & (lane_in // RR == c),
                weight,
                0.0,
            )
        half = width // K
        fine = iota((width, 2 * width), 1)
        beside = lax.rem(fine, half)
        coarse_lane = jnp.where(
            fine < width,
            NEAR + fine // RR,
            beside // RR + jnp.where(beside < half // 2, NEAR + PW, NEAR - half // RR),
        )
        widen = (iota((width, 2 * width), 0) == coarse_lane).astype(jnp.float32)
        gather, widen = [m.astype(jnp.bfloat16) for m in (gather, widen)]
        own_lanes = (lane >= NEAR) & (lane < NEAR + PW)
        of_first = (lane < half // 2) | (lane >= width - half // 2)

        def by_column(column, choices):
            out = choices[0]
            for j in range(1, len(choices)):
                out = jnp.where(jnp.full(out.shape, column, jnp.int32) == j, choices[j], out)
            return out

        def centred(x, k):
            return by_column(
                columns[k], [pltpu.roll(x, (NEAR - LEFT - j * PW) % width, 1) for j in range(RR - 1)]
            )

        span = 8 * len(SIDE_FIELDS)

        def around(want):
            early, late, sides = [bulk_in[want[0], 3 * want[2] + n] for n in range(3)]
            choices = []
            for j in range(RR - 1):
                first = LEFT + j * PW - 4
                x = jnp.where(
                    lane < 2 * span,
                    pltpu.roll(late, (span - first) % width, 1),
                    pltpu.roll(sides, (2 * span - span * j) % width, 1),
                )
                choices.append(jnp.where(lane < span, pltpu.roll(early, (-first) % width, 1), x))
            return [by_column(want[3], choices)]

        def pick_lane(block, index):
            return jnp.sum(jnp.where(lane == index, block, 0.0), axis=1, keepdims=True)

        def pick_row(block, index):
            return jnp.sum(jnp.where(sub == index, block, 0.0), axis=0, keepdims=True)

        def four(west_0, east_1, west_1, east_0):
            out = jnp.where(lane < half // 2, west_0, east_1)
            out = jnp.where(lane >= half, west_1, out)
            return jnp.where(lane >= width - half // 2, east_0, out)

        def keep_rows(t, lines):
            for k in range(K):
                ghost_rows[t, k, 0:2] = lines[2 * k : 2 * k + 2, 0:width]
            far = lines[:, width:]
            both = jnp.where(sub < 1, far[0:1], far[1:2])
            other = jnp.where(sub < 1, far[2:3], far[3:4])
            ghost_rows[t, K] = jnp.where(of_first, both, other)

        for load in loads:
            load.wait()
        for i in range(2):
            own_wet[i] = jnp.where(open_ref[0, i] > 0, depth_ref[0, i], 0.0)
        sources = [state_ref.at[0, f] for f in range(3)] + [own_wet.at[i] for i in range(2)]
        sources.append(state_ref.at[0, 1])
        for k in range(K):
            for side in (1, 0):
                packed = [jnp.zeros((PH, width), jnp.float32) for _ in range(STRIP_TILES)]
                for f, source in enumerate(sources):
                    if f == 5 and side == 0:
                        continue
                    first = 0 if side == 0 else width - STRIP * (2 if f == 5 else 1)
                    for g in range(groups):
                        at = (f % 2) * groups * STRIP + g * STRIP
                        piece = source[k * FINE_ROWS + 8 * g : k * FINE_ROWS + 8 * g + 8]
                        packed[f // 2] = jnp.where(
                            (lane >= at) & (lane < at + STRIP),
                            pltpu.roll(piece, (at - first) % width, 1),
                            packed[f // 2],
                        )
                for i, x in enumerate(packed):
                    if side == 0:
                        low_in[col, k, i] = x
                    else:
                        high_in[row, k, i] = x

        def to_peer(src, dst, sems, first_sem, device):
            pltpu.make_async_remote_copy(
                src_ref=src,
                dst_ref=dst,
                send_sem=sems.at[first_sem],
                recv_sem=sems.at[first_sem + 1],
                device_id=device,
                device_id_type=MESH,
            ).start()

        def in_plane(i):
            return sec, lax.rem(row + i, n_row), col

        def along_nest(i):
            return sec, row, lax.rem(col + i, n_nest)

        pl.semaphore_wait(barrier, tiles - 1)

        @pl.loop(1, n_row)
        def _(i):
            to_peer(high_in.at[row], high_in.at[row], high_sems, 0, in_plane(n_row - i))

        @pl.loop(1, n_nest)
        def _(i):
            to_peer(low_in.at[col], low_in.at[col], low_sems, 0, along_nest(n_nest - i))

        first_copy, bulk_copy = relays()
        first_copy.wait_recv()
        send_to(1, tiles - 1, first_in.at[tile], first_in.at[tile], first_sems.at[2], first_sems.at[3])
        bulk_copy.wait_recv()

        @pl.loop(1, n_row)
        def _(i):
            to_peer(bulk_in.at[row], bulk_in.at[row], bulk_sems, 2, in_plane(n_row - i))

        def pass_on(count, me, wants, pick, out, got, sems, device):
            for i in range(count):
                for k in range(K):
                    for n, x in enumerate(pick(wants[i * K + k])):
                        if i == 0:
                            got[me, k, n] = x
                        else:
                            out[i - 1, k, n] = x
                if i > 0:
                    to_peer(out.at[i - 1], got.at[me], sems[0], sems[1], device(i))

        wait_all(high_in.at[pl.ds(0, n_row - 1)], high_sems.at[1])
        pass_on(
            n_nest,
            col,
            high_wants,
            lambda w: [high_in[w[0], w[2], n] for n in range(STRIP_TILES)],
            high_out,
            high_got,
            (high_sems, 2),
            along_nest,
        )
        wait_all(low_in.at[pl.ds(0, n_nest - 1)], low_sems.at[1])
        pass_on(
            n_row,
            row,
            low_wants,
            lambda w: [low_in[w[1], w[2], n] for n in range(STRIP_TILES)],
            low_out,
            low_got,
            (low_sems, 2),
            in_plane,
        )
        wait_all(bulk_in.at[pl.ds(0, n_row - 1)], bulk_sems.at[3])
        pass_on(
            n_nest,
            col,
            near_wants,
            around,
            near_out,
            near_got,
            (near_sems, 0),
            along_nest,
        )

        wait_all(first_in.at[pl.ds(0, tiles - 1)], first_sems.at[3])
        blocks = [first_in[homes[k]] for k in range(K)]
        middles = [centred(block, k) for k, block in enumerate(blocks)]
        for t in range(2):
            lines = jnp.zeros((PH, width), jnp.float32)
            ends = []
            for k in range(K):
                at = t * (LEFT + (RR - 1) * PW) + bands[k] * (2 * (RR - 1)) + columns[k]
                to_east = at + RR - 1
                cols = jnp.where(
                    lane < width // 2, pick_lane(blocks[k], at), pick_lane(blocks[k], to_east)
                )
                ghost_cols[t, k] = grow_rows(cols)
                ends.append((pick_lane(blocks[k], at + 1), pick_lane(blocks[k], to_east - 1)))
                for i in range(2):
                    line = pick_row(middles[k], 2 * (t * K + bands[k]) + i)
                    lines = jnp.where(sub == 2 * k + i, line, lines)
            (west_0, east_0), (west_1, east_1) = ends
            ghost_cols[t, K] = grow_rows(four(west_0, east_1, west_1, east_0))
            keep_rows(t, dot_by(lines, widen))

        fine_lane = iota((FINE_ROWS, width), 1)
        own_ends = (fine_lane == 0, fine_lane == width - 1)
        slab_ends = (lax.rem(fine_lane, half) == 0, lax.rem(fine_lane, half) == half - 1)
        slots = [pl.ds(k * FINE_ROWS, FINE_ROWS) for k in range(K)]

        def load_own(source):
            return [[source[f, slot] for f in range(3)] for slot in slots]

        def substeps(which, states):
            wets = [
                [slab[3 + i] if k == K else own_wet[i, slots[k]] for i in range(2)] for k in which
            ]
            old_cols, new_cols = [[ghost_cols[t, k] for k in which] for t in range(2)]
            old_rows, new_rows = [[ghost_rows[t, k] for k in which] for t in range(2)]
            for m in range(1, RR + 1):
                for n, k in enumerate(which):
                    cols = old_cols[n] + (m / RR) * (new_cols[n] - old_cols[n])
                    rows = old_rows[n] + (m / RR) * (new_rows[n] - old_rows[n])
                    ends = slab_ends if k == K else own_ends
                    states[n] = slab_step(states[n], wets[n], cols, rows, *ends)
            return states

        def averages(states):
            sums = dot_by(
                jnp.concatenate(
                    [
                        jnp.concatenate([row_sums(x[0]), row_sums(x[1]), row_picks(x[2])], axis=1)
                        for x in states
                    ],
                    axis=0,
                ),
                gather,
            )
            sums = [sums[n * PH : (n + 1) * PH] for n in range(len(states))]
            return [x[:, 0:width] for x in sums], [x[:, width:] for x in sums]

        def send_border(s, coarse, border):
            for k in range(K):
                last = pltpu.roll(coarse[k], PW, 1)
                edge_out[s, 2 * k : 2 * k + 1] = jnp.where(
                    lane[0:1] < 3 * PW, coarse[k][0:1], last[PH - 1 : PH]
                )
                edge_out[s, 2 * k + 1 : 2 * k + 2] = jnp.sum(
                    jnp.where(lane // 16 == sub, border[k], 0.0), axis=0, keepdims=True
                )
            lines = pl.ds(0, 2 * K)
            send_all(edge_out.at[s, lines], edge_in.at[s, tile, lines], ret_send.at[s], ret_recv.at[s])

        def store_own(states):
            for k in range(K):
                for f in range(3):
                    st[f, slots[k]] = states[k][f]

        def next_ghosts(coarse):
            for k in range(K + 1):
                ghost_cols[0, k] = ghost_cols[1, k]
                ghost_rows[0, k] = ghost_rows[1, k]
            lines = jnp.zeros((PH, width), jnp.float32)
            ends = []
            for k in range(K):
                on_left, on_right = [
                    jnp.full((PH, width), cover, jnp.int32) > 0 for cover in near[k]
                ]
                on_left = on_left & (lane >= NEAR - 4) & (lane < NEAR)
                on_right = on_right & (lane >= NEAR + PW) & (lane < NEAR + PW + 4)
                boundary = k * half // RR
                state = []
                for f in range(3):
                    x = patch[k, f, 0:PH]
                    x = jnp.where(own_lanes, pltpu.roll(coarse[k], (NEAR - f * PW) % width, 1), x)
                    low = f * PW + (boundary - 4) % PW
                    x = jnp.where(on_left, pltpu.roll(coarse[K], (NEAR - 4 - low) % width, 1), x)
                    high = f * PW + boundary
                    x = jnp.where(on_right, pltpu.roll(coarse[K], (NEAR + PW - high) % width, 1), x)
                    state.append(jnp.concatenate([x, patch[k, f, PH : 2 * PH]], axis=0))
                level = new_level_ring(state[0], state[1], state[2], COURANT)
                flux_e, flux_s = new_fluxes_ring(state[1], state[2], level, wet[k, 0], wet[k, 1])
                for f, x in enumerate((level, flux_e, flux_s)):
                    patch[k, f] = x
                level8, east8 = level[0:PH], flux_e[0:PH]
                cols = jnp.where(
                    lane < width // 2,
                    pltpu.roll(east8, width - NEAR + 1, 1),
                    pltpu.roll(level8, width - 1 - NEAR - PW, 1),
                )
                ghost_cols[1, k] = grow_rows(cols)
                at = k * half
                ends.append(
                    (
                        pltpu.roll(east8, (at - (NEAR + PW - 1)) % width, 1),
                        pltpu.roll(level8, (at - 1 - NEAR) % width, 1),
                    )
                )
                lines = jnp.where(sub == 2 * k, flux_s[2 * PH - 1 : 2 * PH], lines)
                lines = jnp.where(sub == 2 * k + 1, level[PH : PH + 1], lines)
            (west_0, east_0), (west_1, east_1) = ends
            ghost_cols[1, K] = grow_rows(four(west_0, east_1, west_1, east_0))
            keep_rows(1, dot_by(lines, widen))

        states = substeps(range(K), load_own(state_ref.at[0]))
        store_own(states)
        coarse, border = averages(states)


        send_border(0, coarse, border)

        wait_all(high_got.at[pl.ds(0, n_nest - 1)], high_sems.at[3])
        wait_all(low_got.at[pl.ds(0, n_row - 1)], low_sems.at[3])
        sets = [
            [
                [high_got[high_wants[k][1], k, n] for n in range(STRIP_TILES)],
                [low_got[low_wants[k][0], k, n] for n in range(STRIP_TILES)],
            ]
            for k in range(K)
        ]
        fits = []
        for k in range(K):
            start = k * half
            on_left, on_right = [jnp.full((PH, width), cover, jnp.int32) > 0 for cover in near[k]]
            before = (start - STRIP) % width
            fits.append(
                (
                    on_left & (lane >= before) & (lane < before + STRIP),
                    on_right & (lane >= start) & (lane < start + STRIP),
                    on_left & (lane == before - 1),
                )
            )
        for f in range(5):
            for g in range(groups):
                out = jnp.zeros((PH, width), jnp.float32)
                at = (f % 2) * groups * STRIP + g * STRIP
                for k in range(K):
                    start = k * half
                    before = (start - STRIP) % width
                    left, right = [sets[k][side][f // 2] for side in range(2)]
                    out = jnp.where(fits[k][0], pltpu.roll(left, (before - at) % width, 1), out)
                    out = jnp.where(fits[k][1], pltpu.roll(right, (start - at) % width, 1), out)
                    if f == 1:
                        extra = groups * STRIP + (g + 1) * STRIP - 1
                        out = jnp.where(
                            fits[k][2],
                            pltpu.roll(sets[k][0][2], (before - 1 - extra) % width, 1),
                            out,
                        )
                slab[f, 8 * g : 8 * g + 8] = out

        def load_slab():
            return [slab[f] for f in range(3)]

        def store_slab(state):
            for f in range(3):
                slab[f] = state[f]

        aside = substeps([K], [load_slab()])
        store_slab(aside[0])
        beside_own, _ = averages(aside)

        wait_all(near_got.at[pl.ds(0, n_nest - 1)], near_sems.at[1])
        for k in range(K):
            got = near_got[near_wants[k][1], k, 0]
            early, late, sides = [
                pltpu.roll(got, shift % width, 1) for shift in (NEAR - 4, NEAR - 4 - span, -2 * span)
            ]

            def tile_of(block, spots):
                out = jnp.zeros((PH, width), jnp.float32)
                for target, source in spots:
                    out = jnp.where(sub == target, block[source : source + 1], out)
                return out

            outside = [
                tile_of(early, ((0, 0), (1, 1), (7, 5))),
                tile_of(early, ((0, 2), (7, 6))),
                tile_of(early, ((0, 3), (6, 4), (7, 7))),
                tile_of(late, ((0, 3), (7, 4))),
                tile_of(late, ((0, 5), (6, 6), (7, 7))),
            ]
            for i in range(5):
                beside = jnp.where(
                    lane < NEAR + PW // 2,
                    pltpu.roll(sides, (NEAR - 4 - 8 * i) % width, 1),
                    pltpu.roll(sides, (NEAR + PW - 5 - 8 * i) % width, 1),
                )
                target = patch.at[k, i] if i < 3 else wet.at[k, i - 3]
                target[0:PH] = beside
                target[PH : 2 * PH] = outside[i]
            later[k, 0] = tile_of(late, ((1, 0), (6, 1)))
            later[k, 1] = tile_of(late, ((5, 2), (6, 2)))

        next_ghosts(coarse + beside_own)

        def inner_step(s):
            states = substeps(range(K + 1), load_own(st) + [load_slab()])
            coarse, border = averages(states)
            send_border(s, coarse, border)
            store_own(states)
            store_slab(states[K])

            @pl.when(s == 1)
            def _():
                given = (sub == 1) | (sub == 5) | (sub == 6)
                for k in range(K):
                    for f, value in enumerate((later[k, 0], 0.0, later[k, 1])):
                        patch[k, f, PH : 2 * PH] = jnp.where(given, value, patch[k, f, PH : 2 * PH])

            next_ghosts(coarse)

        for s in range(1, STEPS - 1):
            inner_step(s)
        states = substeps(range(K), load_own(st))
        coarse, _ = averages(states)
        for k in range(K):
            ret_out[k] = coarse[k]
        send_all(ret_out, ret_in.at[pl.ds(tile * K, K)], ret_send.at[STEPS - 1], ret_recv.at[STEPS - 1])
        for k in range(K):
            live = jnp.full((FINE_ROWS, width), lives[k], jnp.int32) > 0
            for f in range(3):
                out_ref[0, f, slots[k]] = jnp.where(live, states[k][f], state_ref[0, f, slots[k]])

        wait_all(first_in.at[pl.ds(0, tiles - 1)], first_sems.at[2])
        wait_all(bulk_in.at[pl.ds(0, n_row - 1)], bulk_sems.at[2])
        wait_all(low_in.at[pl.ds(0, n_nest - 1)], low_sems.at[0])
        wait_all(low_got.at[pl.ds(0, n_row - 1)], low_sems.at[2])
        wait_all(high_in.at[pl.ds(0, n_row - 1)], high_sems.at[0])
        wait_all(high_got.at[pl.ds(0, n_nest - 1)], high_sems.at[2])
        wait_all(near_got.at[pl.ds(0, n_nest - 1)], near_sems.at[0])
        for s in range(STEPS - 1):
            wait_all(edge_in.at[s, :, pl.ds(0, 2 * K)], ret_send.at[s])
        wait_all(ret_in, ret_send.at[STEPS - 1])


def on_device(n_row, n_nest, ocean_state, face_depth, face_open, nest_place, nest_host):
    tiles = n_row * n_nest
    height, width = ocean_state.shape[2:]
    f32 = jnp.float32
    vmem = pl.BlockSpec(memory_space=pltpu.VMEM)
    hbm = pl.BlockSpec(memory_space=pl.ANY)
    smem = pl.BlockSpec(memory_space=pltpu.SMEM)
    dma = pltpu.SemaphoreType.DMA
    return pl.pallas_call(
        functools.partial(kernel, n_row, n_nest),
        out_shape=pltpu.VMEM(ocean_state.shape, f32),
        in_specs=[smem, smem, hbm, hbm, hbm],
        out_specs=vmem,
        scratch_shapes=[
            pltpu.VMEM(ocean_state.shape, f32),
            pltpu.VMEM(face_depth.shape, f32),
            pltpu.VMEM(face_open.shape, jnp.int32),
            dma((3,)),
            pltpu.VMEM((3, height, width), f32),
            pltpu.VMEM((9, height, width), f32),
            pltpu.VMEM((PH, width), f32),
            pltpu.VMEM((tiles, PH, width), f32),
            pltpu.VMEM((3 * K, PH, width), f32),
            pltpu.VMEM((n_row, 3 * K, PH, width), f32),
            pltpu.VMEM((n_nest, K, STRIP_TILES, PH, width), f32),
            pltpu.VMEM((n_row, K, STRIP_TILES, PH, width), f32),
            pltpu.VMEM((n_row, K, STRIP_TILES, PH, width), f32),
            pltpu.VMEM((n_row, K, STRIP_TILES, PH, width), f32),
            pltpu.VMEM((n_nest, K, STRIP_TILES, PH, width), f32),
            pltpu.VMEM((n_nest, K, STRIP_TILES, PH, width), f32),
            pltpu.VMEM((n_nest, K, 1, PH, width), f32),
            pltpu.VMEM((n_nest, K, 1, PH, width), f32),
            pltpu.VMEM((STEPS - 1, PH, width), f32),
            pltpu.VMEM((STEPS - 1, tiles, PH, width), f32),
            pltpu.VMEM((K, PH, width), f32),
            pltpu.VMEM((tiles * K, PH, width), f32),
            pltpu.VMEM((height, width), f32),
            pltpu.VMEM((height, width), f32),
            pltpu.VMEM((height, width), f32),
            pltpu.VMEM((5, height + 2 * HALO, 2 * width), f32),
            pltpu.VMEM((height + 2 * HALO, 2 * width), f32),
            pltpu.VMEM((2, K + 1, FINE_ROWS, width), f32),
            pltpu.VMEM((2, K + 1, PH, width), f32),
            pltpu.VMEM((K, 3, 2 * PH, width), f32),
            pltpu.VMEM((K, 2, 2 * PH, width), f32),
            pltpu.VMEM((K, 2, PH, width), f32),
            pltpu.VMEM((5, FINE_ROWS, width), f32),
            pltpu.VMEM((2, height, width), f32),
            pltpu.VMEM((tiles, PH, width), f32),
            dma((4,)),
            dma((4,)),
            dma((4,)),
            dma((4,)),
            dma((2,)),
            dma((STEPS,)),
            dma((STEPS,)),
            dma((4,)),
            dma((4,)),
        ],
        compiler_params=pltpu.CompilerParams(collective_id=0, has_side_effects=True),
    )(nest_place, nest_host, ocean_state, face_depth, face_open)


def solution(mesh):
    field = P("sec", None, "row", "nest")
    return jax.shard_map(
        functools.partial(on_device, mesh.shape["row"], mesh.shape["nest"]),
        mesh=mesh,
        in_specs=(field, field, field, P(), P()),
        out_specs=field,
        check_vma=False,
    )
```
